32 devices in a mesh: groups: 2 (over x), node: 8 (over z, y), rep: 2 (over core).
Axes of the slice: x: 2, y: 2, z: 4, core: 2. Of those that a mesh axis runs over, the one named last changes fastest.
Arguments:
- normed_input: bfloat16 [4, 1024, 5120], P(('groups', 'rep'), 'node'), parts along dimension 0, may hold values from -6 to 6
- queries: bfloat16 [4, 1024, 2560], P(('groups', 'rep'), 'node'), parts along dimension 0, may hold values from -120 to 120
- rotated_key_heads: bfloat16 [4, 1024, 512], P(('groups', 'rep'), 'node'), parts along dimension 0, may hold values from -6 to 6
- frozen_value_rows: bfloat16 [4, 1024, 512], P(('groups', 'rep'), 'node'), parts along dimension 0, may hold values from -6 to 6
- adapter_down_weight: bfloat16 [5120, 32], replicated, may hold values from -0.078125 to 0.078125
- adapter_up_weight: bfloat16 [32, 512], replicated, may hold values from -1 to 1
- output_gradient: bfloat16 [4, 1024, 2560], P(('groups', 'rep'), 'node'), parts along dimension 0, may hold values from -6 to 6
- parents: int32 [4, 8], P(('groups', 'rep')), parts along dimension 0, may hold values from -1 to 6, as said below
- lengths: int32 [4, 8], P(('groups', 'rep')), parts along dimension 0, may hold values from 32 to 128, as said below
Outputs:
- attended: bfloat16 [4, 1024, 2560], P(('groups', 'rep'), 'node'), parts along dimension 0
- query_grad: bfloat16 [4, 1024, 2560], P(('groups', 'rep'), 'node'), parts along dimension 0
- down_grad: float32 [10240, 32], P('groups'), parts along dimension 0
- up_grad: float32 [64, 512], P('groups'), parts along dimension 0
The draws below stay inside these ranges and needn't reach their ends.
There are 2 independent parts, one for each index of `groups`. The reference program is written for one: setup_inputs(seed, part) draws one part's arguments, and reference() takes and returns one part's arrays. A program takes and returns all parts, laid end to end along the dimension named above; an argument that names none is the same for every part. Nothing has to cross between parts.
Inputs may be any that keep to these rules, and one draw needn't show every extreme that they name: `parents`: slots 0 to 1 form the shared prompt, each the parent of the next, slot 0 the root. Every other slot's parent is slot 1 or a slot below it, and every ancestor of a slot s outside the prompt lies among the slots s - 5 to s - 1. `lengths`: prompt blocks are full.
All inputs are finite; a program needn't handle non-finite values.
Results may differ from the reference program's by a relative error of at most 0.0062.
Values may be sent and summed in bfloat16 or wider, within the bound.
A program may use at most 128 MiB of HBM per device.

```python
import jax
import jax.numpy as jnp
from jax import lax

MODEL_WIDTH = 5120
HQ = 20
KEY_HEADS = 4
HEAD_SIZE = 128
ADAPTER_RANK = 32
BLK = 128
PROMPT = 2
SPAN = 5
TREES = 2
ROWS = 1024
N_NODE = 8
N_REP = 2


def tree_links(tree_key):
    position_index = jnp.arange(N_NODE, dtype=jnp.int32)
    order_scores = jax.random.randint(tree_key, (N_NODE, N_NODE), 0, 1024, dtype=jnp.int32)
    start = jnp.where(position_index < PROMPT, position_index - 1, 0).astype(jnp.int32)

    def extend(carried, tree_position):
        parent_row, lowest = carried
        permitted_mask = (position_index == PROMPT - 1) | (position_index >= PROMPT) & (position_index < tree_position) & (position_index >= tree_position - SPAN) & (lowest >= tree_position - SPAN)
        extra_logit = jnp.where(position_index == tree_position - 1, 400, 0).astype(jnp.int32)
        sorted_order = jnp.where(permitted_mask, (order_scores[tree_position] + extra_logit) * 64 + position_index, -1)
        chosen = jnp.argmax(sorted_order).astype(jnp.int32)
        parent_row = parent_row.at[tree_position].set(chosen)
        lowest = lowest.at[tree_position].set(jnp.where(chosen == PROMPT - 1, tree_position, lowest[chosen]).astype(jnp.int32))
        return ((parent_row, lowest), None)
    (parent_row, lowest), unused = lax.scan(extend, (start, position_index), jnp.arange(PROMPT, N_NODE, dtype=jnp.int32))
    return parent_row


def draw_parents(key, part):
    tree_keys = jax.random.split(jax.random.fold_in(key, 5), N_REP)
    return jax.vmap(tree_links)(tree_keys).astype(jnp.int32)


def draw_lengths(key, part):
    drawn = jax.random.randint(jax.random.fold_in(key, 7), (N_REP, N_NODE), BLK // 4, BLK + 1, dtype=jnp.int32)
    position_index = jnp.arange(N_NODE, dtype=jnp.int32)[None, :]
    drawn = jnp.where(position_index < PROMPT, BLK, drawn)
    drawn = jnp.where(position_index == PROMPT, BLK // 4, drawn)
    return drawn.astype(jnp.int32)


def key_table(key):
    table = jnp.clip(jax.random.normal(jax.random.fold_in(key, 11), (N_REP, N_NODE * BLK, KEY_HEADS * HEAD_SIZE), jnp.float32), -5.0, 5.0)
    return table


def draw_rotated_key_heads(key, part):
    return key_table(key).astype(jnp.bfloat16)


def draw_queries(key, part):
    entries = jnp.clip(jax.random.normal(jax.random.fold_in(key, 13), (N_REP, N_NODE * BLK, HQ * HEAD_SIZE), jnp.float32), -5.0, 5.0)
    return entries.astype(jnp.bfloat16)


def steps_of(rng, extent, cuts, low, largest):
    loudness, own = 1.0, jax.random.fold_in(rng, 6)
    for dim, blocks in cuts:
        heights = jnp.exp(jax.random.uniform(jax.random.fold_in(own, dim), (blocks,), jnp.float32, low / len(cuts), largest / len(cuts)))
        loudness = loudness * jnp.repeat(heights, extent[dim] // blocks).reshape([-1 if axis == dim else 1 for axis in range(len(extent))])
    return loudness


def normal_values(rng, dims, deviation, most, pieces=(), kind=jnp.bfloat16):
    values = deviation * jax.random.normal(rng, dims, jnp.float32)
    if pieces:
        values = values * steps_of(rng, dims, pieces, -0.22, 0.18)
    return jnp.clip(values, -most, most).astype(kind)


def setup_inputs(seed: int = 0, part: int = 0) -> dict:
    key_of = jax.random.split(jax.random.key(seed), 10)
    part_splits = jax.random.split(jax.random.fold_in(key_of[9], part), 10)
    normed_input = normal_values(part_splits[0], (TREES, ROWS, MODEL_WIDTH), 1.0, 6.0, ((0, 2), (1, 8)))
    queries = draw_queries(jax.random.fold_in(jax.random.fold_in(key_of[9], part), 71), part)
    rotated_key_heads = draw_rotated_key_heads(jax.random.fold_in(jax.random.fold_in(key_of[9], part), 71), part)
    frozen_value_rows = normal_values(part_splits[3], (TREES, ROWS, KEY_HEADS * HEAD_SIZE), 1.0, 6.0, ((0, 2), (1, 8)))
    adapter_down_weight = normal_values(key_of[4], (MODEL_WIDTH, ADAPTER_RANK), MODEL_WIDTH ** -0.5, 0.078125)
    adapter_up_weight = normal_values(key_of[5], (ADAPTER_RANK, KEY_HEADS * HEAD_SIZE), ADAPTER_RANK ** -0.5, 1.0)
    output_gradient = normal_values(part_splits[6], (TREES, ROWS, HQ * HEAD_SIZE), 1.0, 6.0, ((0, 2), (1, 8)))
    parents = draw_parents(jax.random.fold_in(jax.random.fold_in(key_of[9], part), 71), part)
    lengths = draw_lengths(jax.random.fold_in(jax.random.fold_in(key_of[9], part), 71), part)
    return dict(normed_input=normed_input, queries=queries, rotated_key_heads=rotated_key_heads, frozen_value_rows=frozen_value_rows, adapter_down_weight=adapter_down_weight, adapter_up_weight=adapter_up_weight, output_gradient=output_gradient, parents=parents, lengths=lengths)


NEGATIVE = -1.0e30
HIGHEST = lax.Precision.HIGHEST


def chain_of(parent_row):
    current = parent_row
    columns = []
    for height in range(PROMPT + SPAN):
        columns.append(current)
        current = jnp.where(current >= 0, parent_row[jnp.maximum(current, 0)], -1).astype(jnp.int32)
    return jnp.stack(columns, 1)


def reference(normed_input, queries, rotated_key_heads, frozen_value_rows, adapter_down_weight, adapter_up_weight, output_gradient, parents, lengths):
    trees = normed_input.shape[0]
    slot_count = parents.shape[1]
    block_rows = normed_input.shape[1] // slot_count
    groups_per = HQ // KEY_HEADS
    key_value_width = KEY_HEADS * HEAD_SIZE
    inverse_root = HEAD_SIZE ** -0.5
    position = jnp.arange(block_rows, dtype=jnp.int32)
    adapter_inner = jnp.dot(normed_input.reshape(-1, MODEL_WIDTH), adapter_down_weight, preferred_element_type=jnp.float32).astype(jnp.bfloat16)
    value_rows = frozen_value_rows.reshape(-1, key_value_width).astype(jnp.float32) + jnp.dot(adapter_inner, adapter_up_weight, preferred_element_type=jnp.float32)
    value_rows = value_rows.astype(jnp.bfloat16).reshape(trees, slot_count, block_rows, KEY_HEADS, HEAD_SIZE)
    adapter_inner = adapter_inner.reshape(trees, slot_count * block_rows, ADAPTER_RANK)
    up_weight_float = adapter_up_weight.astype(jnp.float32)
    count = 1 + PROMPT + SPAN
    not_first = (jnp.arange(count, dtype=jnp.int32) > 0)[:, None, None]
    causal = position[None, :] <= position[:, None]
    down_total = jnp.zeros((MODEL_WIDTH, ADAPTER_RANK), jnp.float32)
    up_total = jnp.zeros((ADAPTER_RANK, key_value_width), jnp.float32)
    attended_all = []
    grads_all = []
    for tree in range(trees):
        own_ids = jnp.arange(slot_count, dtype=jnp.int32)[:, None]
        cand_ids = jnp.concatenate([own_ids, chain_of(parents[tree])], 1).astype(jnp.int32)
        safe_ids = jnp.maximum(cand_ids, 0).astype(jnp.int32)
        keys_tree = rotated_key_heads[tree].reshape(slot_count, block_rows, KEY_HEADS, HEAD_SIZE).astype(jnp.float32)
        values_tree = value_rows[tree].astype(jnp.float32)
        query_tree = queries[tree].reshape(slot_count, block_rows, KEY_HEADS, groups_per, HEAD_SIZE).astype(jnp.float32)
        grad_tree = output_gradient[tree].reshape(slot_count, block_rows, KEY_HEADS, groups_per, HEAD_SIZE)
        length_row = lengths[tree]

        def slot_work(tree_position):
            picked = safe_ids[tree_position]
            usable = cand_ids[tree_position] >= 0
            keys_here = keys_tree[picked]
            values_here = values_tree[picked]
            key_live = position[None, :] < length_row[picked][:, None]
            permitted_mask = (causal[None] | not_first) & key_live[:, None, :] & usable[:, None, None]
            logits = jnp.einsum("ikgd,cjkd->ckgij", query_tree[tree_position], keys_here, precision=HIGHEST) * inverse_root
            logits = jnp.where(permitted_mask[:, None, None], logits, NEGATIVE)
            highest = jnp.max(logits, axis=(0, 4))
            totals = jnp.sum(jnp.exp(logits - highest[None, :, :, :, None]), axis=(0, 4))
            log_total = highest + jnp.log(totals)
            weights = jnp.exp(logits - log_total[None, :, :, :, None])
            rounded = lax.optimization_barrier(weights.astype(jnp.bfloat16)).astype(jnp.float32)
            output = jnp.einsum("ckgij,cjkd->ikgd", rounded, values_here, precision=HIGHEST)
            live = position < length_row[tree_position]
            attended = jnp.where(live[:, None, None, None], output, 0.0).astype(jnp.bfloat16)
            head_gradient = jnp.where(live[:, None, None, None], grad_tree[tree_position], jnp.zeros_like(grad_tree[tree_position])).astype(jnp.float32)
            row_dots = jnp.einsum("ikgd,ikgd->kgi", head_gradient, output, precision=HIGHEST)
            pressure = jnp.einsum("ikgd,cjkd->ckgij", head_gradient, values_here, precision=HIGHEST)
            slopes = (weights * (pressure - row_dots[None, :, :, :, None]) * inverse_root).astype(jnp.bfloat16)
            slopes = lax.optimization_barrier(slopes).astype(jnp.float32)
            query_grad = jnp.einsum("ckgij,cjkd->ikgd", slopes, keys_here, precision=HIGHEST).astype(jnp.bfloat16)
            value_parts = jnp.einsum("ckgij,ikgd->cjkd", rounded, head_gradient, precision=HIGHEST)
            return attended, query_grad, value_parts

        attended, query_grad, value_parts = lax.map(slot_work, jnp.arange(slot_count, dtype=jnp.int32))
        value_total = jnp.zeros((slot_count, block_rows, KEY_HEADS, HEAD_SIZE), jnp.float32)
        value_total = value_total.at[safe_ids.reshape(-1)].add(value_parts.reshape(-1, block_rows, KEY_HEADS, HEAD_SIZE))
        value_flat = value_total.reshape(-1, key_value_width)
        projected = jnp.dot(value_flat, up_weight_float.T, precision=HIGHEST).astype(jnp.bfloat16)
        down_total = down_total + jnp.dot(normed_input[tree].T, projected, preferred_element_type=jnp.float32)
        up_total = up_total + jnp.dot(adapter_inner[tree].astype(jnp.float32).T, value_flat, precision=HIGHEST)
        attended_all.append(attended.reshape(slot_count * block_rows, HQ * HEAD_SIZE))
        grads_all.append(query_grad.reshape(slot_count * block_rows, HQ * HEAD_SIZE))
    factor = (trees * slot_count * block_rows) ** -0.5
    return jnp.stack(attended_all), jnp.stack(grads_all), down_total * factor, up_total * factor
```

```python
import functools
import math

import jax
import jax.numpy as jnp
from jax import lax
from jax.experimental import pallas as pl
from jax.experimental.pallas import tpu as pltpu
from jax.sharding import PartitionSpec as P

KEY_HEADS = 4
HEAD_SIZE = 128
PROMPT = 2
SPAN = 5
STEPS = 1 + PROMPT + SPAN
NEGATIVE = -1e30
F32 = jnp.float32
BF16 = jnp.bfloat16
NT = (((1,), (1,)), ((), ()))
NN = (((1,), (0,)), ((), ()))
TN = (((0,), (0,)), ((), ()))
MESH_ID = pl.DeviceIdType.MESH


def dot(a, b, dims):
    return lax.dot_general(a, b, dims, preferred_element_type=F32)


def split(a):
    high = a.astype(BF16)
    return jnp.concatenate([high, (a - high.astype(F32)).astype(BF16)], axis=1)


def reaches(slot, below):
    return (below > slot) & ((slot < PROMPT) | (below - slot <= SPAN))


def first_pair(own):
    return jnp.maximum((own + 2 * SPAN - SPAN) // 2 - SPAN, 1)


def pair_count(slots):
    most = 1
    for own in range(slots):
        most = max(most, own // 2 - max((own - SPAN) // 2, 1) + 2)
    return most


def peer(node, rep=None):
    target = {"node": node}
    if rep is not None:
        target["rep"] = rep
    return target


def kernel(
    slots, reps, factor,
    parents, lengths, x_ref, q_ref, k_ref, frozen_ref, down_ref, up_ref, g_ref,
    att_ref, qg_ref, down_out, up_out,
    xs, xcat, downs, qs, gs, fs, kbuf, vbuf, lowbuf, score, weight, top, total, inverse, gup,
    atts, qgs, proj, landed, tbuf, upk, upland, parts, gathered, result,
    load_sem, qload, gload, store_a, store_q,
    k_col, k_fwd, k_recv, l_col, l_fwd, l_recv, v_col, v_fwd, v_recv,
    x_send, x_recv, p_send, p_recv, t_send, t_recv, u_send, u_recv,
    r_send, r_recv, a_send, a_recv, b_send, b_recv,
):
    own, rep = lax.axis_index("node"), lax.axis_index("rep")
    heads = qs.shape[0]
    per = heads // KEY_HEADS
    block = qs.shape[1]
    rows = per * block
    width = xs.shape[1]
    half = width // reps
    scale = HEAD_SIZE ** -0.5
    pair = own // 2
    partner = own + 1 - 2 * lax.rem(own, 2)
    pairs = pair - first_pair(own) + 2

    barrier = pltpu.get_barrier_semaphore()
    for step in range(reps):
        other = lax.rem(rep + step, reps)

        def signal(t, carry):
            pl.semaphore_signal(
                barrier, inc=1, device_id=peer(lax.rem(own + t, slots), other),
                device_id_type=MESH_ID,
            )
            return carry

        lax.fori_loop(0 if step else 1, slots, signal, 0)

    def remote(src, dst, send, recv, node, r=None):
        return pltpu.make_async_remote_copy(
            src_ref=src, dst_ref=dst, send_sem=send, recv_sem=recv,
            device_id=peer(node, r), device_id_type=MESH_ID,
        )

    loads = [
        pltpu.make_async_copy(k_ref, kbuf.at[own], load_sem.at[0]),
        pltpu.make_async_copy(down_ref, downs, load_sem.at[1]),
        pltpu.make_async_copy(x_ref, xs, load_sem.at[2]),
        pltpu.make_async_copy(frozen_ref, fs, load_sem.at[3]),
        pltpu.make_async_copy(
            x_ref.at[:, pl.ds(pl.multiple_of(rep * half, 128), half)], xcat.at[rep], load_sem.at[4]
        ),
    ]
    for c in loads:
        c.start()

    def head_copy(source, target, sem, i):
        return pltpu.make_async_copy(
            source.at[:, pl.ds(pl.multiple_of(i * HEAD_SIZE, HEAD_SIZE), HEAD_SIZE)],
            target.at[i], sem.at[i],
        )

    def head_store(source, target, sem, i):
        return pltpu.make_async_copy(
            source.at[i],
            target.at[:, pl.ds(pl.multiple_of(i * HEAD_SIZE, HEAD_SIZE), HEAD_SIZE)],
            sem.at[i],
        )

    def each(low, high, action):
        def body(i, carry):
            action(i)
            return carry

        lax.fori_loop(low, high, body, 0)

    each(0, heads, lambda i: head_copy(q_ref, qs, qload, i).start())
    each(0, heads, lambda i: head_copy(g_ref, gs, gload, i).start())

    chain = []
    current = own
    for _ in range(1, STEPS):
        parent = parents[0, jnp.maximum(current, 0)]
        current = jnp.where(current >= 0, parent, -1)
        chain.append(current)
    own_length = lengths[0, own]

    def limit(slot):
        found = slot == own
        for ancestor in chain:
            found = found | (slot == ancestor)
        return jnp.where(found, lengths[0, slot], 0)

    def unsent(slot):
        same = lax.rem(slot + own, 2) == 0
        lands = same & reaches(slot, 2 * pair) | reaches(slot, own)
        return jnp.logical_not(lands | (slot == own))

    def clear_slot(slot):
        proj[slot] = jnp.zeros(proj.shape[1:], F32)

        @pl.when(unsent(slot))
        def _():
            kbuf[slot] = jnp.zeros(kbuf.shape[1:], BF16)
            vbuf[slot] = jnp.zeros(vbuf.shape[1:], BF16)
            lowbuf[slot] = jnp.zeros(lowbuf.shape[1:], BF16)

    each(0, slots, clear_slot)

    loads[0].wait()
    pl.semaphore_wait(barrier, slots * reps - 1)

    def column(buf, send, recv, t):
        return remote(buf.at[own], buf.at[own], send.at[t], recv.at[own], own + 2 * t)

    def across(buf, send, recv, slot):
        return remote(buf.at[slot], buf.at[slot], send.at[slot], recv.at[slot], partner)

    def columns(action):
        def body(step):
            t = slots // 2 - 1 - step

            @pl.when((own + 2 * t < slots) & reaches(own, 2 * (pair + t)))
            def _():
                action(t)

        each(0, slots // 2 - 1, body)

    def own_across(action):
        @pl.when(reaches(own, partner))
        def _():
            action(own)

    def relayed(action):
        def body(t):
            slot = own - 2 * t

            @pl.when(reaches(slot, 2 * pair))
            def _():
                action(slot)

        each(1, pair + 1, body)

    def forward(buf, send, recv):
        def act(slot):
            across(buf, send, recv, slot).wait_recv()

            @pl.when(reaches(slot, partner))
            def _():
                across(buf, send, recv, slot).start()

        relayed(act)

    def from_partner(buf, send, recv, t):
        slot = partner - 2 * t

        @pl.when(reaches(slot, own))
        def _():
            across(buf, send, recv, slot).wait_recv()

    def send_own(buf, col, fwd, recv):
        own_across(lambda slot: across(buf, fwd, recv, slot).start())
        columns(lambda t: column(buf, col, recv, t).start())

    def drain(buf, col, fwd, recv):
        own_across(lambda slot: across(buf, fwd, recv, slot).wait_send())
        columns(lambda t: column(buf, col, recv, t).wait_send())

        def act(slot):
            @pl.when(reaches(slot, partner))
            def _():
                across(buf, fwd, recv, slot).wait_send()

        relayed(act)

    send_own(kbuf, k_col, k_fwd, k_recv)

    def swap_x(r):
        return remote(
            x_ref.at[:, pl.ds(pl.multiple_of(r * half, 128), half)], xcat.at[rep],
            x_send.at[r], x_recv.at[rep], own, r,
        )

    def other_reps(action):
        for step in range(1, reps):
            action(lax.rem(rep + step, reps))

    other_reps(lambda r: swap_x(r).start())

    loads[1].wait()
    loads[2].wait()
    low = dot(xs[...], downs[...], NN)
    lowbuf[own] = low.T.astype(BF16)
    loads[3].wait()
    vbuf[own] = (fs[...].astype(F32) + dot(low.astype(BF16), up_ref[...], NN)).astype(BF16)
    send_own(lowbuf, l_col, l_fwd, l_recv)
    send_own(vbuf, v_col, v_fwd, v_recv)

    each(0, heads, lambda i: head_copy(q_ref, qs, qload, i).wait())
    each(0, heads, lambda i: head_copy(g_ref, gs, gload, i).wait())

    def stacked(buf, kk):
        return buf[pl.ds(kk * per, per)].reshape(rows, HEAD_SIZE)

    def pair_at(step):
        return jnp.where(step == pairs - 1, 0, pair - step)

    def two(buf, index, kk):
        lanes = pl.ds(pl.multiple_of(kk * HEAD_SIZE, HEAD_SIZE), HEAD_SIZE)
        return buf[pl.ds(2 * index, 2), :, lanes].reshape(2 * block, HEAD_SIZE)

    for kk in range(KEY_HEADS):
        lanes = slice(kk * HEAD_SIZE, (kk + 1) * HEAD_SIZE)
        gup[kk] = dot(stacked(gs, kk), up_ref[:, lanes], NT)

    forward(kbuf, k_fwd, k_recv)
    forward(lowbuf, l_fwd, l_recv)

    key = lax.broadcasted_iota(jnp.int32, (block, 2 * block), 1)
    place = lax.rem(key, block)
    query = lax.broadcasted_iota(jnp.int32, (block, 2 * block), 0)

    def scores(step, mask, first):
        index = pair_at(step)

        def one(kk):
            s = dot(stacked(qs, kk), two(kbuf, index, kk), NT)
            s = jnp.where(mask, s, NEGATIVE)
            score[kk, step] = s
            most = jnp.maximum(s[:, :block], s[:, block:])
            top[kk] = most if first else jnp.maximum(top[kk], most)

        each(0, KEY_HEADS, one)

    from_partner(kbuf, k_fwd, k_recv, 0)
    even, odd = limit(2 * pair), limit(2 * pair + 1)
    here = jnp.where(key < block, 2 * pair, 2 * pair + 1) == own
    mask = (place < jnp.where(key < block, even, odd)) & (jnp.logical_not(here) | (place <= query))
    scores(0, jnp.concatenate([mask] * per, axis=0), True)

    def later(t):
        from_partner(kbuf, k_fwd, k_recv, t)
        index = pair - t

        @pl.when((index == 0) | (index >= first_pair(own)))
        def _():
            step = jnp.where(index == 0, pairs - 1, t)
            even, odd = limit(2 * index), limit(2 * index + 1)
            col = lax.broadcasted_iota(jnp.int32, (rows, 2 * block), 1)
            mask = lax.rem(col, block) < jnp.where(col < block, even, odd)
            scores(step, mask, False)

    each(1, pair + 1, later)

    live = (lax.rem(lax.broadcasted_iota(jnp.int32, (rows, 1), 0), block) < own_length).astype(F32)
    rank = proj.shape[1]

    def weigh(kk):
        most = jnp.max(top[kk], axis=1, keepdims=True)
        total[...] = jnp.zeros_like(total)

        def one(step):
            e = jnp.exp2((score[kk, step] - most) * (scale * math.log2(math.e)))
            score[kk, step] = e
            weight[kk, step] = e.astype(BF16)
            total[...] += e[:, :block] + e[:, block:]

        each(0, pairs, one)
        inv = live / jnp.sum(total[...], axis=1, keepdims=True)
        inverse[kk] = jnp.broadcast_to(inv, (rows, HEAD_SIZE))
        sides = split(gup[kk] * inv)

        def project(step):
            index = pair_at(step)
            both = dot(sides, weight[kk, step], TN)
            both = both[:rank] + both[rank:]
            proj[2 * index] += both[:, :block]
            proj[2 * index + 1] += both[:, block:]

        each(0, pairs, project)

    each(0, KEY_HEADS, weigh)

    def scatter(source, target):
        return remote(
            proj.at[target], landed.at[source], p_send.at[target], p_recv.at[source], target
        )

    def ancestors(action):
        def body(t):
            @pl.when(reaches(t, own))
            def _():
                action(t)

        each(0, slots, body)

    def descendants(action):
        def body(t):
            @pl.when(reaches(own, t))
            def _():
                action(t)

        each(0, slots, body)

    ancestors(lambda t: scatter(own, t).start())
    forward(vbuf, v_fwd, v_recv)

    each(0, pair + 1, lambda t: from_partner(lowbuf, l_fwd, l_recv, t))

    def low_weights(kk):
        total[:, :rank] = jnp.zeros((rows, rank), F32)

        def one(step):
            index = pair_at(step)
            lows = jnp.concatenate([lowbuf[2 * index], lowbuf[2 * index + 1]], axis=1)
            total[:, :rank] += dot(weight[kk, step], lows, NT)

        each(0, pairs, one)
        sides = split(total[:, :rank] * inverse[kk][:, :rank])
        both = dot(sides, stacked(gs, kk), TN)
        upk[kk] = both[:rank] + both[rank:]

    each(0, KEY_HEADS, low_weights)
    share = KEY_HEADS // reps

    def swap_up(r):
        return remote(
            upk.at[pl.ds(r * share, share)], upland.at[rep], u_send.at[r], u_recv.at[rep], own, r
        )

    other_reps(lambda r: swap_up(r).start())

    def add_landed(t):
        remote(
            proj.at[t], landed.at[t], p_send.at[t], p_recv.at[t], t
        ).wait_recv()
        proj[own] += landed[t]

    descendants(add_landed)
    tbuf[rep] = proj[own].astype(BF16)

    def swap_total(r):
        return remote(tbuf.at[rep], tbuf.at[rep], t_send.at[r], t_recv.at[rep], own, r)

    other_reps(lambda r: swap_total(r).start())
    loads[4].wait()

    def arrivals(r):
        remote(
            x_ref.at[:, pl.ds(0, half)], xcat.at[r], x_send.at[r], x_recv.at[r], own, r
        ).wait_recv()
        remote(tbuf.at[r], tbuf.at[r], t_send.at[r], t_recv.at[r], own, r).wait_recv()
        remote(
            upk.at[pl.ds(0, share)], upland.at[r], u_send.at[r], u_recv.at[r], own, r
        ).wait_recv()

    other_reps(arrivals)

    projected = jnp.concatenate([tbuf[r] for r in range(reps)], axis=1)
    ups = upk[pl.ds(rep * share, share)]
    for step in range(1, reps):
        ups = ups + upland[lax.rem(rep + step, reps)]
    upland[rep] = ups
    chunks, _, chunk = parts.shape
    up_half = share * HEAD_SIZE
    for j in range(chunks):
        lo, hi = j * chunk, (j + 1) * chunk
        pieces = []
        if lo < half:
            end = min(hi, half)
            pieces.append(dot(projected, xcat[:, :, lo:end].reshape(reps * block, end - lo), NN))
        for h in range(share):
            if lo <= half + h * HEAD_SIZE < hi:
                pieces.append(upland[rep, h])
        filled = sum(p.shape[1] for p in pieces)
        if filled < chunk:
            pieces.append(jnp.zeros((rank, chunk - filled), F32))
        value = pieces[0] if len(pieces) == 1 else jnp.concatenate(pieces, axis=1)
        parts[j] = value.astype(BF16)

    def reduce_copy(source, node):
        return remote(
            parts.at[node], gathered.at[source], r_send.at[node], r_recv.at[source], node
        )

    def others(action):
        each(1, slots, lambda t: action(lax.rem(own + t, slots)))

    def owners(action):
        def body(node):
            @pl.when(node < chunks)
            def _():
                action(node)

        others(body)

    owners(lambda node: reduce_copy(own, node).start())

    def gather_copy(node, owner):
        return remote(
            result.at[rep, owner], result.at[rep, owner], a_send.at[node], a_recv.at[owner], node
        )

    def swap_result(r, owner):
        return remote(
            result.at[rep, owner], result.at[rep, owner], b_send.at[r, owner],
            b_recv.at[rep, owner], own, r,
        )

    @pl.when(own < chunks)
    def _():
        gathered[own] = parts[own]
        others(lambda node: remote(
            parts.at[own], gathered.at[node], r_send.at[node], r_recv.at[node], node
        ).wait_recv())
        acc = lax.fori_loop(
            0, slots, lambda t, a: a + gathered[t].astype(F32), jnp.zeros((rank, chunk), F32)
        )
        result[rep, own] = (acc * factor).astype(BF16)
        others(lambda node: gather_copy(node, own).start())
        other_reps(lambda r: swap_result(r, own).start())

    each(0, pair + 1, lambda t: from_partner(vbuf, v_fwd, v_recv, t))

    def outputs(kk):
        grad = stacked(gs, kk)
        inv = inverse[kk]
        total[...] = jnp.zeros_like(total)

        def attend(step):
            total[...] += dot(weight[kk, step], two(vbuf, pair_at(step), kk), NN)

        each(0, pairs, attend)
        out = total[...] * inv
        atts[pl.ds(kk * per, per)] = out.astype(BF16).reshape(per, block, HEAD_SIZE)
        dots = jnp.sum(grad.astype(F32) * out, axis=1, keepdims=True)
        slope = inv[:, :1] * scale
        total[...] = jnp.zeros_like(total)

        def back(step):
            index = pair_at(step)
            pressure = dot(grad, two(vbuf, index, kk), NT)
            slopes = (score[kk, step] * ((pressure - dots) * slope)).astype(BF16)
            total[...] += dot(slopes, two(kbuf, index, kk), NN)

        each(0, pairs, back)
        qgs[pl.ds(kk * per, per)] = total[...].astype(BF16).reshape(per, block, HEAD_SIZE)

        def store(i):
            head_store(atts, att_ref, store_a, i).start()
            head_store(qgs, qg_ref, store_q, i).start()

        each(kk * per, (kk + 1) * per, store)

    each(0, KEY_HEADS, outputs)

    def pass_on(owner):
        remote(
            result.at[rep, owner], result.at[rep, owner], a_send.at[owner], a_recv.at[owner], owner
        ).wait_recv()
        other_reps(lambda r: swap_result(r, owner).start())

    owners(pass_on)

    def from_reps(r):
        each(0, chunks, lambda owner: remote(
            result.at[r, owner], result.at[r, owner], b_send.at[r, owner], b_recv.at[r, owner],
            own, r,
        ).wait_recv())

    other_reps(from_reps)
    for r in range(reps):
        for j in range(chunks):
            lo, hi = j * chunk, (j + 1) * chunk
            if lo < half:
                end = min(hi, half)
                down_out[:, r * half + lo:r * half + end] = result[r, j, :, :end - lo].astype(F32)
            if hi > half and lo < half + up_half:
                a, b = max(lo, half), min(hi, half + up_half)
                base = r * up_half - half
                up_out[:, base + a:base + b] = result[r, j, :, a - lo:b - lo].astype(F32)

    drain(kbuf, k_col, k_fwd, k_recv)
    drain(lowbuf, l_col, l_fwd, l_recv)
    drain(vbuf, v_col, v_fwd, v_recv)
    other_reps(lambda r: swap_x(r).wait_send())
    ancestors(lambda t: scatter(own, t).wait_send())
    other_reps(lambda r: swap_up(r).wait_send())
    other_reps(lambda r: swap_total(r).wait_send())
    owners(lambda node: reduce_copy(own, node).wait_send())

    @pl.when(own < chunks)
    def _():
        others(lambda node: gather_copy(node, own).wait_send())

    other_reps(lambda r: each(0, chunks, lambda owner: swap_result(r, owner).wait_send()))
    each(0, heads, lambda i: head_store(atts, att_ref, store_a, i).wait())
    each(0, heads, lambda i: head_store(qgs, qg_ref, store_q, i).wait())


def on_device(x, q, k, frozen, down, up, g, parents, lengths):
    x, q, k, frozen, g = x[0], q[0], k[0], frozen[0], g[0]
    block, width = x.shape
    slots, reps = lax.axis_size("node"), lax.axis_size("rep")
    rank, up_width = up.shape
    heads = q.shape[1] // HEAD_SIZE
    rows = heads // KEY_HEADS * block
    pairs = pair_count(slots)
    tiles = -(-(width + up_width) // reps // 128)
    per = -(-tiles // slots)
    chunks = -(-tiles // per)
    chunk = per * 128
    factor = (slots * reps * block) ** -0.5
    anywhere = pl.BlockSpec(memory_space=pl.ANY)
    vmem = pl.BlockSpec(memory_space=pltpu.VMEM)
    smem = pl.BlockSpec(memory_space=pltpu.SMEM)
    dma = pltpu.SemaphoreType.DMA
    v = pltpu.VMEM
    share = KEY_HEADS // reps
    attended, query_grad, down_sum, up_sum = pl.pallas_call(
        functools.partial(kernel, slots, reps, factor),
        in_specs=[smem, smem, anywhere, anywhere, anywhere, anywhere, anywhere, vmem, anywhere],
        out_specs=[anywhere, anywhere, vmem, vmem],
        out_shape=[
            jax.ShapeDtypeStruct(q.shape, BF16),
            jax.ShapeDtypeStruct(q.shape, BF16),
            jax.ShapeDtypeStruct((rank, width), F32),
            jax.ShapeDtypeStruct((rank, up_width), F32),
        ],
        scratch_shapes=[
            v(x.shape, BF16), v((reps, block, width // reps), BF16), v(down.shape, BF16),
            v((heads, block, HEAD_SIZE), BF16), v((heads, block, HEAD_SIZE), BF16),
            v(frozen.shape, BF16),
            v((slots, block, up_width), BF16), v((slots, block, up_width), BF16),
            v((slots, rank, block), BF16),
            v((KEY_HEADS, pairs, rows, 2 * block), F32),
            v((KEY_HEADS, pairs, rows, 2 * block), BF16),
            v((KEY_HEADS, rows, block), F32), v((rows, HEAD_SIZE), F32),
            v((KEY_HEADS, rows, HEAD_SIZE), F32), v((KEY_HEADS, rows, rank), F32),
            v((heads, block, HEAD_SIZE), BF16), v((heads, block, HEAD_SIZE), BF16),
            v((slots, rank, block), F32), v((slots, rank, block), F32),
            v((reps, rank, block), BF16),
            v((KEY_HEADS, rank, HEAD_SIZE), F32), v((reps, share, rank, HEAD_SIZE), F32),
            v((chunks, rank, chunk), BF16), v((slots, rank, chunk), BF16),
            v((reps, chunks, rank, chunk), BF16),
            dma((5,)), dma((heads,)), dma((heads,)), dma((heads,)), dma((heads,)),
            dma((slots,)), dma((slots,)), dma((slots,)),
            dma((slots,)), dma((slots,)), dma((slots,)),
            dma((slots,)), dma((slots,)), dma((slots,)),
            dma((reps,)), dma((reps,)), dma((slots,)), dma((slots,)),
            dma((reps,)), dma((reps,)), dma((reps,)), dma((reps,)),
            dma((slots,)), dma((slots,)), dma((slots,)), dma((slots,)),
            dma((reps, chunks)), dma((reps, chunks)),
        ],
        compiler_params=pltpu.CompilerParams(
            collective_id=0, has_side_effects=True, vmem_limit_bytes=60 * 1024 * 1024
        ),
        name="tree_attention",
    )(parents, lengths, x, q, k, frozen, down, up, g)
    return attended[None], query_grad[None], down_sum.T, up_sum


def solution(mesh):
    rows = P(("groups", "rep"), "node", None)
    table = P(("groups", "rep"), None)
    return jax.shard_map(
        on_device,
        mesh=mesh,
        in_specs=(rows, rows, rows, rows, P(), P(), rows, table, table),
        out_specs=(rows, rows, P("groups", None), P("groups", None)),
        check_vma=False,
    )
```

```python
import functools
import math

import jax
import jax.numpy as jnp
from jax import lax
from jax.experimental import pallas as pl
from jax.experimental.pallas import tpu as pltpu
from jax.sharding import PartitionSpec as P

KEY_HEADS = 4
HEAD_SIZE = 128
PROMPT = 2
SPAN = 5
STEPS = 1 + PROMPT + SPAN
NEGATIVE = -1e30
F32 = jnp.float32
BF16 = jnp.bfloat16
NT = (((1,), (1,)), ((), ()))
NN = (((1,), (0,)), ((), ()))
TN = (((0,), (0,)), ((), ()))
MESH_ID = pl.DeviceIdType.MESH


def dot(a, b, dims):
    return lax.dot_general(a, b, dims, preferred_element_type=F32)


def split(a):
    high = a.astype(BF16)
    return jnp.concatenate([high, (a - high.astype(F32)).astype(BF16)], axis=1)


def reaches(slot, below):
    return (below > slot) & ((slot < PROMPT) | (below - slot <= SPAN))


def first_pair(own):
    return jnp.maximum((own + 2 * SPAN - SPAN) // 2 - SPAN, 1)


def pair_count(slots):
    most = 1
    for own in range(slots):
        most = max(most, own // 2 - max((own - SPAN) // 2, 1) + 2)
    return most


def peer(node, rep=None):
    target = {"node": node}
    if rep is not None:
        target["rep"] = rep
    return target


def kernel(
    slots, reps, factor,
    parents, lengths, x_ref, q_ref, k_ref, frozen_ref, down_ref, up_ref, g_ref,
    att_ref, qg_ref, result,
    xs, xcat, downs, qs, gs, fs, kbuf, vbuf, lowbuf, score, weight, tops, facs, total, gup,
    atts, qgs, proj, landed, tbuf, upk, upland, parts, gathered,
    load_sem, qload, gload, store_a, store_q,
    k_col, k_fwd, k_recv, l_col, l_fwd, l_recv, v_col, v_fwd, v_recv,
    x_send, x_recv, p_send, p_recv, t_send, t_recv, u_send, u_recv,
    r_send, r_recv, a_send, a_recv, b_send, b_recv,
):
    own, rep = lax.axis_index("node"), lax.axis_index("rep")
    heads = qs.shape[0]
    per = heads // KEY_HEADS
    block = qs.shape[1]
    rows = per * block
    width = xs.shape[1]
    half = width // reps
    scale = HEAD_SIZE ** -0.5
    pair = own // 2
    partner = own + 1 - 2 * lax.rem(own, 2)
    pairs = pair - first_pair(own) + 2

    barrier = pltpu.get_barrier_semaphore()
    for step in range(reps):
        other = lax.rem(rep + step, reps)

        def signal(t, carry):
            pl.semaphore_signal(
                barrier, inc=1, device_id=peer(lax.rem(own + t, slots), other),
                device_id_type=MESH_ID,
            )
            return carry

        lax.fori_loop(0 if step else 1, slots, signal, 0)

    def remote(src, dst, send, recv, node, r=None):
        return pltpu.make_async_remote_copy(
            src_ref=src, dst_ref=dst, send_sem=send, recv_sem=recv,
            device_id=peer(node, r), device_id_type=MESH_ID,
        )

    loads = [
        pltpu.make_async_copy(k_ref, kbuf.at[own], load_sem.at[0]),
        pltpu.make_async_copy(down_ref, downs, load_sem.at[1]),
        pltpu.make_async_copy(x_ref, xs, load_sem.at[2]),
        pltpu.make_async_copy(frozen_ref, fs, load_sem.at[3]),
        pltpu.make_async_copy(
            x_ref.at[:, pl.ds(pl.multiple_of(rep * half, 128), half)], xcat.at[rep], load_sem.at[4]
        ),
    ]
    for c in loads:
        c.start()

    def head_copy(source, target, sem, i):
        return pltpu.make_async_copy(
            source.at[:, pl.ds(pl.multiple_of(i * HEAD_SIZE, HEAD_SIZE), HEAD_SIZE)],
            target.at[i], sem.at[i],
        )

    def head_store(source, target, sem, i):
        return pltpu.make_async_copy(
            source.at[i],
            target.at[:, pl.ds(pl.multiple_of(i * HEAD_SIZE, HEAD_SIZE), HEAD_SIZE)],
            sem.at[i],
        )

    def each(low, high, action):
        def body(i, carry):
            action(i)
            return carry

        lax.fori_loop(low, high, body, 0)

    each(0, heads, lambda i: head_copy(q_ref, qs, qload, i).start())
    each(0, heads, lambda i: head_copy(g_ref, gs, gload, i).start())

    chain = []
    current = own
    for _ in range(1, STEPS):
        parent = parents[0, jnp.maximum(current, 0)]
        current = jnp.where(current >= 0, parent, -1)
        chain.append(current)
    own_length = lengths[0, own]

    def limit(slot):
        found = slot == own
        for ancestor in chain:
            found = found | (slot == ancestor)
        return jnp.where(found, lengths[0, slot], 0)

    def unsent(slot):
        same = lax.rem(slot + own, 2) == 0
        lands = same & reaches(slot, 2 * pair) | reaches(slot, own)
        return jnp.logical_not(lands | (slot == own))

    def clear_slot(slot):
        proj[slot] = jnp.zeros(proj.shape[1:], F32)

        @pl.when(unsent(slot))
        def _():
            kbuf[slot] = jnp.zeros(kbuf.shape[1:], BF16)
            vbuf[slot] = jnp.zeros(vbuf.shape[1:], BF16)
            lowbuf[slot] = jnp.zeros(lowbuf.shape[1:], BF16)

    each(0, slots, clear_slot)

    loads[0].wait()
    pl.semaphore_wait(barrier, slots * reps - 1)

    def column(buf, send, recv, t):
        return remote(buf.at[own], buf.at[own], send.at[t], recv.at[own], own + 2 * t)

    def across(buf, send, recv, slot):
        return remote(buf.at[slot], buf.at[slot], send.at[slot], recv.at[slot], partner)

    def columns(action):
        def body(step):
            t = slots // 2 - 1 - step

            @pl.when((own + 2 * t < slots) & reaches(own, 2 * (pair + t)))
            def _():
                action(t)

        each(0, slots // 2 - 1, body)

    def own_across(action):
        @pl.when(reaches(own, partner))
        def _():
            action(own)

    def relayed(action):
        def body(t):
            slot = own - 2 * t

            @pl.when(reaches(slot, 2 * pair))
            def _():
                action(slot)

        each(1, pair + 1, body)

    def forward(buf, send, recv, t):
        slot = own - 2 * t

        @pl.when((t <= pair) & reaches(slot, 2 * pair))
        def _():
            across(buf, send, recv, slot).wait_recv()

            @pl.when(reaches(slot, partner))
            def _():
                across(buf, send, recv, slot).start()

    def from_partner(buf, send, recv, t):
        slot = partner - 2 * t

        @pl.when(reaches(slot, own))
        def _():
            across(buf, send, recv, slot).wait_recv()

    def send_own(buf, col, fwd, recv):
        own_across(lambda slot: across(buf, fwd, recv, slot).start())
        columns(lambda t: column(buf, col, recv, t).start())

    def drain(buf, col, fwd, recv):
        own_across(lambda slot: across(buf, fwd, recv, slot).wait_send())
        columns(lambda t: column(buf, col, recv, t).wait_send())

        def act(slot):
            @pl.when(reaches(slot, partner))
            def _():
                across(buf, fwd, recv, slot).wait_send()

        relayed(act)

    send_own(kbuf, k_col, k_fwd, k_recv)

    def swap_x(r):
        return remote(
            x_ref.at[:, pl.ds(pl.multiple_of(r * half, 128), half)], xcat.at[rep],
            x_send.at[r], x_recv.at[rep], own, r,
        )

    def other_reps(action):
        for step in range(1, reps):
            action(lax.rem(rep + step, reps))

    other_reps(lambda r: swap_x(r).start())

    loads[1].wait()
    loads[2].wait()
    low = dot(downs[...], xs[...], NT).astype(BF16)
    lowbuf[own] = low
    loads[3].wait()
    vbuf[own] = (fs[...].astype(F32) + dot(low, up_ref[...], TN)).astype(BF16)
    send_own(lowbuf, l_col, l_fwd, l_recv)

    each(0, heads, lambda i: head_copy(q_ref, qs, qload, i).wait())
    each(0, heads, lambda i: head_copy(g_ref, gs, gload, i).wait())

    def stacked(buf, kk):
        return buf[pl.ds(kk * per, per)].reshape(rows, HEAD_SIZE)

    def pair_at(step):
        return jnp.where(step == pairs - 1, 0, pair - step)

    def two(buf, index, kk):
        lanes = pl.ds(pl.multiple_of(kk * HEAD_SIZE, HEAD_SIZE), HEAD_SIZE)
        return buf[pl.ds(2 * index, 2), :, lanes].reshape(2 * block, HEAD_SIZE)

    for kk in range(KEY_HEADS):
        lanes = slice(kk * HEAD_SIZE, (kk + 1) * HEAD_SIZE)
        gup[kk] = dot(stacked(gs, kk), up_ref[:, lanes], NT)

    tune = scale * math.log2(math.e)
    rank = proj.shape[1]

    def wide(column):
        return jnp.broadcast_to(column, (rows, HEAD_SIZE))

    def scores(step, mask, first):
        index = pair_at(step)

        def one(kk):
            s = dot(stacked(qs, kk), two(kbuf, index, kk), NT)
            s = jnp.where(mask, s, NEGATIVE)
            most = jnp.max(jnp.maximum(s[:, :block], s[:, block:]), axis=1, keepdims=True)
            if not first:
                most = jnp.maximum(most, tops[kk, step - 1][:, :1])
            e = jnp.exp2((s - most) * tune)
            score[kk, step] = e
            weight[kk, step] = e.astype(BF16)
            tops[kk, step] = wide(most)
            facs[kk, step] = wide(jnp.sum(e[:, :block] + e[:, block:], axis=1, keepdims=True))

        each(0, KEY_HEADS, one)

    key = lax.broadcasted_iota(jnp.int32, (block, 2 * block), 1)
    place = lax.rem(key, block)
    query = lax.broadcasted_iota(jnp.int32, (block, 2 * block), 0)
    forward(kbuf, k_fwd, k_recv, 1)
    from_partner(kbuf, k_fwd, k_recv, 0)
    even, odd = limit(2 * pair), limit(2 * pair + 1)
    here = jnp.where(key < block, 2 * pair, 2 * pair + 1) == own
    mask = (place < jnp.where(key < block, even, odd)) & (jnp.logical_not(here) | (place <= query))
    scores(0, jnp.concatenate([mask] * per, axis=0), True)
    forward(kbuf, k_fwd, k_recv, 2)
    send_own(vbuf, v_col, v_fwd, v_recv)

    def later(t):
        @pl.when(t == pair)
        def _():
            forward(vbuf, v_fwd, v_recv, 1)

        from_partner(kbuf, k_fwd, k_recv, t)
        index = pair - t

        @pl.when((index == 0) | (index >= first_pair(own)))
        def _():
            step = jnp.where(index == 0, pairs - 1, t)
            even, odd = limit(2 * index), limit(2 * index + 1)
            col = lax.broadcasted_iota(jnp.int32, (rows, 2 * block), 1)
            mask = lax.rem(col, block) < jnp.where(col < block, even, odd)
            scores(step, mask, False)

        forward(kbuf, k_fwd, k_recv, t + 2)

    each(1, pair + 1, later)

    live = (lax.rem(lax.broadcasted_iota(jnp.int32, (rows, 1), 0), block) < own_length).astype(F32)

    def weigh(kk):
        most = tops[kk, pairs - 1]
        total[...] = jnp.zeros_like(total)

        def add(step):
            fall = jnp.exp2((tops[kk, step] - most) * tune)
            total[...] += facs[kk, step] * fall
            facs[kk, step] = fall

        each(0, pairs, add)
        total[...] = live / total[...]

        def project(step):
            index = pair_at(step)
            fac = facs[kk, step] * total[...]
            facs[kk, step] = fac
            both = dot(split(gup[kk] * fac[:, :rank]), weight[kk, step], TN)
            both = both[:rank] + both[rank:]
            proj[2 * index] += both[:, :block]
            proj[2 * index + 1] += both[:, block:]

        each(0, pairs, project)

    each(0, KEY_HEADS, weigh)

    def scatter(source, target):
        return remote(
            proj.at[target], landed.at[source], p_send.at[target], p_recv.at[source], target
        )

    def ancestors(action):
        def body(t):
            @pl.when(reaches(t, own))
            def _():
                action(t)

        each(0, slots, body)

    def descendants(action):
        def body(t):
            @pl.when(reaches(own, t))
            def _():
                action(t)

        each(0, slots, body)

    ancestors(lambda t: scatter(own, t).start())
    each(1, pair + 1, lambda t: forward(lowbuf, l_fwd, l_recv, t))
    each(2, pair + 1, lambda t: forward(vbuf, v_fwd, v_recv, t))
    each(0, pair + 1, lambda t: from_partner(lowbuf, l_fwd, l_recv, t))

    def low_weights(kk):
        total[:, :rank] = jnp.zeros((rows, rank), F32)

        def one(step):
            index = pair_at(step)
            lows = jnp.concatenate([lowbuf[2 * index], lowbuf[2 * index + 1]], axis=1)
            total[:, :rank] += dot(weight[kk, step], lows, NT) * facs[kk, step][:, :rank]

        each(0, pairs, one)
        sides = split(total[:, :rank])
        both = dot(sides, stacked(gs, kk), TN)
        upk[kk] = both[:rank] + both[rank:]

    each(0, KEY_HEADS, low_weights)
    share = KEY_HEADS // reps

    def swap_up(r):
        return remote(
            upk.at[pl.ds(r * share, share)], upland.at[rep], u_send.at[r], u_recv.at[rep], own, r
        )

    other_reps(lambda r: swap_up(r).start())

    def add_landed(t):
        remote(
            proj.at[t], landed.at[t], p_send.at[t], p_recv.at[t], t
        ).wait_recv()
        proj[own] += landed[t]

    descendants(add_landed)
    tbuf[rep] = proj[own].astype(BF16)

    def swap_total(r):
        return remote(tbuf.at[rep], tbuf.at[rep], t_send.at[r], t_recv.at[rep], own, r)

    other_reps(lambda r: swap_total(r).start())
    loads[4].wait()

    def arrivals(r):
        remote(
            x_ref.at[:, pl.ds(0, half)], xcat.at[r], x_send.at[r], x_recv.at[r], own, r
        ).wait_recv()
        remote(tbuf.at[r], tbuf.at[r], t_send.at[r], t_recv.at[r], own, r).wait_recv()
        remote(
            upk.at[pl.ds(0, share)], upland.at[r], u_send.at[r], u_recv.at[r], own, r
        ).wait_recv()

    other_reps(arrivals)

    projected = jnp.concatenate([tbuf[r] for r in range(reps)], axis=1)
    ups = upk[pl.ds(rep * share, share)]
    for step in range(1, reps):
        ups = ups + upland[lax.rem(rep + step, reps)]
    upland[rep] = ups
    chunks, _, chunk = parts.shape
    for j in range(chunks):
        lo, hi = j * chunk, (j + 1) * chunk
        pieces = []
        if lo < half:
            end = min(hi, half)
            pieces.append(dot(projected, xcat[:, :, lo:end].reshape(reps * block, end - lo), NN))
        for h in range(share):
            if lo <= half + h * HEAD_SIZE < hi:
                pieces.append(upland[rep, h])
        filled = sum(p.shape[1] for p in pieces)
        if filled < chunk:
            pieces.append(jnp.zeros((rank, chunk - filled), F32))
        value = pieces[0] if len(pieces) == 1 else jnp.concatenate(pieces, axis=1)
        parts[j] = value.astype(BF16)

    def reduce_copy(source, node):
        return remote(
            parts.at[node], gathered.at[source], r_send.at[node], r_recv.at[source], node
        )

    def others(action):
        each(1, slots, lambda t: action(lax.rem(own + t, slots)))

    def owners(action):
        def body(node):
            @pl.when(node < chunks)
            def _():
                action(node)

        others(body)

    owners(lambda node: reduce_copy(own, node).start())

    each(0, pair + 1, lambda t: from_partner(vbuf, v_fwd, v_recv, t))

    def outputs(kk):
        grad = stacked(gs, kk)
        total[...] = jnp.zeros_like(total)

        def attend(step):
            total[...] += dot(weight[kk, step], two(vbuf, pair_at(step), kk), NN) * facs[kk, step]

        each(0, pairs, attend)
        out = total[...]
        atts[pl.ds(kk * per, per)] = out.astype(BF16).reshape(per, block, HEAD_SIZE)
        dots = jnp.sum(grad.astype(F32) * out, axis=1, keepdims=True)
        total[...] = jnp.zeros_like(total)

        def back(step):
            index = pair_at(step)
            pressure = dot(grad, two(vbuf, index, kk), NT)
            slope = facs[kk, step] * scale
            slopes = (score[kk, step] * ((pressure - dots) * jnp.concatenate([slope, slope], axis=1))).astype(BF16)
            total[...] += dot(slopes, two(kbuf, index, kk), NN)

        each(0, pairs, back)
        qgs[pl.ds(kk * per, per)] = total[...].astype(BF16).reshape(per, block, HEAD_SIZE)

        def store(i):
            head_store(atts, att_ref, store_a, i).start()
            head_store(qgs, qg_ref, store_q, i).start()

        each(kk * per, (kk + 1) * per, store)

    outputs_early = 1
    each(0, outputs_early, outputs)

    def gather_copy(node, owner):
        return remote(
            result.at[rep, owner], result.at[rep, owner], a_send.at[node], a_recv.at[owner], node
        )

    def swap_result(r, owner):
        return remote(
            result.at[rep, owner], result.at[rep, owner], b_send.at[r, owner],
            b_recv.at[rep, owner], own, r,
        )

    @pl.when(own < chunks)
    def _():
        gathered[own] = parts[own]
        others(lambda node: remote(
            parts.at[own], gathered.at[node], r_send.at[node], r_recv.at[node], node
        ).wait_recv())
        acc = lax.fori_loop(
            0, slots, lambda t, a: a + gathered[t].astype(F32), jnp.zeros((rank, chunk), F32)
        )
        result[rep, own] = (acc * factor).astype(BF16)
        others(lambda node: gather_copy(node, own).start())
        other_reps(lambda r: swap_result(r, own).start())

    each(outputs_early, KEY_HEADS, outputs)

    def pass_on(owner):
        remote(
            result.at[rep, owner], result.at[rep, owner], a_send.at[owner], a_recv.at[owner], owner
        ).wait_recv()
        other_reps(lambda r: swap_result(r, owner).start())

    owners(pass_on)

    def from_reps(r):
        each(0, chunks, lambda owner: remote(
            result.at[r, owner], result.at[r, owner], b_send.at[r, owner], b_recv.at[r, owner],
            own, r,
        ).wait_recv())

    other_reps(from_reps)
    drain(kbuf, k_col, k_fwd, k_recv)
    drain(lowbuf, l_col, l_fwd, l_recv)
    drain(vbuf, v_col, v_fwd, v_recv)
    other_reps(lambda r: swap_x(r).wait_send())
    ancestors(lambda t: scatter(own, t).wait_send())
    other_reps(lambda r: swap_up(r).wait_send())
    other_reps(lambda r: swap_total(r).wait_send())
    owners(lambda node: reduce_copy(own, node).wait_send())

    @pl.when(own < chunks)
    def _():
        others(lambda node: gather_copy(node, own).wait_send())

    other_reps(lambda r: each(0, chunks, lambda owner: swap_result(r, owner).wait_send()))
    each(0, heads, lambda i: head_store(atts, att_ref, store_a, i).wait())
    each(0, heads, lambda i: head_store(qgs, qg_ref, store_q, i).wait())


def finish(cuts, a_ref, b_ref, r_ref, att_ref, qg_ref, down_ref, up_ref, a, b, res, down, up, ins, outs, sems):
    step = a_ref.shape[0] // cuts

    def move(i, source, target, sem, part):
        at = pl.ds(part * step, step)
        return pltpu.make_async_copy(source.at[at], target.at[at], sem.at[i, part])

    load = pltpu.make_async_copy(r_ref, res, sems.at[0])
    load.start()
    pieces = [(0, a_ref, a, att_ref), (1, b_ref, b, qg_ref)]
    for part in range(cuts):
        for i, source, buf, _ in pieces:
            move(i, source, buf, ins, part).start()
    load.wait()
    reps, chunks, rank, chunk = res.shape
    half = down.shape[1] // reps
    up_half = up.shape[1] // reps
    for r in range(reps):
        for j in range(chunks):
            lo, hi = j * chunk, (j + 1) * chunk
            if lo < half:
                end = min(hi, half)
                down[:, r * half + lo:r * half + end] = res[r, j, :, :end - lo].astype(F32)
            if hi > half and lo < half + up_half:
                first, last = max(lo, half), min(hi, half + up_half)
                base = r * up_half - half
                up[:, base + first:base + last] = res[r, j, :, first - lo:last - lo].astype(F32)
    stores = [
        pltpu.make_async_copy(down, down_ref, sems.at[1]),
        pltpu.make_async_copy(up, up_ref, sems.at[2]),
    ]
    for c in stores:
        c.start()
    for part in range(cuts):
        for i, source, buf, target in pieces:
            move(i, source, buf, ins, part).wait()
            move(i, buf, target, outs, part).start()
    for part in range(cuts):
        for i, source, buf, target in pieces:
            move(i, buf, target, outs, part).wait()
    for c in stores:
        c.wait()


def on_device(x, q, k, frozen, down, up, g, parents, lengths):
    x, q, k, frozen, g = x[0], q[0], k[0], frozen[0], g[0]
    block, width = x.shape
    slots, reps = lax.axis_size("node"), lax.axis_size("rep")
    rank, up_width = up.shape
    heads = q.shape[1] // HEAD_SIZE
    rows = heads // KEY_HEADS * block
    pairs = pair_count(slots)
    tiles = -(-(width + up_width) // reps // 128)
    per = -(-tiles // slots)
    chunks = -(-tiles // per)
    chunk = per * 128
    factor = (slots * reps * block) ** -0.5
    anywhere = pl.BlockSpec(memory_space=pl.ANY)
    vmem = pl.BlockSpec(memory_space=pltpu.VMEM)
    smem = pl.BlockSpec(memory_space=pltpu.SMEM)
    dma = pltpu.SemaphoreType.DMA
    v = pltpu.VMEM
    share = KEY_HEADS // reps
    attended, query_grad, result = pl.pallas_call(
        functools.partial(kernel, slots, reps, factor),
        in_specs=[smem, smem, anywhere, anywhere, anywhere, anywhere, anywhere, vmem, anywhere],
        out_specs=[anywhere, anywhere, vmem],
        out_shape=[
            jax.ShapeDtypeStruct(q.shape, BF16),
            jax.ShapeDtypeStruct(q.shape, BF16),
            jax.ShapeDtypeStruct((reps, chunks, rank, chunk), BF16),
        ],
        scratch_shapes=[
            v(x.shape, BF16), v((reps, block, width // reps), BF16), v((rank, width), BF16),
            v((heads, block, HEAD_SIZE), BF16), v((heads, block, HEAD_SIZE), BF16),
            v(frozen.shape, BF16),
            v((slots, block, up_width), BF16), v((slots, block, up_width), BF16),
            v((slots, rank, block), BF16),
            v((KEY_HEADS, pairs, rows, 2 * block), F32),
            v((KEY_HEADS, pairs, rows, 2 * block), BF16),
            v((KEY_HEADS, pairs, rows, HEAD_SIZE), F32), v((KEY_HEADS, pairs, rows, HEAD_SIZE), F32),
            v((rows, HEAD_SIZE), F32), v((KEY_HEADS, rows, rank), F32),
            v((heads, block, HEAD_SIZE), BF16), v((heads, block, HEAD_SIZE), BF16),
            v((slots, rank, block), F32), v((slots, rank, block), F32),
            v((reps, rank, block), BF16),
            v((KEY_HEADS, rank, HEAD_SIZE), F32), v((reps, share, rank, HEAD_SIZE), F32),
            v((chunks, rank, chunk), BF16), v((slots, rank, chunk), BF16),
            dma((5,)), dma((heads,)), dma((heads,)), dma((heads,)), dma((heads,)),
            dma((slots,)), dma((slots,)), dma((slots,)),
            dma((slots,)), dma((slots,)), dma((slots,)),
            dma((slots,)), dma((slots,)), dma((slots,)),
            dma((reps,)), dma((reps,)), dma((slots,)), dma((slots,)),
            dma((reps,)), dma((reps,)), dma((reps,)), dma((reps,)),
            dma((slots,)), dma((slots,)), dma((slots,)), dma((slots,)),
            dma((reps, chunks)), dma((reps, chunks)),
        ],
        compiler_params=pltpu.CompilerParams(
            collective_id=0, has_side_effects=True, vmem_limit_bytes=60 * 1024 * 1024
        ),
        name="tree_attention",
    )(parents, lengths, x, q, k, frozen, down.T, up, g)
    cuts = 2
    attended, query_grad, down_sum, up_sum = pl.pallas_call(
        functools.partial(finish, cuts),
        in_specs=[anywhere, anywhere, anywhere],
        out_specs=[anywhere, anywhere, anywhere, anywhere],
        out_shape=[
            jax.ShapeDtypeStruct(q.shape, BF16),
            jax.ShapeDtypeStruct(q.shape, BF16),
            jax.ShapeDtypeStruct((rank, width), F32),
            jax.ShapeDtypeStruct((rank, up_width), F32),
        ],
        scratch_shapes=[
            v(q.shape, BF16), v(q.shape, BF16), v(result.shape, BF16),
            v((rank, width), F32), v((rank, up_width), F32),
            dma((2, cuts)), dma((2, cuts)), dma((3,)),
        ],
        compiler_params=pltpu.CompilerParams(vmem_limit_bytes=60 * 1024 * 1024),
        name="finish",
    )(attended, query_grad, result)
    return attended[None], query_grad[None], down_sum.T, up_sum


def solution(mesh):
    rows = P(("groups", "rep"), "node", None)
    table = P(("groups", "rep"), None)
    return jax.shard_map(
        on_device,
        mesh=mesh,
        in_specs=(rows, rows, rows, rows, P(), P(), rows, table, table),
        out_specs=(rows, rows, P("groups", None), P("groups", None)),
        check_vma=False,
    )
```

```python
import functools
import math

import jax
import jax.numpy as jnp
from jax import lax
from jax.experimental import pallas as pl
from jax.experimental.pallas import tpu as pltpu
from jax.sharding import PartitionSpec as P

KEY_HEADS = 4
HEAD_SIZE = 128
PROMPT = 2
SPAN = 5
STEPS = 1 + PROMPT + SPAN
NEGATIVE = -1e30
F32 = jnp.float32
BF16 = jnp.bfloat16
NT = (((1,), (1,)), ((), ()))
NN = (((1,), (0,)), ((), ()))
TN = (((0,), (0,)), ((), ()))
MESH_ID = pl.DeviceIdType.MESH


def dot(a, b, dims):
    return lax.dot_general(a, b, dims, preferred_element_type=F32)


def reaches(slot, below):
    return (below > slot) & ((slot < PROMPT) | (below - slot <= SPAN))


def first_pair(own):
    return jnp.maximum((own + 2 * SPAN - SPAN) // 2 - SPAN, 1)


def pair_count(slots):
    most = 1
    for own in range(slots):
        most = max(most, own // 2 - max((own - SPAN) // 2, 1) + 2)
    return most


def peer(node, rep=None):
    target = {"node": node}
    if rep is not None:
        target["rep"] = rep
    return target


def kernel(
    slots, reps, factor,
    parents, lengths, x_ref, q_ref, k_ref, frozen_ref, down_ref, up_ref, g_ref,
    att_ref, qg_ref, result,
    xs, xcat, downs, qs, gs, fs, kbuf, vbuf, lowbuf, score, weight, tops, facs, acc, gup, gtr,
    vgrad, both, atts, qgs, proj, landed, tbuf, upk, upland, parts, gathered,
    load_sem, kload, qload, gload, store_a, store_q,
    k_col, k_fwd, k_recv, l_col, l_fwd, l_recv, v_col, v_fwd, v_recv,
    x_send, x_recv, p_send, p_recv, t_send, t_recv, u_send, u_recv,
    r_send, r_recv, a_send, a_recv, b_send, b_recv,
):
    own, rep = lax.axis_index("node"), lax.axis_index("rep")
    heads = qs.shape[0]
    per = heads // KEY_HEADS
    block = qs.shape[1]
    rows = per * block
    width = xs.shape[1]
    half = width // reps
    scale = HEAD_SIZE ** -0.5
    pair = own // 2
    partner = own + 1 - 2 * lax.rem(own, 2)
    pairs = pair - first_pair(own) + 2

    barrier = pltpu.get_barrier_semaphore()
    for step in range(reps):
        other = lax.rem(rep + step, reps)

        def signal(t, carry):
            pl.semaphore_signal(
                barrier, inc=1, device_id=peer(lax.rem(own + t, slots), other),
                device_id_type=MESH_ID,
            )
            return carry

        lax.fori_loop(0 if step else 1, slots, signal, 0)

    def remote(src, dst, send, recv, node, r=None):
        return pltpu.make_async_remote_copy(
            src_ref=src, dst_ref=dst, send_sem=send, recv_sem=recv,
            device_id=peer(node, r), device_id_type=MESH_ID,
        )

    loads = [
        pltpu.make_async_copy(down_ref, downs, load_sem.at[1]),
        pltpu.make_async_copy(x_ref, xs, load_sem.at[2]),
        pltpu.make_async_copy(frozen_ref, fs, load_sem.at[3]),
        pltpu.make_async_copy(
            x_ref.at[:, pl.ds(pl.multiple_of(rep * half, 128), half)], xcat.at[rep], load_sem.at[0]
        ),
    ]
    def key_load(kk):
        return pltpu.make_async_copy(
            k_ref.at[:, pl.ds(pl.multiple_of(kk * HEAD_SIZE, HEAD_SIZE), HEAD_SIZE)],
            kbuf.at[own, kk], kload.at[kk],
        )

    for kk in range(KEY_HEADS):
        key_load(kk).start()
    for c in loads:
        c.start()

    def head_copy(source, target, sem, i):
        return pltpu.make_async_copy(
            source.at[:, pl.ds(pl.multiple_of(i * HEAD_SIZE, HEAD_SIZE), HEAD_SIZE)],
            target.at[i], sem.at[i],
        )

    def head_store(source, target, sem, i):
        return pltpu.make_async_copy(
            source.at[i],
            target.at[:, pl.ds(pl.multiple_of(i * HEAD_SIZE, HEAD_SIZE), HEAD_SIZE)],
            sem.at[i],
        )

    def each(low, high, action):
        def body(i, carry):
            action(i)
            return carry

        lax.fori_loop(low, high, body, 0)

    each(0, heads, lambda i: head_copy(q_ref, qs, qload, i).start())
    each(0, heads, lambda i: head_copy(g_ref, gs, gload, i).start())

    chain = []
    current = own
    for _ in range(1, STEPS):
        parent = parents[0, jnp.maximum(current, 0)]
        current = jnp.where(current >= 0, parent, -1)
        chain.append(current)
    own_length = lengths[0, own]

    def limit(slot):
        found = slot == own
        for ancestor in chain:
            found = found | (slot == ancestor)
        return jnp.where(found, lengths[0, slot], 0)

    def unsent(slot):
        same = lax.rem(slot + own, 2) == 0
        lands = same & reaches(slot, 2 * pair) | reaches(slot, own)
        return jnp.logical_not(lands | (slot == own))

    def clear_slot(slot):
        proj[slot] = jnp.zeros(proj.shape[1:], F32)

        @pl.when(unsent(slot))
        def _():
            kbuf[slot] = jnp.zeros(kbuf.shape[1:], BF16)
            vbuf[slot] = jnp.zeros(vbuf.shape[1:], BF16)
            lowbuf[slot] = jnp.zeros(lowbuf.shape[1:], BF16)

    each(0, slots, clear_slot)

    for kk in range(KEY_HEADS):
        key_load(kk).wait()
    pl.semaphore_wait(barrier, slots * reps - 1)

    class Stream:
        def __init__(self, buf, col, fwd, recv):
            self.buf, self.col, self.fwd, self.recv = buf, col, fwd, recv

        def column(self, t, kk):
            return remote(
                self.buf.at[own, kk], self.buf.at[own, kk], self.col.at[t, kk],
                self.recv.at[own, kk], own + 2 * t,
            )

        def across(self, slot, kk):
            return remote(
                self.buf.at[slot, kk], self.buf.at[slot, kk], self.fwd.at[slot, kk],
                self.recv.at[slot, kk], partner,
            )

        def own_copies(self, kk, action):
            @pl.when(reaches(own, partner))
            def _():
                action(self.across(own, kk))

            def body(step):
                t = slots // 2 - 1 - step

                @pl.when((own + 2 * t < slots) & reaches(own, 2 * (pair + t)))
                def _():
                    action(self.column(t, kk))

            each(0, slots // 2 - 1, body)

        def send(self, kk):
            self.own_copies(kk, lambda c: c.start())

        def forward(self, kk):
            def body(t):
                slot = own - 2 * t

                @pl.when(reaches(slot, 2 * pair))
                def _():
                    self.across(slot, kk).wait_recv()

                    @pl.when(reaches(slot, partner))
                    def _():
                        self.across(slot, kk).start()

            each(1, pair + 1, body)

        def from_partner(self, t, kk):
            slot = partner - 2 * t

            @pl.when(reaches(slot, own))
            def _():
                self.across(slot, kk).wait_recv()

        def drain(self, kk):
            self.own_copies(kk, lambda c: c.wait_send())

            def body(t):
                slot = own - 2 * t

                @pl.when(reaches(slot, 2 * pair) & reaches(slot, partner))
                def _():
                    self.across(slot, kk).wait_send()

            each(1, pair + 1, body)

    keys = Stream(kbuf, k_col, k_fwd, k_recv)
    values = Stream(vbuf, v_col, v_fwd, v_recv)
    lows = Stream(lowbuf, l_col, l_fwd, l_recv)
    each(0, KEY_HEADS, keys.send)

    def swap_x(r):
        return remote(
            x_ref.at[:, pl.ds(pl.multiple_of(r * half, 128), half)], xcat.at[rep],
            x_send.at[r], x_recv.at[rep], own, r,
        )

    def other_reps(action):
        for step in range(1, reps):
            action(lax.rem(rep + step, reps))

    other_reps(lambda r: swap_x(r).start())

    loads[0].wait()
    loads[1].wait()
    low = dot(downs[...], xs[...], NT).astype(BF16)
    lowbuf[own, 0] = low
    loads[2].wait()
    own_values = (fs[...].astype(F32) + dot(low, up_ref[...], TN)).astype(BF16)
    for kk in range(KEY_HEADS):
        vbuf[own, kk] = own_values[:, kk * HEAD_SIZE:(kk + 1) * HEAD_SIZE]
    lows.send(0)

    each(0, heads, lambda i: head_copy(q_ref, qs, qload, i).wait())
    each(0, heads, lambda i: head_copy(g_ref, gs, gload, i).wait())

    def stacked(buf, kk):
        return buf[pl.ds(kk * per, per)].reshape(rows, HEAD_SIZE)

    def pair_at(step):
        return jnp.where(step == pairs - 1, 0, pair - step)

    def two(buf, index, kk):
        return buf[pl.ds(2 * index, 2), kk].reshape(2 * block, HEAD_SIZE)

    for kk in range(KEY_HEADS):
        lanes = slice(kk * HEAD_SIZE, (kk + 1) * HEAD_SIZE)
        gup[kk] = dot(up_ref[:, lanes], stacked(gs, kk), NT)
        for i in range(per):
            at = slice(i * block, (i + 1) * block)
            gtr[kk, :, at] = gs[kk * per + i].astype(F32).T.astype(BF16)

    tune = scale * math.log2(math.e)
    rank = proj.shape[1]
    eights = 2 * block // 8

    def times(a, row):
        return (a.reshape(-1, 8, rows) * row[None]).reshape(a.shape)

    def eight(row):
        return jnp.broadcast_to(row, (8, rows))

    def scores(kk, step, mask, first):
        s = dot(two(kbuf, pair_at(step), kk), stacked(qs, kk), NT)
        s = jnp.where(mask, s, NEGATIVE).reshape(eights, 8, rows)
        most = eight(jnp.max(jnp.max(s, axis=0), axis=0, keepdims=True))
        if not first:
            most = jnp.maximum(most, tops[kk, step - 1])
        e = jnp.exp2((s - most[None]) * tune)
        score[kk, step] = e.reshape(2 * block, rows)
        weight[kk, step] = e.reshape(2 * block, rows).astype(BF16)
        tops[kk, step] = most
        facs[kk, step] = eight(jnp.sum(jnp.sum(e, axis=0), axis=0, keepdims=True))

    def seen(index):
        return limit(2 * index), limit(2 * index + 1)

    def own_pair(kk):
        keys.from_partner(0, kk)
        key = lax.broadcasted_iota(jnp.int32, (2 * block, block), 0)
        place = lax.rem(key, block)
        query = lax.broadcasted_iota(jnp.int32, (2 * block, block), 1)
        even, odd = seen(pair)
        here = jnp.where(key < block, 2 * pair, 2 * pair + 1) == own
        mask = (place < jnp.where(key < block, even, odd)) & (
            jnp.logical_not(here) | (place <= query)
        )
        scores(kk, 0, jnp.concatenate([mask] * per, axis=1), True)

    def other_pairs(kk):
        def body(t):
            keys.from_partner(t, kk)
            index = pair - t

            @pl.when((index == 0) | (index >= first_pair(own)))
            def _():
                even, odd = seen(index)
                key = lax.broadcasted_iota(jnp.int32, (2 * block, rows), 0)
                mask = lax.rem(key, block) < jnp.where(key < block, even, odd)
                scores(kk, jnp.where(index == 0, pairs - 1, t), mask, False)

        each(1, pair + 1, body)

    keys.forward(0)

    def arrive(kk):
        @pl.when(kk + 1 < KEY_HEADS)
        def _():
            keys.forward(kk + 1)

        own_pair(kk)

        @pl.when(kk == 0)
        def _():
            each(0, KEY_HEADS, values.send)

        other_pairs(kk)

    each(0, KEY_HEADS, arrive)
    values.forward(0)
    live = (
        lax.rem(lax.broadcasted_iota(jnp.int32, (8, rows), 1), block) < own_length
    ).astype(F32)

    def clear_both(step):
        both[step] = jnp.zeros(both.shape[1:], F32)

    each(0, pairs, clear_both)

    def weigh(kk):
        most = tops[kk, pairs - 1]

        def add(step, total):
            fall = jnp.exp2((tops[kk, step] - most) * tune)
            total = total + facs[kk, step] * fall
            facs[kk, step] = fall
            return total

        inverse = live / lax.fori_loop(0, pairs, add, jnp.zeros((8, rows), F32))

        def project(step):
            fac = facs[kk, step] * inverse
            facs[kk, step] = fac
            side = times(gup[kk], fac)
            high = side.astype(BF16)
            right = jnp.concatenate(
                [times(gtr[kk].astype(F32), fac).astype(BF16), high,
                 (side - high.astype(F32)).astype(BF16)], axis=0,
            )
            out = dot(weight[kk, step], right, NT)
            vgrad[kk, step] = out[:, :HEAD_SIZE].astype(BF16)
            both[step] += out[:, HEAD_SIZE:]

        each(0, pairs, project)

    each(0, KEY_HEADS, weigh)

    def place(step):
        index = pair_at(step)
        turned = both[step].T
        turned = turned[:rank] + turned[rank:]
        proj[2 * index] = turned[:, :block]
        proj[2 * index + 1] = turned[:, block:]

    each(0, pairs, place)

    def scatter(source, target):
        return remote(
            proj.at[target], landed.at[source], p_send.at[target], p_recv.at[source], target
        )

    def ancestors(action):
        def body(t):
            @pl.when(reaches(t, own))
            def _():
                action(t)

        each(0, slots, body)

    def descendants(action):
        def body(t):
            @pl.when(reaches(own, t))
            def _():
                action(t)

        each(0, slots, body)

    ancestors(lambda t: scatter(own, t).start())
    lows.forward(0)
    values.forward(1)
    values.forward(2)
    each(0, pair + 1, lambda t: lows.from_partner(t, 0))

    def low_weights(kk):
        upk[kk] = jnp.zeros(upk.shape[1:], F32)

        def one(step):
            index = pair_at(step)
            low = jnp.concatenate([lowbuf[2 * index, 0], lowbuf[2 * index + 1, 0]], axis=1)
            upk[kk] += dot(low, vgrad[kk, step], NN)

        each(0, pairs, one)

    each(0, KEY_HEADS, low_weights)
    values.forward(3)
    share = KEY_HEADS // reps

    def swap_up(r):
        return remote(
            upk.at[pl.ds(r * share, share)], upland.at[rep], u_send.at[r], u_recv.at[rep], own, r
        )

    other_reps(lambda r: swap_up(r).start())

    def add_landed(t):
        remote(
            proj.at[t], landed.at[t], p_send.at[t], p_recv.at[t], t
        ).wait_recv()
        proj[own] += landed[t]

    descendants(add_landed)
    tbuf[rep] = proj[own].astype(BF16)

    def swap_total(r):
        return remote(tbuf.at[rep], tbuf.at[rep], t_send.at[r], t_recv.at[rep], own, r)

    other_reps(lambda r: swap_total(r).start())
    loads[3].wait()

    def arrivals(r):
        remote(
            x_ref.at[:, pl.ds(0, half)], xcat.at[r], x_send.at[r], x_recv.at[r], own, r
        ).wait_recv()
        remote(tbuf.at[r], tbuf.at[r], t_send.at[r], t_recv.at[r], own, r).wait_recv()
        remote(
            upk.at[pl.ds(0, share)], upland.at[r], u_send.at[r], u_recv.at[r], own, r
        ).wait_recv()

    other_reps(arrivals)

    projected = jnp.concatenate([tbuf[r] for r in range(reps)], axis=1)
    ups = upk[pl.ds(rep * share, share)]
    for step in range(1, reps):
        ups = ups + upland[lax.rem(rep + step, reps)]
    upland[rep] = ups
    chunks, _, chunk = parts.shape
    for j in range(chunks):
        lo, hi = j * chunk, (j + 1) * chunk
        pieces = []
        if lo < half:
            end = min(hi, half)
            pieces.append(dot(projected, xcat[:, :, lo:end].reshape(reps * block, end - lo), NN))
        for h in range(share):
            if lo <= half + h * HEAD_SIZE < hi:
                pieces.append(upland[rep, h])
        filled = sum(p.shape[1] for p in pieces)
        if filled < chunk:
            pieces.append(jnp.zeros((rank, chunk - filled), F32))
        value = pieces[0] if len(pieces) == 1 else jnp.concatenate(pieces, axis=1)
        parts[j] = value.astype(BF16)

    def reduce_copy(source, node):
        return remote(
            parts.at[node], gathered.at[source], r_send.at[node], r_recv.at[source], node
        )

    def others(action):
        each(1, slots, lambda t: action(lax.rem(own + t, slots)))

    def owners(action):
        def body(node):
            @pl.when(node < chunks)
            def _():
                action(node)

        others(body)

    owners(lambda node: reduce_copy(own, node).start())

    def outputs(kk):
        each(0, pair + 1, lambda t: values.from_partner(t, kk))
        grad = stacked(gs, kk)
        acc[...] = jnp.zeros_like(acc)

        def attend(step):
            acc[...] += times(
                dot(two(vbuf, pair_at(step), kk), weight[kk, step], TN), facs[kk, step]
            )

        each(0, pairs, attend)
        out = acc[...]
        dots = (gtr[kk].astype(F32) * out).reshape(HEAD_SIZE // 8, 8, rows)
        dots = eight(jnp.sum(jnp.sum(dots, axis=0), axis=0, keepdims=True))
        for i in range(per):
            atts[kk * per + i] = acc[:, i * block:(i + 1) * block].T.astype(BF16)
        acc[...] = jnp.zeros_like(acc)

        def back(step):
            index = pair_at(step)
            pressure = dot(two(vbuf, index, kk), grad, NT).reshape(eights, 8, rows)
            slopes = (pressure - dots[None]) * (facs[kk, step] * scale)[None]
            slopes = score[kk, step] * slopes.reshape(2 * block, rows)
            acc[...] += dot(two(kbuf, index, kk), slopes.astype(BF16), TN)

        each(0, pairs, back)
        for i in range(per):
            qgs[kk * per + i] = acc[:, i * block:(i + 1) * block].T.astype(BF16)

        def store(i):
            head_store(atts, att_ref, store_a, i).start()
            head_store(qgs, qg_ref, store_q, i).start()

        each(kk * per, (kk + 1) * per, store)

    outputs_early = 2
    each(0, outputs_early, outputs)

    def gather_copy(node, owner):
        return remote(
            result.at[rep, owner], result.at[rep, owner], a_send.at[node], a_recv.at[owner], node
        )

    def swap_result(r, owner):
        return remote(
            result.at[rep, owner], result.at[rep, owner], b_send.at[r, owner],
            b_recv.at[rep, owner], own, r,
        )

    @pl.when(own < chunks)
    def _():
        gathered[own] = parts[own]
        others(lambda node: remote(
            parts.at[own], gathered.at[node], r_send.at[node], r_recv.at[node], node
        ).wait_recv())
        acc = lax.fori_loop(
            0, slots, lambda t, a: a + gathered[t].astype(F32), jnp.zeros((rank, chunk), F32)
        )
        result[rep, own] = (acc * factor).astype(BF16)
        others(lambda node: gather_copy(node, own).start())
        other_reps(lambda r: swap_result(r, own).start())

    each(outputs_early, KEY_HEADS, outputs)

    def pass_on(owner):
        remote(
            result.at[rep, owner], result.at[rep, owner], a_send.at[owner], a_recv.at[owner], owner
        ).wait_recv()
        other_reps(lambda r: swap_result(r, owner).start())

    owners(pass_on)

    def from_reps(r):
        each(0, chunks, lambda owner: remote(
            result.at[r, owner], result.at[r, owner], b_send.at[r, owner], b_recv.at[r, owner],
            own, r,
        ).wait_recv())

    other_reps(from_reps)
    each(0, KEY_HEADS, keys.drain)
    lows.drain(0)
    each(0, KEY_HEADS, values.drain)
    other_reps(lambda r: swap_x(r).wait_send())
    ancestors(lambda t: scatter(own, t).wait_send())
    other_reps(lambda r: swap_up(r).wait_send())
    other_reps(lambda r: swap_total(r).wait_send())
    owners(lambda node: reduce_copy(own, node).wait_send())

    @pl.when(own < chunks)
    def _():
        others(lambda node: gather_copy(node, own).wait_send())

    other_reps(lambda r: each(0, chunks, lambda owner: swap_result(r, owner).wait_send()))
    each(0, heads, lambda i: head_store(atts, att_ref, store_a, i).wait())
    each(0, heads, lambda i: head_store(qgs, qg_ref, store_q, i).wait())


def finish(cuts, a_ref, b_ref, r_ref, att_ref, qg_ref, down_ref, up_ref, a, b, res, down, up, ins, outs, sems):
    step = a_ref.shape[0] // cuts

    def move(i, source, target, sem, part):
        at = pl.ds(part * step, step)
        return pltpu.make_async_copy(source.at[at], target.at[at], sem.at[i, part])

    load = pltpu.make_async_copy(r_ref, res, sems.at[0])
    load.start()
    pieces = [(0, a_ref, a, att_ref), (1, b_ref, b, qg_ref)]
    for part in range(cuts):
        for i, source, buf, _ in pieces:
            move(i, source, buf, ins, part).start()
    load.wait()
    reps, chunks, rank, chunk = res.shape
    half = down.shape[1] // reps
    up_half = up.shape[1] // reps
    for r in range(reps):
        for j in range(chunks):
            lo, hi = j * chunk, (j + 1) * chunk
            if lo < half:
                end = min(hi, half)
                down[:, r * half + lo:r * half + end] = res[r, j, :, :end - lo].astype(F32)
            if hi > half and lo < half + up_half:
                first, last = max(lo, half), min(hi, half + up_half)
                base = r * up_half - half
                up[:, base + first:base + last] = res[r, j, :, first - lo:last - lo].astype(F32)
    stores = [
        pltpu.make_async_copy(down, down_ref, sems.at[1]),
        pltpu.make_async_copy(up, up_ref, sems.at[2]),
    ]
    for c in stores:
        c.start()
    for part in range(cuts):
        for i, source, buf, target in pieces:
            move(i, source, buf, ins, part).wait()
            move(i, buf, target, outs, part).start()
    for part in range(cuts):
        for i, source, buf, target in pieces:
            move(i, buf, target, outs, part).wait()
    for c in stores:
        c.wait()


def on_device(x, q, k, frozen, down, up, g, parents, lengths):
    x, q, k, frozen, g = x[0], q[0], k[0], frozen[0], g[0]
    block, width = x.shape
    slots, reps = lax.axis_size("node"), lax.axis_size("rep")
    rank, up_width = up.shape
    heads = q.shape[1] // HEAD_SIZE
    rows = heads // KEY_HEADS * block
    pairs = pair_count(slots)
    tiles = -(-(width + up_width) // reps // 128)
    per = -(-tiles // slots)
    chunks = -(-tiles // per)
    chunk = per * 128
    factor = (slots * reps * block) ** -0.5
    anywhere = pl.BlockSpec(memory_space=pl.ANY)
    vmem = pl.BlockSpec(memory_space=pltpu.VMEM)
    smem = pl.BlockSpec(memory_space=pltpu.SMEM)
    dma = pltpu.SemaphoreType.DMA
    v = pltpu.VMEM
    share = KEY_HEADS // reps
    attended, query_grad, result = pl.pallas_call(
        functools.partial(kernel, slots, reps, factor),
        in_specs=[smem, smem, anywhere, anywhere, anywhere, anywhere, anywhere, vmem, anywhere],
        out_specs=[anywhere, anywhere, vmem],
        out_shape=[
            jax.ShapeDtypeStruct(q.shape, BF16),
            jax.ShapeDtypeStruct(q.shape, BF16),
            jax.ShapeDtypeStruct((reps, chunks, rank, chunk), BF16),
        ],
        scratch_shapes=[
            v(x.shape, BF16), v((reps, block, width // reps), BF16), v((rank, width), BF16),
            v((heads, block, HEAD_SIZE), BF16), v((heads, block, HEAD_SIZE), BF16),
            v(frozen.shape, BF16),
            v((slots, KEY_HEADS, block, HEAD_SIZE), BF16),
            v((slots, KEY_HEADS, block, HEAD_SIZE), BF16),
            v((slots, 1, rank, block), BF16),
            v((KEY_HEADS, pairs, 2 * block, rows), F32),
            v((KEY_HEADS, pairs, 2 * block, rows), BF16),
            v((KEY_HEADS, pairs, 8, rows), F32), v((KEY_HEADS, pairs, 8, rows), F32),
            v((HEAD_SIZE, rows), F32), v((KEY_HEADS, rank, rows), F32),
            v((KEY_HEADS, HEAD_SIZE, rows), BF16),
            v((KEY_HEADS, pairs, 2 * block, HEAD_SIZE), BF16),
            v((pairs, 2 * block, 2 * rank), F32),
            v((heads, block, HEAD_SIZE), BF16), v((heads, block, HEAD_SIZE), BF16),
            v((slots, rank, block), F32), v((slots, rank, block), F32),
            v((reps, rank, block), BF16),
            v((KEY_HEADS, rank, HEAD_SIZE), F32), v((reps, share, rank, HEAD_SIZE), F32),
            v((chunks, rank, chunk), BF16), v((slots, rank, chunk), BF16),
            dma((4,)), dma((KEY_HEADS,)), dma((heads,)), dma((heads,)), dma((heads,)), dma((heads,)),
            dma((slots, KEY_HEADS)), dma((slots, KEY_HEADS)), dma((slots, KEY_HEADS)),
            dma((slots, 1)), dma((slots, 1)), dma((slots, 1)),
            dma((slots, KEY_HEADS)), dma((slots, KEY_HEADS)), dma((slots, KEY_HEADS)),
            dma((reps,)), dma((reps,)), dma((slots,)), dma((slots,)),
            dma((reps,)), dma((reps,)), dma((reps,)), dma((reps,)),
            dma((slots,)), dma((slots,)), dma((slots,)), dma((slots,)),
            dma((reps, chunks)), dma((reps, chunks)),
        ],
        compiler_params=pltpu.CompilerParams(
            collective_id=0, has_side_effects=True, vmem_limit_bytes=60 * 1024 * 1024
        ),
        name="tree_attention",
    )(parents, lengths, x, q, k, frozen, down.T, up, g)
    cuts = 2
    attended, query_grad, down_sum, up_sum = pl.pallas_call(
        functools.partial(finish, cuts),
        in_specs=[anywhere, anywhere, anywhere],
        out_specs=[anywhere, anywhere, anywhere, anywhere],
        out_shape=[
            jax.ShapeDtypeStruct(q.shape, BF16),
            jax.ShapeDtypeStruct(q.shape, BF16),
            jax.ShapeDtypeStruct((rank, width), F32),
            jax.ShapeDtypeStruct((rank, up_width), F32),
        ],
        scratch_shapes=[
            v(q.shape, BF16), v(q.shape, BF16), v(result.shape, BF16),
            v((rank, width), F32), v((rank, up_width), F32),
            dma((2, cuts)), dma((2, cuts)), dma((3,)),
        ],
        compiler_params=pltpu.CompilerParams(vmem_limit_bytes=60 * 1024 * 1024),
        name="finish",
    )(attended, query_grad, result)
    return attended[None], query_grad[None], down_sum.T, up_sum


def solution(mesh):
    rows = P(("groups", "rep"), "node", None)
    table = P(("groups", "rep"), None)
    return jax.shard_map(
        on_device,
        mesh=mesh,
        in_specs=(rows, rows, rows, rows, P(), P(), rows, table, table),
        out_specs=(rows, rows, P("groups", None), P("groups", None)),
        check_vma=False,
    )
```

```python
import functools
import math

import jax
import jax.numpy as jnp
from jax import lax
from jax.experimental import pallas as pl
from jax.experimental.pallas import tpu as pltpu
from jax.sharding import PartitionSpec as P

KEY_HEADS = 4
HEAD_SIZE = 128
PROMPT = 2
SPAN = 5
STEPS = 1 + PROMPT + SPAN
NEGATIVE = -1e30
F32 = jnp.float32
BF16 = jnp.bfloat16
NT = (((1,), (1,)), ((), ()))
NN = (((1,), (0,)), ((), ()))
TN = (((0,), (0,)), ((), ()))
MESH_ID = pl.DeviceIdType.MESH


def dot(a, b, dims):
    return lax.dot_general(a, b, dims, preferred_element_type=F32)


def reaches(slot, below):
    return (below > slot) & ((slot < PROMPT) | (below - slot <= SPAN))


def first_pair(own):
    return jnp.maximum((own + 2 * SPAN - SPAN) // 2 - SPAN, 1)


def pair_count(slots):
    most = 1
    for own in range(slots):
        most = max(most, own // 2 - max((own - SPAN) // 2, 1) + 2)
    return most


def peer(node, rep=None):
    target = {"node": node}
    if rep is not None:
        target["rep"] = rep
    return target


def kernel(
    slots, reps, factor,
    parents, lengths, x_ref, q_ref, k_ref, frozen_ref, down_ref, up_ref, g_ref,
    att_ref, qg_ref, result,
    xs, xcat, downs, qs, gs, fs, kbuf, vbuf, lowbuf, score, weight, tops, facs, acc, gup, gtr,
    vgrad, both, invs, atts, qgs, proj, mine, landed, tbuf, upk, upland, parts, gathered,
    load_sem, stored, k_recv, l_recv, v_recv, col_send, fwd_send, l_col, l_fwd,
    x_recv, x_send, t_recv, t_send, u_recv, u_send, p_recv, p_send,
    r_recv, r_send, a_recv, a_send, b_recv, b_send,
):
    own, rep = lax.axis_index("node"), lax.axis_index("rep")
    heads = qs.shape[0]
    per = heads // KEY_HEADS
    block = qs.shape[1]
    rows = per * block
    width = xs.shape[1]
    half = width // reps
    scale = HEAD_SIZE ** -0.5
    pair = own // 2
    partner = own + 1 - 2 * lax.rem(own, 2)
    pairs = pair - first_pair(own) + 2

    barrier = pltpu.get_barrier_semaphore()
    for step in range(reps):
        other = lax.rem(rep + step, reps)

        def signal(t, carry):
            pl.semaphore_signal(
                barrier, inc=1, device_id=peer(lax.rem(own + t, slots), other),
                device_id_type=MESH_ID,
            )
            return carry

        lax.fori_loop(0 if step else 1, slots, signal, 0)

    def remote(src, dst, send, recv, node, r=None):
        return pltpu.make_async_remote_copy(
            src_ref=src, dst_ref=dst, send_sem=send, recv_sem=recv,
            device_id=peer(node, r), device_id_type=MESH_ID,
        )

    loads = [
        pltpu.make_async_copy(down_ref, downs, load_sem.at[1]),
        pltpu.make_async_copy(x_ref, xs, load_sem.at[2]),
        pltpu.make_async_copy(frozen_ref, fs, load_sem.at[3]),
        pltpu.make_async_copy(
            x_ref.at[:, pl.ds(pl.multiple_of(rep * half, 128), half)], xcat.at[rep], load_sem.at[0]
        ),
    ]
    def key_load(kk):
        return pltpu.make_async_copy(
            k_ref.at[:, pl.ds(pl.multiple_of(kk * HEAD_SIZE, HEAD_SIZE), HEAD_SIZE)],
            kbuf.at[own, kk], load_sem.at[4],
        )

    for kk in range(KEY_HEADS):
        key_load(kk).start()
    for c in loads:
        c.start()

    def head_copy(source, target, sem, i):
        return pltpu.make_async_copy(
            source.at[:, pl.ds(pl.multiple_of(i * HEAD_SIZE, HEAD_SIZE), HEAD_SIZE)],
            target.at[i], sem,
        )

    def head_store(source, target, sem, i):
        return pltpu.make_async_copy(
            source.at[i],
            target.at[:, pl.ds(pl.multiple_of(i * HEAD_SIZE, HEAD_SIZE), HEAD_SIZE)],
            sem,
        )

    def all_of(buf, sem):
        return pltpu.make_async_copy(buf, buf, sem)

    def each(low, high, action):
        def body(i, carry):
            action(i)
            return carry

        lax.fori_loop(low, high, body, 0)

    each(0, heads, lambda i: head_copy(q_ref, qs, load_sem.at[5], i).start())
    each(0, heads, lambda i: head_copy(g_ref, gs, load_sem.at[6], i).start())

    chain = []
    current = own
    for _ in range(1, STEPS):
        parent = parents[0, jnp.maximum(current, 0)]
        current = jnp.where(current >= 0, parent, -1)
        chain.append(current)
    own_length = lengths[0, own]

    def limit(slot):
        found = slot == own
        for ancestor in chain:
            found = found | (slot == ancestor)
        return jnp.where(found, lengths[0, slot], 0)

    def unsent(slot):
        same = lax.rem(slot + own, 2) == 0
        lands = same & reaches(slot, 2 * pair) | reaches(slot, own)
        return jnp.logical_not(lands | (slot == own))

    def clear_slot(slot):
        @pl.when(unsent(slot))
        def _():
            kbuf[slot] = jnp.zeros(kbuf.shape[1:], BF16)
            vbuf[slot] = jnp.zeros(vbuf.shape[1:], BF16)
            lowbuf[slot] = jnp.zeros(lowbuf.shape[1:], BF16)

    each(0, slots, clear_slot)

    all_of(kbuf.at[own], load_sem.at[4]).wait()
    pl.semaphore_wait(barrier, slots * reps - 1)

    class Stream:
        def __init__(self, buf, col, fwd, recv):
            self.buf, self.col, self.fwd, self.recv = buf, col, fwd, recv

        def column(self, t, kk):
            block = self.buf.at[own, kk]
            return remote(block, block, self.col.at[t], self.recv(own, kk), own + 2 * t)

        def across(self, slot, kk):
            block = self.buf.at[slot, kk]
            return remote(
                block, block, self.fwd.at[(own - slot) // 2], self.recv(slot, kk), partner
            )

        def arrival(self, slot, kk):
            block = self.buf.at[slot, kk]
            return remote(block, block, self.fwd.at[0], self.recv(slot, kk), partner)

        def targets(self, across, column):
            @pl.when(reaches(own, partner))
            def _():
                across()

            def body(step):
                t = slots // 2 - 1 - step

                @pl.when((own + 2 * t < slots) & reaches(own, 2 * (pair + t)))
                def _():
                    column(t)

            each(0, slots // 2 - 1, body)

        def send(self, kk):
            self.targets(
                lambda: self.across(own, kk).start(), lambda t: self.column(t, kk).start()
            )

        def forward(self, kk):
            def body(t):
                slot = own - 2 * t

                @pl.when(reaches(slot, 2 * pair))
                def _():
                    self.arrival(slot, kk).wait_recv()

                    @pl.when(reaches(slot, partner))
                    def _():
                        self.across(slot, kk).start()

            each(1, pair + 1, body)

        def from_partner(self, t, kk):
            slot = partner - 2 * t

            @pl.when(reaches(slot, own))
            def _():
                self.arrival(slot, kk).wait_recv()

        def drain(self, sent):
            self.targets(
                lambda: all_of(sent, self.fwd.at[0]).wait(),
                lambda t: all_of(sent, self.col.at[t]).wait(),
            )

            def body(t):
                slot = own - 2 * t

                @pl.when(reaches(slot, 2 * pair) & reaches(slot, partner))
                def _():
                    all_of(sent, self.fwd.at[t]).wait()

            each(1, pair + 1, body)

    keys = Stream(kbuf, col_send, fwd_send, lambda slot, kk: k_recv.at[slot, kk])
    values = Stream(vbuf, col_send, fwd_send, lambda slot, kk: v_recv.at[slot, kk])
    lows = Stream(lowbuf, l_col, l_fwd, lambda slot, kk: l_recv.at[slot])
    each(0, KEY_HEADS, keys.send)

    def swap_x(r):
        return remote(
            x_ref.at[:, pl.ds(pl.multiple_of(r * half, 128), half)], xcat.at[rep],
            x_send.at[r], x_recv.at[rep], own, r,
        )

    def other_reps(action):
        for step in range(1, reps):
            action(lax.rem(rep + step, reps))

    other_reps(lambda r: swap_x(r).start())

    loads[0].wait()
    loads[1].wait()
    low = dot(downs[...], xs[...], NT).astype(BF16)
    lowbuf[own, 0] = low
    loads[2].wait()
    own_values = (fs[...].astype(F32) + dot(low, up_ref[...], TN)).astype(BF16)
    for kk in range(KEY_HEADS):
        vbuf[own, kk] = own_values[:, kk * HEAD_SIZE:(kk + 1) * HEAD_SIZE]
    lows.send(0)

    all_of(qs, load_sem.at[5]).wait()
    all_of(gs, load_sem.at[6]).wait()

    def stacked(buf, kk):
        return buf[pl.ds(kk * per, per)].reshape(rows, HEAD_SIZE)

    def pair_at(step):
        return jnp.where(step == pairs - 1, 0, pair - step)

    def two(buf, index, kk):
        return buf[pl.ds(2 * index, 2), kk].reshape(2 * block, HEAD_SIZE)

    for kk in range(KEY_HEADS):
        lanes = slice(kk * HEAD_SIZE, (kk + 1) * HEAD_SIZE)
        gup[kk] = dot(up_ref[:, lanes], stacked(gs, kk), NT)
        for i in range(per):
            at = slice(i * block, (i + 1) * block)
            gtr[kk, :, at] = gs[kk * per + i].astype(F32).T.astype(BF16)

    tune = scale * math.log2(math.e)
    rank = proj.shape[1]
    eights = 2 * block // 8

    def times(a, row):
        return (a.reshape(-1, 8, rows) * row[None]).reshape(a.shape)

    def eight(row):
        return jnp.broadcast_to(row, (8, rows))

    def scores(kk, step, mask, first):
        s = dot(two(kbuf, pair_at(step), kk), stacked(qs, kk), NT)
        s = jnp.where(mask, s, NEGATIVE).reshape(eights, 8, rows)
        most = eight(jnp.max(jnp.max(s, axis=0), axis=0, keepdims=True))
        if not first:
            most = jnp.maximum(most, tops[kk, step - 1])
        e = jnp.exp2((s - most[None]) * tune)
        score[kk, step] = e.reshape(2 * block, rows)
        weight[kk, step] = e.reshape(2 * block, rows).astype(BF16)
        tops[kk, step] = most
        facs[kk, step] = eight(jnp.sum(jnp.sum(e, axis=0), axis=0, keepdims=True))

    def seen(index):
        return limit(2 * index), limit(2 * index + 1)

    def own_pair(kk):
        keys.from_partner(0, kk)
        key = lax.broadcasted_iota(jnp.int32, (2 * block, block), 0)
        place = lax.rem(key, block)
        query = lax.broadcasted_iota(jnp.int32, (2 * block, block), 1)
        even, odd = seen(pair)
        here = jnp.where(key < block, 2 * pair, 2 * pair + 1) == own
        mask = (place < jnp.where(key < block, even, odd)) & (
            jnp.logical_not(here) | (place <= query)
        )
        scores(kk, 0, jnp.concatenate([mask] * per, axis=1), True)

    def other_pairs(kk):
        def body(t):
            keys.from_partner(t, kk)
            index = pair - t

            @pl.when((index == 0) | (index >= first_pair(own)))
            def _():
                even, odd = seen(index)
                key = lax.broadcasted_iota(jnp.int32, (2 * block, rows), 0)
                mask = lax.rem(key, block) < jnp.where(key < block, even, odd)
                scores(kk, jnp.where(index == 0, pairs - 1, t), mask, False)

        each(1, pair + 1, body)

    keys.forward(0)

    def arrive(kk):
        @pl.when(kk + 1 < KEY_HEADS)
        def _():
            keys.forward(kk + 1)

        @pl.when(kk == KEY_HEADS - 1)
        def _():
            lows.forward(0)

        own_pair(kk)

        @pl.when(kk == 0)
        def _():
            each(0, KEY_HEADS, values.send)

        other_pairs(kk)

    each(0, KEY_HEADS, arrive)
    values.forward(0)
    live = (
        lax.rem(lax.broadcasted_iota(jnp.int32, (8, rows), 1), block) < own_length
    ).astype(F32)

    def weigh(kk):
        most = tops[kk, pairs - 1]

        def add(step, total):
            fall = jnp.exp2((tops[kk, step] - most) * tune)
            total = total + facs[kk, step] * fall
            facs[kk, step] = fall
            return total

        invs[kk] = live / lax.fori_loop(0, pairs, add, jnp.zeros((8, rows), F32))

    each(0, KEY_HEADS, weigh)

    def scatter(source, target):
        return remote(
            proj.at[target], landed.at[source], p_send.at[target], p_recv.at[source], target
        )

    def project(i):
        step = pairs - 1 - i
        index = pair_at(step)
        both[...] = jnp.zeros_like(both)

        def head(kk):
            fac = facs[kk, step] * invs[kk]
            facs[kk, step] = fac
            side = times(gup[kk], fac)
            high = side.astype(BF16)
            right = jnp.concatenate(
                [times(gtr[kk].astype(F32), fac).astype(BF16), high,
                 (side - high.astype(F32)).astype(BF16)], axis=0,
            )
            out = dot(weight[kk, step], right, NT)
            vgrad[kk, step] = out[:, :HEAD_SIZE].astype(BF16)
            both[...] += out[:, HEAD_SIZE:]

        each(0, KEY_HEADS, head)
        turned = both[...].T
        turned = turned[:rank] + turned[rank:]
        for parity in range(2):
            slot = 2 * index + parity
            mine[parity] = turned[:, parity * block:(parity + 1) * block]
            proj[slot] = mine[parity].astype(BF16)

            @pl.when(reaches(slot, own))
            def _():
                scatter(own, slot).start()

    each(0, pairs, project)

    def ancestors(action):
        def body(t):
            @pl.when(reaches(t, own))
            def _():
                action(t)

        each(0, slots, body)

    def descendants(action):
        def body(t):
            @pl.when(reaches(own, t))
            def _():
                action(t)

        each(0, slots, body)

    values.forward(1)
    values.forward(2)
    each(0, pair + 1, lambda t: lows.from_partner(t, 0))

    def low_weights(kk):
        upk[kk] = jnp.zeros(upk.shape[1:], F32)

        def one(step):
            index = pair_at(step)
            low = jnp.concatenate([lowbuf[2 * index, 0], lowbuf[2 * index + 1, 0]], axis=1)
            upk[kk] += dot(low, vgrad[kk, step], NN)

        each(0, pairs, one)

    each(0, KEY_HEADS, low_weights)
    values.forward(3)
    share = KEY_HEADS // reps

    def swap_up(r):
        return remote(
            upk.at[pl.ds(r * share, share)], upland.at[rep], u_send.at[r], u_recv.at[rep], own, r
        )

    other_reps(lambda r: swap_up(r).start())

    descendants(lambda t: remote(
        proj.at[t], landed.at[t], p_send.at[t], p_recv.at[t], t
    ).wait_recv())
    total = mine[lax.rem(own, 2)]

    def add_landed(t):
        @pl.when(reaches(own, t))
        def _():
            mine[0] += landed[t].astype(F32)

    mine[0] = total
    each(0, slots, add_landed)
    tbuf[rep] = mine[0].astype(BF16)

    def swap_total(r):
        return remote(tbuf.at[rep], tbuf.at[rep], t_send.at[r], t_recv.at[rep], own, r)

    other_reps(lambda r: swap_total(r).start())
    loads[3].wait()

    def arrivals(r):
        remote(
            x_ref.at[:, pl.ds(0, half)], xcat.at[r], x_send.at[r], x_recv.at[r], own, r
        ).wait_recv()
        remote(tbuf.at[r], tbuf.at[r], t_send.at[r], t_recv.at[r], own, r).wait_recv()
        remote(
            upk.at[pl.ds(0, share)], upland.at[r], u_send.at[r], u_recv.at[r], own, r
        ).wait_recv()

    other_reps(arrivals)

    projected = jnp.concatenate([tbuf[r] for r in range(reps)], axis=1)
    ups = upk[pl.ds(rep * share, share)]
    for step in range(1, reps):
        ups = ups + upland[lax.rem(rep + step, reps)]
    upland[rep] = ups
    chunks, _, chunk = parts.shape
    for j in range(chunks):
        lo, hi = j * chunk, (j + 1) * chunk
        pieces = []
        if lo < half:
            end = min(hi, half)
            pieces.append(dot(projected, xcat[:, :, lo:end].reshape(reps * block, end - lo), NN))
        for h in range(share):
            if lo <= half + h * HEAD_SIZE < hi:
                pieces.append(upland[rep, h])
        filled = sum(p.shape[1] for p in pieces)
        if filled < chunk:
            pieces.append(jnp.zeros((rank, chunk - filled), F32))
        value = pieces[0] if len(pieces) == 1 else jnp.concatenate(pieces, axis=1)
        parts[j] = value.astype(BF16)

    def reduce_copy(source, node):
        return remote(
            parts.at[node], gathered.at[source], r_send, r_recv, node
        )

    def others(action):
        each(1, slots, lambda t: action(lax.rem(own + t, slots)))

    def owners(action):
        def body(node):
            @pl.when(node < chunks)
            def _():
                action(node)

        others(body)

    owners(lambda node: reduce_copy(own, node).start())

    def outputs(kk):
        each(0, pair + 1, lambda t: values.from_partner(t, kk))
        grad = stacked(gs, kk)
        acc[...] = jnp.zeros_like(acc)

        def attend(step):
            acc[...] += times(
                dot(two(vbuf, pair_at(step), kk), weight[kk, step], TN), facs[kk, step]
            )

        each(0, pairs, attend)
        out = acc[...]
        dots = (gtr[kk].astype(F32) * out).reshape(HEAD_SIZE // 8, 8, rows)
        dots = eight(jnp.sum(jnp.sum(dots, axis=0), axis=0, keepdims=True))
        for i in range(per):
            atts[kk * per + i] = acc[:, i * block:(i + 1) * block].T.astype(BF16)
        acc[...] = jnp.zeros_like(acc)

        def back(step):
            index = pair_at(step)
            pressure = dot(two(vbuf, index, kk), grad, NT).reshape(eights, 8, rows)
            slopes = (pressure - dots[None]) * (facs[kk, step] * scale)[None]
            slopes = score[kk, step] * slopes.reshape(2 * block, rows)
            acc[...] += dot(two(kbuf, index, kk), slopes.astype(BF16), TN)

        each(0, pairs, back)
        for i in range(per):
            qgs[kk * per + i] = acc[:, i * block:(i + 1) * block].T.astype(BF16)

        def store(i):
            head_store(atts, att_ref, stored.at[0], i).start()
            head_store(qgs, qg_ref, stored.at[1], i).start()

        each(kk * per, (kk + 1) * per, store)

    outputs_early = 2
    each(0, outputs_early, outputs)

    def gather_copy(node, owner):
        return remote(
            result.at[rep, owner], result.at[rep, owner], a_send, a_recv.at[owner], node
        )

    def swap_result(r, owner):
        return remote(
            result.at[rep, owner], result.at[rep, owner], b_send.at[r], b_recv.at[rep], own, r
        )

    @pl.when(own < chunks)
    def _():
        gathered[own] = parts[own]
        all_of(gathered.at[pl.ds(0, slots - 1)], r_recv).wait()
        acc = lax.fori_loop(
            0, slots, lambda t, a: a + gathered[t].astype(F32), jnp.zeros((rank, chunk), F32)
        )
        result[rep, own] = (acc * factor).astype(BF16)
        others(lambda node: gather_copy(node, own).start())
        other_reps(lambda r: swap_result(r, own).start())

    each(outputs_early, KEY_HEADS, outputs)

    def pass_on(owner):
        remote(
            result.at[rep, owner], result.at[rep, owner], a_send, a_recv.at[owner], owner
        ).wait_recv()
        other_reps(lambda r: swap_result(r, owner).start())

    owners(pass_on)

    other_reps(lambda r: all_of(result.at[r], b_recv.at[r]).wait())
    keys.drain(kbuf.at[pl.ds(0, 2)])
    lows.drain(lowbuf.at[0])
    other_reps(lambda r: swap_x(r).wait_send())
    ancestors(lambda t: scatter(own, t).wait_send())
    other_reps(lambda r: swap_up(r).wait_send())
    other_reps(lambda r: swap_total(r).wait_send())

    @pl.when(own < chunks)
    def _():
        all_of(parts.at[pl.ds(0, chunks - 1)], r_send).wait()
        all_of(gathered.at[pl.ds(0, slots - 1)], a_send).wait()

    @pl.when(own >= chunks)
    def _():
        all_of(parts, r_send).wait()

    other_reps(lambda r: all_of(result.at[rep], b_send.at[r]).wait())
    all_of(atts, stored.at[0]).wait()
    all_of(qgs, stored.at[1]).wait()


def finish(cuts, a_ref, b_ref, r_ref, att_ref, qg_ref, down_ref, up_ref, a, b, res, down, up, ins, outs, sems):
    step = a_ref.shape[0] // cuts

    def move(i, source, target, sem, part):
        at = pl.ds(part * step, step)
        return pltpu.make_async_copy(source.at[at], target.at[at], sem.at[i, part])

    load = pltpu.make_async_copy(r_ref, res, sems.at[0])
    load.start()
    pieces = [(0, a_ref, a, att_ref), (1, b_ref, b, qg_ref)]
    for part in range(cuts):
        for i, source, buf, _ in pieces:
            move(i, source, buf, ins, part).start()
    load.wait()
    reps, chunks, rank, chunk = res.shape
    half = down.shape[1] // reps
    up_half = up.shape[1] // reps
    for r in range(reps):
        for j in range(chunks):
            lo, hi = j * chunk, (j + 1) * chunk
            if lo < half:
                end = min(hi, half)
                down[:, r * half + lo:r * half + end] = res[r, j, :, :end - lo].astype(F32)
            if hi > half and lo < half + up_half:
                first, last = max(lo, half), min(hi, half + up_half)
                base = r * up_half - half
                up[:, base + first:base + last] = res[r, j, :, first - lo:last - lo].astype(F32)
    stores = [
        pltpu.make_async_copy(down, down_ref, sems.at[1]),
        pltpu.make_async_copy(up, up_ref, sems.at[2]),
    ]
    for c in stores:
        c.start()
    for part in range(cuts):
        for i, source, buf, target in pieces:
            move(i, source, buf, ins, part).wait()
            move(i, buf, target, outs, part).start()
    for part in range(cuts):
        for i, source, buf, target in pieces:
            move(i, buf, target, outs, part).wait()
    for c in stores:
        c.wait()


def on_device(x, q, k, frozen, down, up, g, parents, lengths):
    x, q, k, frozen, g = x[0], q[0], k[0], frozen[0], g[0]
    block, width = x.shape
    slots, reps = lax.axis_size("node"), lax.axis_size("rep")
    rank, up_width = up.shape
    heads = q.shape[1] // HEAD_SIZE
    rows = heads // KEY_HEADS * block
    pairs = pair_count(slots)
    tiles = -(-(width + up_width) // reps // 128)
    per = -(-tiles // slots)
    chunks = -(-tiles // per)
    chunk = per * 128
    factor = (slots * reps * block) ** -0.5
    anywhere = pl.BlockSpec(memory_space=pl.ANY)
    vmem = pl.BlockSpec(memory_space=pltpu.VMEM)
    smem = pl.BlockSpec(memory_space=pltpu.SMEM)
    dma = pltpu.SemaphoreType.DMA
    v = pltpu.VMEM
    share = KEY_HEADS // reps
    attended, query_grad, result = pl.pallas_call(
        functools.partial(kernel, slots, reps, factor),
        in_specs=[smem, smem, anywhere, anywhere, anywhere, anywhere, anywhere, vmem, anywhere],
        out_specs=[anywhere, anywhere, vmem],
        out_shape=[
            jax.ShapeDtypeStruct(q.shape, BF16),
            jax.ShapeDtypeStruct(q.shape, BF16),
            jax.ShapeDtypeStruct((reps, chunks, rank, chunk), BF16),
        ],
        scratch_shapes=[
            v(x.shape, BF16), v((reps, block, width // reps), BF16), v((rank, width), BF16),
            v((heads, block, HEAD_SIZE), BF16), v((heads, block, HEAD_SIZE), BF16),
            v(frozen.shape, BF16),
            v((slots, KEY_HEADS, block, HEAD_SIZE), BF16),
            v((slots, KEY_HEADS, block, HEAD_SIZE), BF16),
            v((slots, 1, rank, block), BF16),
            v((KEY_HEADS, pairs, 2 * block, rows), F32),
            v((KEY_HEADS, pairs, 2 * block, rows), BF16),
            v((KEY_HEADS, pairs, 8, rows), F32), v((KEY_HEADS, pairs, 8, rows), F32),
            v((HEAD_SIZE, rows), F32), v((KEY_HEADS, rank, rows), F32),
            v((KEY_HEADS, HEAD_SIZE, rows), BF16),
            v((KEY_HEADS, pairs, 2 * block, HEAD_SIZE), BF16),
            v((2 * block, 2 * rank), F32), v((KEY_HEADS, 8, rows), F32),
            v((heads, block, HEAD_SIZE), BF16), v((heads, block, HEAD_SIZE), BF16),
            v((slots, rank, block), BF16), v((2, rank, block), F32), v((slots, rank, block), BF16),
            v((reps, rank, block), BF16),
            v((KEY_HEADS, rank, HEAD_SIZE), F32), v((reps, share, rank, HEAD_SIZE), F32),
            v((chunks, rank, chunk), BF16), v((slots, rank, chunk), BF16),
            dma((7,)), dma((2,)),
            dma((slots, KEY_HEADS)), dma((slots,)), dma((slots, KEY_HEADS)),
            dma((slots // 2,)), dma((slots // 2,)), dma((slots // 2,)), dma((slots // 2,)),
            dma((reps,)), dma((reps,)), dma((reps,)), dma((reps,)), dma((reps,)), dma((reps,)),
            dma((slots,)), dma((slots,)), dma, dma, dma((slots,)), dma, dma((reps,)), dma((reps,)),
        ],
        compiler_params=pltpu.CompilerParams(
            collective_id=0, has_side_effects=True, vmem_limit_bytes=60 * 1024 * 1024
        ),
        name="tree_attention",
    )(parents, lengths, x, q, k, frozen, down.T, up, g)
    cuts = 2
    attended, query_grad, down_sum, up_sum = pl.pallas_call(
        functools.partial(finish, cuts),
        in_specs=[anywhere, anywhere, anywhere],
        out_specs=[anywhere, anywhere, anywhere, anywhere],
        out_shape=[
            jax.ShapeDtypeStruct(q.shape, BF16),
            jax.ShapeDtypeStruct(q.shape, BF16),
            jax.ShapeDtypeStruct((rank, width), F32),
            jax.ShapeDtypeStruct((rank, up_width), F32),
        ],
        scratch_shapes=[
            v(q.shape, BF16), v(q.shape, BF16), v(result.shape, BF16),
            v((rank, width), F32), v((rank, up_width), F32),
            dma((2, cuts)), dma((2, cuts)), dma((3,)),
        ],
        compiler_params=pltpu.CompilerParams(vmem_limit_bytes=60 * 1024 * 1024),
        name="finish",
    )(attended, query_grad, result)
    return attended[None], query_grad[None], down_sum.T, up_sum


def solution(mesh):
    rows = P(("groups", "rep"), "node", None)
    table = P(("groups", "rep"), None)
    return jax.shard_map(
        on_device,
        mesh=mesh,
        in_specs=(rows, rows, rows, rows, P(), P(), rows, table, table),
        out_specs=(rows, rows, P("groups", None), P("groups", None)),
        check_vma=False,
    )
```

```python
import functools
import math

import jax
import jax.numpy as jnp
from jax import lax
from jax.experimental import pallas as pl
from jax.experimental.pallas import tpu as pltpu
from jax.sharding import PartitionSpec as P

KEY_HEADS = 4
HEAD_SIZE = 128
PROMPT = 2
SPAN = 5
STEPS = 1 + PROMPT + SPAN
NEGATIVE = -1e30
F32 = jnp.float32
BF16 = jnp.bfloat16
NT = (((1,), (1,)), ((), ()))
NN = (((1,), (0,)), ((), ()))
TN = (((0,), (0,)), ((), ()))
MESH_ID = pl.DeviceIdType.MESH


def dot(a, b, dims):
    return lax.dot_general(a, b, dims, preferred_element_type=F32)


def reaches(slot, below):
    return (below > slot) & ((slot < PROMPT) | (below - slot <= SPAN))


def first_pair(own):
    return jnp.maximum((own + 2 * SPAN - SPAN) // 2 - SPAN, 1)


def pair_count(slots):
    most = 1
    for own in range(slots):
        most = max(most, own // 2 - max((own - SPAN) // 2, 1) + 2)
    return most


def peer(node, rep=None):
    target = {"node": node}
    if rep is not None:
        target["rep"] = rep
    return target


def kernel(
    slots, reps, factor,
    parents, lengths, x_ref, q_ref, k_ref, frozen_ref, down_ref, up_ref, g_ref,
    att_ref, qg_ref, result,
    xs, xcat, downs, qs, gs, fs, kbuf, vbuf, lowbuf, score, weight, tops, facs, acc, gup, gtr,
    vgrad, both, invs, atts, qgs, proj, mine, landed, tbuf, upk, upland, parts, gathered,
    load_sem, stored, k_recv, l_recv, v_recv, col_send, fwd_send, on_send, turn_send, l_col, l_fwd, l_on,
    x_recv, x_send, t_recv, t_send, u_recv, u_send, p_recv, p_send,
    r_recv, r_send, a_recv, a_send, b_recv, b_send,
):
    own, rep = lax.axis_index("node"), lax.axis_index("rep")
    heads = qs.shape[0]
    per = heads // KEY_HEADS
    block = qs.shape[1]
    rows = per * block
    width = xs.shape[1]
    half = width // reps
    scale = HEAD_SIZE ** -0.5
    pair = own // 2
    partner = own + 1 - 2 * lax.rem(own, 2)
    pairs = pair - first_pair(own) + 2

    barrier = pltpu.get_barrier_semaphore()
    for step in range(reps):
        other = lax.rem(rep + step, reps)

        def signal(t, carry):
            pl.semaphore_signal(
                barrier, inc=1, device_id=peer(lax.rem(own + t, slots), other),
                device_id_type=MESH_ID,
            )
            return carry

        lax.fori_loop(0 if step else 1, slots, signal, 0)

    def remote(src, dst, send, recv, node, r=None):
        return pltpu.make_async_remote_copy(
            src_ref=src, dst_ref=dst, send_sem=send, recv_sem=recv,
            device_id=peer(node, r), device_id_type=MESH_ID,
        )

    loads = [
        pltpu.make_async_copy(down_ref, downs, load_sem.at[1]),
        pltpu.make_async_copy(x_ref, xs, load_sem.at[2]),
        pltpu.make_async_copy(frozen_ref, fs, load_sem.at[3]),
        pltpu.make_async_copy(
            x_ref.at[:, pl.ds(pl.multiple_of(rep * half, 128), half)], xcat.at[rep], load_sem.at[0]
        ),
    ]
    def key_load(kk):
        return pltpu.make_async_copy(
            k_ref.at[:, pl.ds(pl.multiple_of(kk * HEAD_SIZE, HEAD_SIZE), HEAD_SIZE)],
            kbuf.at[own, kk], load_sem.at[4],
        )

    for kk in range(KEY_HEADS):
        key_load(kk).start()
    for c in loads:
        c.start()

    def head_copy(source, target, sem, i):
        return pltpu.make_async_copy(
            source.at[:, pl.ds(pl.multiple_of(i * HEAD_SIZE, HEAD_SIZE), HEAD_SIZE)],
            target.at[i], sem,
        )

    def head_store(source, target, sem, i):
        return pltpu.make_async_copy(
            source.at[i],
            target.at[:, pl.ds(pl.multiple_of(i * HEAD_SIZE, HEAD_SIZE), HEAD_SIZE)],
            sem,
        )

    def all_of(buf, sem):
        return pltpu.make_async_copy(buf, buf, sem)

    def each(low, high, action):
        def body(i, carry):
            action(i)
            return carry

        lax.fori_loop(low, high, body, 0)

    each(0, heads, lambda i: head_copy(q_ref, qs, load_sem.at[5], i).start())
    each(0, heads, lambda i: head_copy(g_ref, gs, load_sem.at[6], i).start())

    chain = []
    current = own
    for _ in range(1, STEPS):
        parent = parents[0, jnp.maximum(current, 0)]
        current = jnp.where(current >= 0, parent, -1)
        chain.append(current)
    own_length = lengths[0, own]

    def limit(slot):
        found = slot == own
        for ancestor in chain:
            found = found | (slot == ancestor)
        return jnp.where(found, lengths[0, slot], 0)

    def unsent(slot):
        same = lax.rem(slot + own, 2) == 0
        lands = same & reaches(slot, 2 * pair) | reaches(slot, own)
        return jnp.logical_not(lands | (slot == own))

    def clear_slot(slot):
        @pl.when(unsent(slot))
        def _():
            kbuf[slot] = jnp.zeros(kbuf.shape[1:], BF16)
            vbuf[slot] = jnp.zeros(vbuf.shape[1:], BF16)
            lowbuf[slot] = jnp.zeros(lowbuf.shape[1:], BF16)

    each(0, slots, clear_slot)

    all_of(kbuf.at[own], load_sem.at[4]).wait()
    pl.semaphore_wait(barrier, slots * reps - 1)

    class Stream:
        def __init__(self, buf, col, fwd, on, recv, turns=False):
            self.buf, self.col, self.fwd, self.on, self.recv = buf, col, fwd, on, recv
            self.turns = turns

        def move(self, slot, kk, send, node):
            block = self.buf.at[slot, kk]
            return remote(block, block, send, self.recv(slot, kk), node)

        def arrived(self, slot, kk):
            self.move(slot, kk, self.fwd.at[0], partner).wait_recv()

        def targets(self, across, column):
            @pl.when(reaches(own, partner))
            def _():
                across()

            for t in (2, 1):
                @pl.when((own + 2 * t < slots) & reaches(own, 2 * (pair + t)))
                def _():
                    column(t)

        def send(self, kk):
            self.targets(
                lambda: self.move(own, kk, self.fwd.at[0], partner).start(),
                lambda t: self.move(own, kk, self.col.at[t], own + 2 * t).start(),
            )

        def passing(self, receive, onward, across):
            def body(t):
                slot = own - 2 * t

                @pl.when(reaches(slot, 2 * pair))
                def _():
                    receive(slot)

                    @pl.when((t >= 2) & (own + 2 < slots) & reaches(slot, 2 * pair + 2))
                    def _():
                        onward(slot, t)

                    crosses = reaches(slot, partner)
                    if self.turns:
                        crosses = crosses & ((t > 1) | (own > partner))

                    @pl.when(crosses)
                    def _():
                        across(slot, t)

            each(1, pair + 1, body)

        def turning(self, action):
            @pl.when((own > partner) & (own + 2 < slots) & reaches(partner, own + 2))
            def _():
                action()

        def forward(self, kk):
            if self.turns:
                @pl.when(own > partner)
                def _():
                    self.arrived(partner, kk)

                self.turning(lambda: self.move(partner, kk, turn_send, own + 2).start())
            self.passing(
                lambda slot: self.arrived(slot, kk),
                lambda slot, t: self.move(slot, kk, self.on.at[t], own + 2).start(),
                lambda slot, t: self.move(slot, kk, self.fwd.at[t], partner).start(),
            )

        def from_partner(self, t, kk):
            slot = partner - 2 * t

            @pl.when(reaches(slot, own) & ((t > 0) | (not self.turns)))
            def _():
                self.arrived(slot, kk)

    keys = Stream(kbuf, col_send, fwd_send, on_send, lambda slot, kk: k_recv.at[slot, kk])
    values = Stream(
        vbuf, col_send, fwd_send, on_send, lambda slot, kk: v_recv.at[slot, kk], turns=True
    )
    lows = Stream(lowbuf, l_col, l_fwd, l_on, lambda slot, kk: l_recv.at[slot])
    each(0, KEY_HEADS, keys.send)

    def swap_x(r):
        return remote(
            x_ref.at[:, pl.ds(pl.multiple_of(r * half, 128), half)], xcat.at[rep],
            x_send.at[r], x_recv.at[rep], own, r,
        )

    def other_reps(action):
        for step in range(1, reps):
            action(lax.rem(rep + step, reps))

    other_reps(lambda r: swap_x(r).start())

    loads[0].wait()
    loads[1].wait()
    low = dot(downs[...], xs[...], NT).astype(BF16)
    lowbuf[own, 0] = low
    loads[2].wait()
    own_values = (fs[...].astype(F32) + dot(low, up_ref[...], TN)).astype(BF16)
    for kk in range(KEY_HEADS):
        vbuf[own, kk] = own_values[:, kk * HEAD_SIZE:(kk + 1) * HEAD_SIZE]
    lows.send(0)

    all_of(qs, load_sem.at[5]).wait()
    all_of(gs, load_sem.at[6]).wait()

    def stacked(buf, kk):
        return buf[pl.ds(kk * per, per)].reshape(rows, HEAD_SIZE)

    def pair_at(step):
        return jnp.where(step == pairs - 1, 0, pair - step)

    def two(buf, index, kk):
        return buf[pl.ds(2 * index, 2), kk].reshape(2 * block, HEAD_SIZE)

    for kk in range(KEY_HEADS):
        lanes = slice(kk * HEAD_SIZE, (kk + 1) * HEAD_SIZE)
        gup[kk] = dot(up_ref[:, lanes], stacked(gs, kk), NT)
        for i in range(per):
            at = slice(i * block, (i + 1) * block)
            gtr[kk, :, at] = gs[kk * per + i].astype(F32).T.astype(BF16)

    tune = scale * math.log2(math.e)
    rank = proj.shape[1]
    eights = 2 * block // 8

    def times(a, row):
        return (a.reshape(-1, 8, rows) * row[None]).reshape(a.shape)

    def eight(row):
        return jnp.broadcast_to(row, (8, rows))

    def scores(kk, step, mask, first):
        s = dot(two(kbuf, pair_at(step), kk), stacked(qs, kk), NT)
        s = jnp.where(mask, s, NEGATIVE).reshape(eights, 8, rows)
        most = eight(jnp.max(jnp.max(s, axis=0), axis=0, keepdims=True))
        if not first:
            most = jnp.maximum(most, tops[kk, step - 1])
        e = jnp.exp2((s - most[None]) * tune)
        score[kk, step] = e.reshape(2 * block, rows)
        weight[kk, step] = e.reshape(2 * block, rows).astype(BF16)
        tops[kk, step] = most
        facs[kk, step] = eight(jnp.sum(jnp.sum(e, axis=0), axis=0, keepdims=True))

    def seen(index):
        return limit(2 * index), limit(2 * index + 1)

    def own_pair(kk):
        keys.from_partner(0, kk)
        key = lax.broadcasted_iota(jnp.int32, (2 * block, block), 0)
        place = lax.rem(key, block)
        query = lax.broadcasted_iota(jnp.int32, (2 * block, block), 1)
        even, odd = seen(pair)
        here = jnp.where(key < block, 2 * pair, 2 * pair + 1) == own
        mask = (place < jnp.where(key < block, even, odd)) & (
            jnp.logical_not(here) | (place <= query)
        )
        scores(kk, 0, jnp.concatenate([mask] * per, axis=1), True)

    def other_pairs(kk):
        def body(t):
            keys.from_partner(t, kk)
            index = pair - t

            @pl.when((index == 0) | (index >= first_pair(own)))
            def _():
                even, odd = seen(index)
                key = lax.broadcasted_iota(jnp.int32, (2 * block, rows), 0)
                mask = lax.rem(key, block) < jnp.where(key < block, even, odd)
                scores(kk, jnp.where(index == 0, pairs - 1, t), mask, False)

        each(1, pair + 1, body)

    keys.forward(0)

    def arrive(kk):
        @pl.when(kk + 1 < KEY_HEADS)
        def _():
            keys.forward(kk + 1)

        @pl.when(kk == KEY_HEADS - 1)
        def _():
            lows.forward(0)

        own_pair(kk)

        @pl.when(kk == 0)
        def _():
            each(0, KEY_HEADS, values.send)

        other_pairs(kk)

    each(0, KEY_HEADS, arrive)
    values.forward(0)
    live = (
        lax.rem(lax.broadcasted_iota(jnp.int32, (8, rows), 1), block) < own_length
    ).astype(F32)

    def weigh(kk):
        most = tops[kk, pairs - 1]

        def add(step, total):
            fall = jnp.exp2((tops[kk, step] - most) * tune)
            total = total + facs[kk, step] * fall
            facs[kk, step] = fall
            return total

        invs[kk] = live / lax.fori_loop(0, pairs, add, jnp.zeros((8, rows), F32))

    each(0, KEY_HEADS, weigh)

    def scatter(source, target):
        return remote(
            proj.at[target], landed.at[source], p_send.at[target], p_recv.at[source], target
        )

    def project(i):
        step = pairs - 1 - i
        index = pair_at(step)
        both[...] = jnp.zeros_like(both)

        def head(kk):
            fac = facs[kk, step] * invs[kk]
            facs[kk, step] = fac
            side = times(gup[kk], fac)
            high = side.astype(BF16)
            right = jnp.concatenate(
                [times(gtr[kk].astype(F32), fac).astype(BF16), high,
                 (side - high.astype(F32)).astype(BF16)], axis=0,
            )
            out = dot(weight[kk, step], right, NT)
            vgrad[kk, step] = out[:, :HEAD_SIZE].astype(BF16)
            both[...] += out[:, HEAD_SIZE:]

        each(0, KEY_HEADS, head)
        turned = both[...].T
        turned = turned[:rank] + turned[rank:]
        for parity in range(2):
            slot = 2 * index + parity
            mine[parity] = turned[:, parity * block:(parity + 1) * block]
            proj[slot] = mine[parity].astype(BF16)

            @pl.when(reaches(slot, own))
            def _():
                scatter(own, slot).start()

    each(0, pairs, project)

    def ancestors(action):
        def body(t):
            @pl.when(reaches(t, own))
            def _():
                action(t)

        each(0, slots, body)

    def descendants(action):
        def body(t):
            @pl.when(reaches(own, t))
            def _():
                action(t)

        each(0, slots, body)

    values.forward(1)
    values.forward(2)
    each(0, pair + 1, lambda t: lows.from_partner(t, 0))

    def low_weights(kk):
        upk[kk] = jnp.zeros(upk.shape[1:], F32)

        def one(step):
            index = pair_at(step)
            low = jnp.concatenate([lowbuf[2 * index, 0], lowbuf[2 * index + 1, 0]], axis=1)
            upk[kk] += dot(low, vgrad[kk, step], NN)

        each(0, pairs, one)

    each(0, KEY_HEADS, low_weights)
    values.forward(3)
    share = KEY_HEADS // reps

    def swap_up(r):
        return remote(
            upk.at[pl.ds(r * share, share)], upland.at[rep], u_send.at[r], u_recv.at[rep], own, r
        )

    other_reps(lambda r: swap_up(r).start())

    descendants(lambda t: remote(
        proj.at[t], landed.at[t], p_send.at[t], p_recv.at[t], t
    ).wait_recv())
    total = mine[lax.rem(own, 2)]

    def add_landed(t):
        @pl.when(reaches(own, t))
        def _():
            mine[0] += landed[t].astype(F32)

    mine[0] = total
    each(0, slots, add_landed)
    tbuf[rep] = mine[0].astype(BF16)

    def swap_total(r):
        return remote(tbuf.at[rep], tbuf.at[rep], t_send.at[r], t_recv.at[rep], own, r)

    other_reps(lambda r: swap_total(r).start())
    loads[3].wait()

    def arrivals(r):
        remote(
            x_ref.at[:, pl.ds(0, half)], xcat.at[r], x_send.at[r], x_recv.at[r], own, r
        ).wait_recv()
        remote(tbuf.at[r], tbuf.at[r], t_send.at[r], t_recv.at[r], own, r).wait_recv()
        remote(
            upk.at[pl.ds(0, share)], upland.at[r], u_send.at[r], u_recv.at[r], own, r
        ).wait_recv()

    other_reps(arrivals)

    projected = jnp.concatenate([tbuf[r] for r in range(reps)], axis=1)
    ups = upk[pl.ds(rep * share, share)]
    for step in range(1, reps):
        ups = ups + upland[lax.rem(rep + step, reps)]
    upland[rep] = ups
    chunks, _, chunk = parts.shape
    for j in range(chunks):
        lo, hi = j * chunk, (j + 1) * chunk
        pieces = []
        if lo < half:
            end = min(hi, half)
            pieces.append(dot(projected, xcat[:, :, lo:end].reshape(reps * block, end - lo), NN))
        for h in range(share):
            if lo <= half + h * HEAD_SIZE < hi:
                pieces.append(upland[rep, h])
        filled = sum(p.shape[1] for p in pieces)
        if filled < chunk:
            pieces.append(jnp.zeros((rank, chunk - filled), F32))
        value = pieces[0] if len(pieces) == 1 else jnp.concatenate(pieces, axis=1)
        parts[j] = value.astype(BF16)

    def reduce_copy(source, node):
        return remote(
            parts.at[node], gathered.at[source], r_send, r_recv, node
        )

    def others(action):
        each(1, slots, lambda t: action(lax.rem(own + t, slots)))

    def owners(action):
        def body(node):
            @pl.when(node < chunks)
            def _():
                action(node)

        others(body)

    owners(lambda node: reduce_copy(own, node).start())

    def outputs(kk):
        each(0, pair + 1, lambda t: values.from_partner(t, kk))
        grad = stacked(gs, kk)
        acc[...] = jnp.zeros_like(acc)

        def attend(step):
            acc[...] += times(
                dot(two(vbuf, pair_at(step), kk), weight[kk, step], TN), facs[kk, step]
            )

        each(0, pairs, attend)
        out = acc[...]
        dots = (gtr[kk].astype(F32) * out).reshape(HEAD_SIZE // 8, 8, rows)
        dots = eight(jnp.sum(jnp.sum(dots, axis=0), axis=0, keepdims=True))
        for i in range(per):
            atts[kk * per + i] = acc[:, i * block:(i + 1) * block].T.astype(BF16)
        acc[...] = jnp.zeros_like(acc)

        def back(step):
            index = pair_at(step)
            pressure = dot(two(vbuf, index, kk), grad, NT).reshape(eights, 8, rows)
            slopes = (pressure - dots[None]) * (facs[kk, step] * scale)[None]
            slopes = score[kk, step] * slopes.reshape(2 * block, rows)
            acc[...] += dot(two(kbuf, index, kk), slopes.astype(BF16), TN)

        each(0, pairs, back)
        for i in range(per):
            qgs[kk * per + i] = acc[:, i * block:(i + 1) * block].T.astype(BF16)

        def store(i):
            head_store(atts, att_ref, stored.at[0], i).start()
            head_store(qgs, qg_ref, stored.at[1], i).start()

        each(kk * per, (kk + 1) * per, store)

    outputs_early = 2
    each(0, outputs_early, outputs)

    def gather_copy(node, owner):
        return remote(
            result.at[rep, owner], result.at[rep, owner], a_send, a_recv.at[owner], node
        )

    def swap_result(r, owner):
        return remote(
            result.at[rep, owner], result.at[rep, owner], b_send.at[r], b_recv.at[rep], own, r
        )

    @pl.when(own < chunks)
    def _():
        gathered[own] = parts[own]
        all_of(gathered.at[pl.ds(0, slots - 1)], r_recv).wait()
        acc = lax.fori_loop(
            0, slots, lambda t, a: a + gathered[t].astype(F32), jnp.zeros((rank, chunk), F32)
        )
        result[rep, own] = (acc * factor).astype(BF16)
        others(lambda node: gather_copy(node, own).start())
        other_reps(lambda r: swap_result(r, own).start())

    each(outputs_early, KEY_HEADS, outputs)

    def pass_on(owner):
        remote(
            result.at[rep, owner], result.at[rep, owner], a_send, a_recv.at[owner], owner
        ).wait_recv()
        other_reps(lambda r: swap_result(r, owner).start())

    owners(pass_on)

    other_reps(lambda r: all_of(result.at[r], b_recv.at[r]).wait())
    heads_of_two = kbuf.at[pl.ds(0, 2)]

    def crossed(t):
        both_cross = (t > 1) | (own > partner)

        @pl.when(both_cross)
        def _():
            all_of(heads_of_two, fwd_send.at[t]).wait()

        @pl.when(jnp.logical_not(both_cross))
        def _():
            all_of(kbuf.at[0], fwd_send.at[t]).wait()

    keys.targets(
        lambda: all_of(heads_of_two, fwd_send.at[0]).wait(),
        lambda t: all_of(heads_of_two, col_send.at[t]).wait(),
    )
    keys.passing(
        lambda slot: None,
        lambda slot, t: all_of(heads_of_two, on_send.at[t]).wait(),
        lambda slot, t: crossed(t),
    )
    values.turning(lambda: all_of(kbuf.at[0], turn_send).wait())
    lows.targets(
        lambda: all_of(lowbuf.at[0], l_fwd.at[0]).wait(),
        lambda t: all_of(lowbuf.at[0], l_col.at[t]).wait(),
    )
    lows.passing(
        lambda slot: None,
        lambda slot, t: all_of(lowbuf.at[0], l_on.at[t]).wait(),
        lambda slot, t: all_of(lowbuf.at[0], l_fwd.at[t]).wait(),
    )
    other_reps(lambda r: swap_x(r).wait_send())
    ancestors(lambda t: scatter(own, t).wait_send())
    other_reps(lambda r: swap_up(r).wait_send())
    other_reps(lambda r: swap_total(r).wait_send())

    @pl.when(own < chunks)
    def _():
        all_of(parts.at[pl.ds(0, chunks - 1)], r_send).wait()
        all_of(gathered.at[pl.ds(0, slots - 1)], a_send).wait()

    @pl.when(own >= chunks)
    def _():
        all_of(parts, r_send).wait()

    other_reps(lambda r: all_of(result.at[rep], b_send.at[r]).wait())
    all_of(atts, stored.at[0]).wait()
    all_of(qgs, stored.at[1]).wait()


def finish(cuts, a_ref, b_ref, r_ref, att_ref, qg_ref, down_ref, up_ref, a, b, res, down, up, ins, outs, sems):
    step = a_ref.shape[0] // cuts

    def move(i, source, target, sem, part):
        at = pl.ds(part * step, step)
        return pltpu.make_async_copy(source.at[at], target.at[at], sem.at[i, part])

    load = pltpu.make_async_copy(r_ref, res, sems.at[0])
    load.start()
    pieces = [(0, a_ref, a, att_ref), (1, b_ref, b, qg_ref)]
    for part in range(cuts):
        for i, source, buf, _ in pieces:
            move(i, source, buf, ins, part).start()
    load.wait()
    reps, chunks, rank, chunk = res.shape
    half = down.shape[1] // reps
    up_half = up.shape[1] // reps
    for r in range(reps):
        for j in range(chunks):
            lo, hi = j * chunk, (j + 1) * chunk
            if lo < half:
                end = min(hi, half)
                down[:, r * half + lo:r * half + end] = res[r, j, :, :end - lo].astype(F32)
            if hi > half and lo < half + up_half:
                first, last = max(lo, half), min(hi, half + up_half)
                base = r * up_half - half
                up[:, base + first:base + last] = res[r, j, :, first - lo:last - lo].astype(F32)
    stores = [
        pltpu.make_async_copy(down, down_ref, sems.at[1]),
        pltpu.make_async_copy(up, up_ref, sems.at[2]),
    ]
    for c in stores:
        c.start()
    for part in range(cuts):
        for i, source, buf, target in pieces:
            move(i, source, buf, ins, part).wait()
            move(i, buf, target, outs, part).start()
    for part in range(cuts):
        for i, source, buf, target in pieces:
            move(i, buf, target, outs, part).wait()
    for c in stores:
        c.wait()


def on_device(x, q, k, frozen, down, up, g, parents, lengths):
    x, q, k, frozen, g = x[0], q[0], k[0], frozen[0], g[0]
    block, width = x.shape
    slots, reps = lax.axis_size("node"), lax.axis_size("rep")
    rank, up_width = up.shape
    heads = q.shape[1] // HEAD_SIZE
    rows = heads // KEY_HEADS * block
    pairs = pair_count(slots)
    tiles = -(-(width + up_width) // reps // 128)
    per = -(-tiles // slots)
    chunks = -(-tiles // per)
    chunk = per * 128
    factor = (slots * reps * block) ** -0.5
    anywhere = pl.BlockSpec(memory_space=pl.ANY)
    vmem = pl.BlockSpec(memory_space=pltpu.VMEM)
    smem = pl.BlockSpec(memory_space=pltpu.SMEM)
    dma = pltpu.SemaphoreType.DMA
    v = pltpu.VMEM
    share = KEY_HEADS // reps
    attended, query_grad, result = pl.pallas_call(
        functools.partial(kernel, slots, reps, factor),
        in_specs=[smem, smem, anywhere, anywhere, anywhere, anywhere, anywhere, vmem, anywhere],
        out_specs=[anywhere, anywhere, vmem],
        out_shape=[
            jax.ShapeDtypeStruct(q.shape, BF16),
            jax.ShapeDtypeStruct(q.shape, BF16),
            jax.ShapeDtypeStruct((reps, chunks, rank, chunk), BF16),
        ],
        scratch_shapes=[
            v(x.shape, BF16), v((reps, block, width // reps), BF16), v((rank, width), BF16),
            v((heads, block, HEAD_SIZE), BF16), v((heads, block, HEAD_SIZE), BF16),
            v(frozen.shape, BF16),
            v((slots, KEY_HEADS, block, HEAD_SIZE), BF16),
            v((slots, KEY_HEADS, block, HEAD_SIZE), BF16),
            v((slots, 1, rank, block), BF16),
            v((KEY_HEADS, pairs, 2 * block, rows), F32),
            v((KEY_HEADS, pairs, 2 * block, rows), BF16),
            v((KEY_HEADS, pairs, 8, rows), F32), v((KEY_HEADS, pairs, 8, rows), F32),
            v((HEAD_SIZE, rows), F32), v((KEY_HEADS, rank, rows), F32),
            v((KEY_HEADS, HEAD_SIZE, rows), BF16),
            v((KEY_HEADS, pairs, 2 * block, HEAD_SIZE), BF16),
            v((2 * block, 2 * rank), F32), v((KEY_HEADS, 8, rows), F32),
            v((heads, block, HEAD_SIZE), BF16), v((heads, block, HEAD_SIZE), BF16),
            v((slots, rank, block), BF16), v((2, rank, block), F32), v((slots, rank, block), BF16),
            v((reps, rank, block), BF16),
            v((KEY_HEADS, rank, HEAD_SIZE), F32), v((reps, share, rank, HEAD_SIZE), F32),
            v((chunks, rank, chunk), BF16), v((slots, rank, chunk), BF16),
            dma((7,)), dma((2,)),
            dma((slots, KEY_HEADS)), dma((slots,)), dma((slots, KEY_HEADS)),
            dma((3,)), dma((slots // 2,)), dma((slots // 2,)), dma,
            dma((3,)), dma((slots // 2,)), dma((slots // 2,)),
            dma((reps,)), dma((reps,)), dma((reps,)), dma((reps,)), dma((reps,)), dma((reps,)),
            dma((slots,)), dma((slots,)), dma, dma, dma((slots,)), dma, dma((reps,)), dma((reps,)),
        ],
        compiler_params=pltpu.CompilerParams(
            collective_id=0, has_side_effects=True, vmem_limit_bytes=60 * 1024 * 1024
        ),
        name="tree_attention",
    )(parents, lengths, x, q, k, frozen, down.T, up, g)
    cuts = 2
    attended, query_grad, down_sum, up_sum = pl.pallas_call(
        functools.partial(finish, cuts),
        in_specs=[anywhere, anywhere, anywhere],
        out_specs=[anywhere, anywhere, anywhere, anywhere],
        out_shape=[
            jax.ShapeDtypeStruct(q.shape, BF16),
            jax.ShapeDtypeStruct(q.shape, BF16),
            jax.ShapeDtypeStruct((rank, width), F32),
            jax.ShapeDtypeStruct((rank, up_width), F32),
        ],
        scratch_shapes=[
            v(q.shape, BF16), v(q.shape, BF16), v(result.shape, BF16),
            v((rank, width), F32), v((rank, up_width), F32),
            dma((2, cuts)), dma((2, cuts)), dma((3,)),
        ],
        compiler_params=pltpu.CompilerParams(vmem_limit_bytes=60 * 1024 * 1024),
        name="finish",
    )(attended, query_grad, result)
    return attended[None], query_grad[None], down_sum.T, up_sum


def solution(mesh):
    rows = P(("groups", "rep"), "node", None)
    table = P(("groups", "rep"), None)
    return jax.shard_map(
        on_device,
        mesh=mesh,
        in_specs=(rows, rows, rows, rows, P(), P(), rows, table, table),
        out_specs=(rows, rows, P("groups", None), P("groups", None)),
        check_vma=False,
    )
```

```python
import functools
import math

import jax
import jax.numpy as jnp
from jax import lax
from jax.experimental import pallas as pl
from jax.experimental.pallas import tpu as pltpu
from jax.sharding import PartitionSpec as P

KEY_HEADS = 4
HEAD_SIZE = 128
PROMPT = 2
SPAN = 5
STEPS = 1 + PROMPT + SPAN
NEGATIVE = -1e30
F32 = jnp.float32
BF16 = jnp.bfloat16
NT = (((1,), (1,)), ((), ()))
NN = (((1,), (0,)), ((), ()))
TN = (((0,), (0,)), ((), ()))
MESH_ID = pl.DeviceIdType.MESH


def dot(a, b, dims):
    return lax.dot_general(a, b, dims, preferred_element_type=F32)


def reaches(slot, below):
    return (below > slot) & ((slot < PROMPT) | (below - slot <= SPAN))


def first_pair(own):
    return jnp.maximum((own + 2 * SPAN - SPAN) // 2 - SPAN, 1)


def pair_count(slots):
    most = 1
    for own in range(slots):
        most = max(most, own // 2 - max((own - SPAN) // 2, 1) + 2)
    return most


def peer(node, rep=None):
    target = {"node": node}
    if rep is not None:
        target["rep"] = rep
    return target


def kernel(
    slots, reps, factor,
    parents, lengths, x_ref, q_ref, k_ref, frozen_ref, down_ref, up_ref, g_ref,
    att_ref, qg_ref, result,
    xs, xcat, downs, qs, gs, fs, kbuf, vbuf, lowbuf, score, weight, tops, facs, acc, gup, gtr,
    vgrad, both, invs, proj, mine, landed, tbuf, upk, upland, parts, gathered,
    load_sem, k_recv, l_recv, v_recv, col_send, fwd_send, on_send, turn_send, l_col, l_fwd, l_on,
    x_recv, x_send, t_recv, t_send, u_recv, u_send, p_recv, p_send,
    r_recv, r_send, a_recv, a_send, b_recv, b_send,
):
    own, rep = lax.axis_index("node"), lax.axis_index("rep")
    heads = qs.shape[0]
    per = heads // KEY_HEADS
    block = qs.shape[1]
    rows = per * block
    width = xs.shape[1]
    half = width // reps
    scale = HEAD_SIZE ** -0.5
    pair = own // 2
    partner = own + 1 - 2 * lax.rem(own, 2)
    pairs = pair - first_pair(own) + 2

    barrier = pltpu.get_barrier_semaphore()
    for step in range(reps):
        other = lax.rem(rep + step, reps)

        def signal(t, carry):
            pl.semaphore_signal(
                barrier, inc=1, device_id=peer(lax.rem(own + t, slots), other),
                device_id_type=MESH_ID,
            )
            return carry

        lax.fori_loop(0 if step else 1, slots, signal, 0)

    def remote(src, dst, send, recv, node, r=None):
        return pltpu.make_async_remote_copy(
            src_ref=src, dst_ref=dst, send_sem=send, recv_sem=recv,
            device_id=peer(node, r), device_id_type=MESH_ID,
        )

    loads = [
        pltpu.make_async_copy(down_ref, downs, load_sem.at[1]),
        pltpu.make_async_copy(x_ref, xs, load_sem.at[2]),
        pltpu.make_async_copy(frozen_ref, fs, load_sem.at[3]),
        pltpu.make_async_copy(
            x_ref.at[:, pl.ds(pl.multiple_of(rep * half, 128), half)], xcat.at[rep], load_sem.at[0]
        ),
    ]
    def key_load(kk):
        return pltpu.make_async_copy(
            k_ref.at[:, pl.ds(pl.multiple_of(kk * HEAD_SIZE, HEAD_SIZE), HEAD_SIZE)],
            kbuf.at[own, kk], load_sem.at[4],
        )

    for kk in range(KEY_HEADS):
        key_load(kk).start()
    for c in loads:
        c.start()

    def head_copy(source, target, sem, i):
        return pltpu.make_async_copy(
            source.at[:, pl.ds(pl.multiple_of(i * HEAD_SIZE, HEAD_SIZE), HEAD_SIZE)],
            target.at[i], sem,
        )

    def all_of(buf, sem):
        return pltpu.make_async_copy(buf, buf, sem)

    def each(low, high, action):
        def body(i, carry):
            action(i)
            return carry

        lax.fori_loop(low, high, body, 0)

    each(0, heads, lambda i: head_copy(q_ref, qs, load_sem.at[5], i).start())
    each(0, heads, lambda i: head_copy(g_ref, gs, load_sem.at[6], i).start())

    chain = []
    current = own
    for _ in range(1, STEPS):
        parent = parents[0, jnp.maximum(current, 0)]
        current = jnp.where(current >= 0, parent, -1)
        chain.append(current)
    own_length = lengths[0, own]

    def limit(slot):
        found = slot == own
        for ancestor in chain:
            found = found | (slot == ancestor)
        return jnp.where(found, lengths[0, slot], 0)

    def unsent(slot):
        same = lax.rem(slot + own, 2) == 0
        lands = same & reaches(slot, 2 * pair) | reaches(slot, own)
        return jnp.logical_not(lands | (slot == own))

    def clear_slot(slot):
        @pl.when(unsent(slot))
        def _():
            kbuf[slot] = jnp.zeros(kbuf.shape[1:], BF16)
            vbuf[slot] = jnp.zeros(vbuf.shape[1:], BF16)
            lowbuf[slot] = jnp.zeros(lowbuf.shape[1:], BF16)

    each(0, slots, clear_slot)

    all_of(kbuf.at[own], load_sem.at[4]).wait()
    pl.semaphore_wait(barrier, slots * reps - 1)

    class Stream:
        def __init__(self, buf, col, fwd, on, recv, turns=False):
            self.buf, self.col, self.fwd, self.on, self.recv = buf, col, fwd, on, recv
            self.turns = turns

        def move(self, slot, kk, send, node):
            block = self.buf.at[slot, kk]
            return remote(block, block, send, self.recv(slot, kk), node)

        def arrived(self, slot, kk):
            self.move(slot, kk, self.fwd.at[0], partner).wait_recv()

        def targets(self, across, column):
            @pl.when(reaches(own, partner))
            def _():
                across()

            for t in (2, 1):
                @pl.when((own + 2 * t < slots) & reaches(own, 2 * (pair + t)))
                def _():
                    column(t)

        def send(self, kk):
            self.targets(
                lambda: self.move(own, kk, self.fwd.at[0], partner).start(),
                lambda t: self.move(own, kk, self.col.at[t], own + 2 * t).start(),
            )

        def passing(self, receive, onward, across):
            def body(t):
                slot = own - 2 * t

                @pl.when(reaches(slot, 2 * pair))
                def _():
                    receive(slot)

                    @pl.when((t >= 2) & (own + 2 < slots) & reaches(slot, 2 * pair + 2))
                    def _():
                        onward(slot, t)

                    crosses = reaches(slot, partner)
                    if self.turns:
                        crosses = crosses & ((t > 1) | (own > partner))

                    @pl.when(crosses)
                    def _():
                        across(slot, t)

            each(1, pair + 1, body)

        def turning(self, action):
            @pl.when((own > partner) & (own + 2 < slots) & reaches(partner, own + 2))
            def _():
                action()

        def forward(self, kk):
            if self.turns:
                @pl.when(own > partner)
                def _():
                    self.arrived(partner, kk)

                self.turning(lambda: self.move(partner, kk, turn_send, own + 2).start())
            self.passing(
                lambda slot: self.arrived(slot, kk),
                lambda slot, t: self.move(slot, kk, self.on.at[t], own + 2).start(),
                lambda slot, t: self.move(slot, kk, self.fwd.at[t], partner).start(),
            )

        def from_partner(self, t, kk):
            slot = partner - 2 * t

            @pl.when(reaches(slot, own) & ((t > 0) | (not self.turns)))
            def _():
                self.arrived(slot, kk)

    keys = Stream(kbuf, col_send, fwd_send, on_send, lambda slot, kk: k_recv.at[slot, kk])
    values = Stream(
        vbuf, col_send, fwd_send, on_send, lambda slot, kk: v_recv.at[slot, kk], turns=True
    )
    lows = Stream(lowbuf, l_col, l_fwd, l_on, lambda slot, kk: l_recv.at[slot])
    each(0, KEY_HEADS, keys.send)

    def swap_x(r):
        return remote(
            x_ref.at[:, pl.ds(pl.multiple_of(r * half, 128), half)], xcat.at[rep],
            x_send.at[r], x_recv.at[rep], own, r,
        )

    def other_reps(action):
        for step in range(1, reps):
            action(lax.rem(rep + step, reps))

    other_reps(lambda r: swap_x(r).start())

    loads[0].wait()
    loads[1].wait()
    low = dot(downs[...], xs[...], NT).astype(BF16)
    lowbuf[own, 0] = low
    loads[2].wait()
    own_values = (fs[...].astype(F32) + dot(low, up_ref[...], TN)).astype(BF16)
    for kk in range(KEY_HEADS):
        vbuf[own, kk] = own_values[:, kk * HEAD_SIZE:(kk + 1) * HEAD_SIZE]
    lows.send(0)

    all_of(qs, load_sem.at[5]).wait()
    all_of(gs, load_sem.at[6]).wait()

    def stacked(buf, kk):
        return buf[pl.ds(kk * per, per)].reshape(rows, HEAD_SIZE)

    def pair_at(step):
        return jnp.where(step == pairs - 1, 0, pair - step)

    def two(buf, index, kk):
        return buf[pl.ds(2 * index, 2), kk].reshape(2 * block, HEAD_SIZE)

    for kk in range(KEY_HEADS):
        lanes = slice(kk * HEAD_SIZE, (kk + 1) * HEAD_SIZE)
        gup[kk] = dot(up_ref[:, lanes], stacked(gs, kk), NT)
        for i in range(per):
            at = slice(i * block, (i + 1) * block)
            gtr[kk, :, at] = gs[kk * per + i].astype(F32).T.astype(BF16)

    tune = scale * math.log2(math.e)
    rank = proj.shape[1]
    eights = 2 * block // 8

    def times(a, row):
        return (a.reshape(-1, 8, rows) * row[None]).reshape(a.shape)

    def eight(row):
        return jnp.broadcast_to(row, (8, rows))

    def scores(kk, step, mask, first):
        s = dot(two(kbuf, pair_at(step), kk), stacked(qs, kk), NT)
        s = jnp.where(mask, s, NEGATIVE).reshape(eights, 8, rows)
        most = eight(jnp.max(jnp.max(s, axis=0), axis=0, keepdims=True))
        if not first:
            most = jnp.maximum(most, tops[kk, step - 1])
        e = jnp.exp2((s - most[None]) * tune)
        score[kk, step] = e.reshape(2 * block, rows)
        weight[kk, step] = e.reshape(2 * block, rows).astype(BF16)
        tops[kk, step] = most
        facs[kk, step] = eight(jnp.sum(jnp.sum(e, axis=0), axis=0, keepdims=True))

    def seen(index):
        return limit(2 * index), limit(2 * index + 1)

    def own_pair(kk):
        keys.from_partner(0, kk)
        key = lax.broadcasted_iota(jnp.int32, (2 * block, block), 0)
        place = lax.rem(key, block)
        query = lax.broadcasted_iota(jnp.int32, (2 * block, block), 1)
        even, odd = seen(pair)
        here = jnp.where(key < block, 2 * pair, 2 * pair + 1) == own
        mask = (place < jnp.where(key < block, even, odd)) & (
            jnp.logical_not(here) | (place <= query)
        )
        scores(kk, 0, jnp.concatenate([mask] * per, axis=1), True)

    def other_pairs(kk):
        def body(t):
            keys.from_partner(t, kk)
            index = pair - t

            @pl.when((index == 0) | (index >= first_pair(own)))
            def _():
                even, odd = seen(index)
                key = lax.broadcasted_iota(jnp.int32, (2 * block, rows), 0)
                mask = lax.rem(key, block) < jnp.where(key < block, even, odd)
                scores(kk, jnp.where(index == 0, pairs - 1, t), mask, False)

        each(1, pair + 1, body)

    keys.forward(0)

    def arrive(kk):
        @pl.when(kk + 1 < KEY_HEADS)
        def _():
            keys.forward(kk + 1)

        @pl.when(kk == KEY_HEADS - 1)
        def _():
            lows.forward(0)

        own_pair(kk)

        @pl.when(kk == 0)
        def _():
            each(0, KEY_HEADS, values.send)

        other_pairs(kk)

    each(0, KEY_HEADS, arrive)
    values.forward(0)
    live = (
        lax.rem(lax.broadcasted_iota(jnp.int32, (8, rows), 1), block) < own_length
    ).astype(F32)

    def weigh(kk):
        most = tops[kk, pairs - 1]

        def add(step, total):
            fall = jnp.exp2((tops[kk, step] - most) * tune)
            total = total + facs[kk, step] * fall
            facs[kk, step] = fall
            return total

        invs[kk] = live / lax.fori_loop(0, pairs, add, jnp.zeros((8, rows), F32))

    each(0, KEY_HEADS, weigh)

    def scatter(source, target):
        return remote(
            proj.at[target], landed.at[source], p_send.at[target], p_recv.at[source], target
        )

    def project(i):
        step = pairs - 1 - i
        index = pair_at(step)
        both[...] = jnp.zeros_like(both)

        def head(kk):
            fac = facs[kk, step] * invs[kk]
            facs[kk, step] = fac
            side = times(gup[kk], fac)
            high = side.astype(BF16)
            right = jnp.concatenate(
                [times(gtr[kk].astype(F32), fac).astype(BF16), high,
                 (side - high.astype(F32)).astype(BF16)], axis=0,
            )
            out = dot(weight[kk, step], right, NT)
            vgrad[kk, step] = out[:, :HEAD_SIZE].astype(BF16)
            both[...] += out[:, HEAD_SIZE:]

        each(0, KEY_HEADS, head)
        turned = both[...].T
        turned = turned[:rank] + turned[rank:]
        for parity in range(2):
            slot = 2 * index + parity
            mine[parity] = turned[:, parity * block:(parity + 1) * block]
            proj[slot] = mine[parity].astype(BF16)

            @pl.when(reaches(slot, own))
            def _():
                scatter(own, slot).start()

    each(0, pairs, project)

    def ancestors(action):
        def body(t):
            @pl.when(reaches(t, own))
            def _():
                action(t)

        each(0, slots, body)

    def descendants(action):
        def body(t):
            @pl.when(reaches(own, t))
            def _():
                action(t)

        each(0, slots, body)

    values.forward(1)
    values.forward(2)
    each(0, pair + 1, lambda t: lows.from_partner(t, 0))

    def low_weights(kk):
        upk[kk] = jnp.zeros(upk.shape[1:], F32)

        def one(step):
            index = pair_at(step)
            low = jnp.concatenate([lowbuf[2 * index, 0], lowbuf[2 * index + 1, 0]], axis=1)
            upk[kk] += dot(low, vgrad[kk, step], NN)

        each(0, pairs, one)

    each(0, KEY_HEADS, low_weights)
    values.forward(3)
    share = KEY_HEADS // reps

    def swap_up(r):
        return remote(
            upk.at[pl.ds(r * share, share)], upland.at[rep], u_send.at[r], u_recv.at[rep], own, r
        )

    other_reps(lambda r: swap_up(r).start())

    descendants(lambda t: remote(
        proj.at[t], landed.at[t], p_send.at[t], p_recv.at[t], t
    ).wait_recv())
    total = mine[lax.rem(own, 2)]

    def add_landed(t):
        @pl.when(reaches(own, t))
        def _():
            mine[0] += landed[t].astype(F32)

    mine[0] = total
    each(0, slots, add_landed)
    tbuf[rep] = mine[0].astype(BF16)

    def swap_total(r):
        return remote(tbuf.at[rep], tbuf.at[rep], t_send.at[r], t_recv.at[rep], own, r)

    other_reps(lambda r: swap_total(r).start())
    loads[3].wait()

    def arrivals(r):
        remote(
            x_ref.at[:, pl.ds(0, half)], xcat.at[r], x_send.at[r], x_recv.at[r], own, r
        ).wait_recv()
        remote(tbuf.at[r], tbuf.at[r], t_send.at[r], t_recv.at[r], own, r).wait_recv()
        remote(
            upk.at[pl.ds(0, share)], upland.at[r], u_send.at[r], u_recv.at[r], own, r
        ).wait_recv()

    other_reps(arrivals)

    projected = jnp.concatenate([tbuf[r] for r in range(reps)], axis=1)
    ups = upk[pl.ds(rep * share, share)]
    for step in range(1, reps):
        ups = ups + upland[lax.rem(rep + step, reps)]
    upland[rep] = ups
    chunks, _, chunk = parts.shape
    for j in range(chunks):
        lo, hi = j * chunk, (j + 1) * chunk
        pieces = []
        if lo < half:
            end = min(hi, half)
            pieces.append(dot(projected, xcat[:, :, lo:end].reshape(reps * block, end - lo), NN))
        for h in range(share):
            if lo <= half + h * HEAD_SIZE < hi:
                pieces.append(upland[rep, h])
        filled = sum(p.shape[1] for p in pieces)
        if filled < chunk:
            pieces.append(jnp.zeros((rank, chunk - filled), F32))
        value = pieces[0] if len(pieces) == 1 else jnp.concatenate(pieces, axis=1)
        parts[j] = value.astype(BF16)

    def reduce_copy(source, node):
        return remote(
            parts.at[node], gathered.at[source], r_send, r_recv, node
        )

    def others(action):
        each(1, slots, lambda t: action(lax.rem(own + t, slots)))

    def owners(action):
        def body(node):
            @pl.when(node < chunks)
            def _():
                action(node)

        others(body)

    owners(lambda node: reduce_copy(own, node).start())

    def outputs(kk):
        each(0, pair + 1, lambda t: values.from_partner(t, kk))
        grad = stacked(gs, kk)
        acc[...] = jnp.zeros_like(acc)

        def attend(step):
            acc[...] += times(
                dot(two(vbuf, pair_at(step), kk), weight[kk, step], TN), facs[kk, step]
            )

        each(0, pairs, attend)
        out = acc[...]
        dots = (gtr[kk].astype(F32) * out).reshape(HEAD_SIZE // 8, 8, rows)
        dots = eight(jnp.sum(jnp.sum(dots, axis=0), axis=0, keepdims=True))
        for i in range(per):
            att_ref[:, pl.ds(pl.multiple_of((kk * per + i) * HEAD_SIZE, HEAD_SIZE), HEAD_SIZE)] = (
                acc[:, i * block:(i + 1) * block].T.astype(BF16)
            )
        acc[...] = jnp.zeros_like(acc)

        def back(step):
            index = pair_at(step)
            pressure = dot(two(vbuf, index, kk), grad, NT).reshape(eights, 8, rows)
            slopes = (pressure - dots[None]) * (facs[kk, step] * scale)[None]
            slopes = score[kk, step] * slopes.reshape(2 * block, rows)
            acc[...] += dot(two(kbuf, index, kk), slopes.astype(BF16), TN)

        each(0, pairs, back)
        for i in range(per):
            qg_ref[:, pl.ds(pl.multiple_of((kk * per + i) * HEAD_SIZE, HEAD_SIZE), HEAD_SIZE)] = (
                acc[:, i * block:(i + 1) * block].T.astype(BF16)
            )

    outputs_early = 2
    each(0, outputs_early, outputs)

    def gather_copy(node, owner):
        return remote(
            result.at[rep, owner], result.at[rep, owner], a_send, a_recv.at[owner], node
        )

    def swap_result(r, owner):
        return remote(
            result.at[rep, owner], result.at[rep, owner], b_send.at[r], b_recv.at[rep], own, r
        )

    @pl.when(own < chunks)
    def _():
        gathered[own] = parts[own]
        all_of(gathered.at[pl.ds(0, slots - 1)], r_recv).wait()
        acc = lax.fori_loop(
            0, slots, lambda t, a: a + gathered[t].astype(F32), jnp.zeros((rank, chunk), F32)
        )
        result[rep, own] = (acc * factor).astype(BF16)
        others(lambda node: gather_copy(node, own).start())
        other_reps(lambda r: swap_result(r, own).start())

    each(outputs_early, KEY_HEADS, outputs)

    def pass_on(owner):
        remote(
            result.at[rep, owner], result.at[rep, owner], a_send, a_recv.at[owner], owner
        ).wait_recv()
        other_reps(lambda r: swap_result(r, owner).start())

    owners(pass_on)

    other_reps(lambda r: all_of(result.at[r], b_recv.at[r]).wait())
    heads_of_two = kbuf.at[pl.ds(0, 2)]

    def crossed(t):
        both_cross = (t > 1) | (own > partner)

        @pl.when(both_cross)
        def _():
            all_of(heads_of_two, fwd_send.at[t]).wait()

        @pl.when(jnp.logical_not(both_cross))
        def _():
            all_of(kbuf.at[0], fwd_send.at[t]).wait()

    keys.targets(
        lambda: all_of(heads_of_two, fwd_send.at[0]).wait(),
        lambda t: all_of(heads_of_two, col_send.at[t]).wait(),
    )
    keys.passing(
        lambda slot: None,
        lambda slot, t: all_of(heads_of_two, on_send.at[t]).wait(),
        lambda slot, t: crossed(t),
    )
    values.turning(lambda: all_of(kbuf.at[0], turn_send).wait())
    lows.targets(
        lambda: all_of(lowbuf.at[0], l_fwd.at[0]).wait(),
        lambda t: all_of(lowbuf.at[0], l_col.at[t]).wait(),
    )
    lows.passing(
        lambda slot: None,
        lambda slot, t: all_of(lowbuf.at[0], l_on.at[t]).wait(),
        lambda slot, t: all_of(lowbuf.at[0], l_fwd.at[t]).wait(),
    )
    other_reps(lambda r: swap_x(r).wait_send())
    ancestors(lambda t: scatter(own, t).wait_send())
    other_reps(lambda r: swap_up(r).wait_send())
    other_reps(lambda r: swap_total(r).wait_send())

    @pl.when(own < chunks)
    def _():
        all_of(parts.at[pl.ds(0, chunks - 1)], r_send).wait()
        all_of(gathered.at[pl.ds(0, slots - 1)], a_send).wait()

    @pl.when(own >= chunks)
    def _():
        all_of(parts, r_send).wait()

    other_reps(lambda r: all_of(result.at[rep], b_send.at[r]).wait())


def finish(a_ref, b_ref, res, att_ref, qg_ref, down_ref, up_ref, down, up, sems):
    stores = [
        pltpu.make_async_copy(source, target, sems.at[i])
        for i, (source, target) in enumerate(
            [(a_ref, att_ref), (b_ref, qg_ref), (down, down_ref), (up, up_ref)]
        )
    ]
    for c in stores[:2]:
        c.start()
    reps, chunks, rank, chunk = res.shape
    half = down.shape[1] // reps
    up_half = up.shape[1] // reps
    for r in range(reps):
        for j in range(chunks):
            lo, hi = j * chunk, (j + 1) * chunk
            if lo < half:
                end = min(hi, half)
                down[:, r * half + lo:r * half + end] = res[r, j, :, :end - lo].astype(F32)
            if hi > half and lo < half + up_half:
                first, last = max(lo, half), min(hi, half + up_half)
                base = r * up_half - half
                up[:, base + first:base + last] = res[r, j, :, first - lo:last - lo].astype(F32)
    for c in stores[2:]:
        c.start()
    for c in stores:
        c.wait()


def on_device(x, q, k, frozen, down, up, g, parents, lengths):
    x, q, k, frozen, g = x[0], q[0], k[0], frozen[0], g[0]
    block, width = x.shape
    slots, reps = lax.axis_size("node"), lax.axis_size("rep")
    rank, up_width = up.shape
    heads = q.shape[1] // HEAD_SIZE
    rows = heads // KEY_HEADS * block
    pairs = pair_count(slots)
    tiles = -(-(width + up_width) // reps // 128)
    per = -(-tiles // slots)
    chunks = -(-tiles // per)
    chunk = per * 128
    factor = (slots * reps * block) ** -0.5
    anywhere = pl.BlockSpec(memory_space=pl.ANY)
    vmem = pl.BlockSpec(memory_space=pltpu.VMEM)
    smem = pl.BlockSpec(memory_space=pltpu.SMEM)
    dma = pltpu.SemaphoreType.DMA
    v = pltpu.VMEM
    share = KEY_HEADS // reps
    attended, query_grad, result = pl.pallas_call(
        functools.partial(kernel, slots, reps, factor),
        in_specs=[smem, smem, anywhere, anywhere, anywhere, anywhere, anywhere, vmem, anywhere],
        out_specs=[vmem, vmem, vmem],
        out_shape=[v(q.shape, BF16), v(q.shape, BF16), v((reps, chunks, rank, chunk), BF16)],
        scratch_shapes=[
            v(x.shape, BF16), v((reps, block, width // reps), BF16), v((rank, width), BF16),
            v((heads, block, HEAD_SIZE), BF16), v((heads, block, HEAD_SIZE), BF16),
            v(frozen.shape, BF16),
            v((slots, KEY_HEADS, block, HEAD_SIZE), BF16),
            v((slots, KEY_HEADS, block, HEAD_SIZE), BF16),
            v((slots, 1, rank, block), BF16),
            v((KEY_HEADS, pairs, 2 * block, rows), F32),
            v((KEY_HEADS, pairs, 2 * block, rows), BF16),
            v((KEY_HEADS, pairs, 8, rows), F32), v((KEY_HEADS, pairs, 8, rows), F32),
            v((HEAD_SIZE, rows), F32), v((KEY_HEADS, rank, rows), F32),
            v((KEY_HEADS, HEAD_SIZE, rows), BF16),
            v((KEY_HEADS, pairs, 2 * block, HEAD_SIZE), BF16),
            v((2 * block, 2 * rank), F32), v((KEY_HEADS, 8, rows), F32),
            v((slots, rank, block), BF16), v((2, rank, block), F32), v((slots, rank, block), BF16),
            v((reps, rank, block), BF16),
            v((KEY_HEADS, rank, HEAD_SIZE), F32), v((reps, share, rank, HEAD_SIZE), F32),
            v((chunks, rank, chunk), BF16), v((slots, rank, chunk), BF16),
            dma((7,)),
            dma((slots, KEY_HEADS)), dma((slots,)), dma((slots, KEY_HEADS)),
            dma((3,)), dma((slots // 2,)), dma((slots // 2,)), dma,
            dma((3,)), dma((slots // 2,)), dma((slots // 2,)),
            dma((reps,)), dma((reps,)), dma((reps,)), dma((reps,)), dma((reps,)), dma((reps,)),
            dma((slots,)), dma((slots,)), dma, dma, dma((slots,)), dma, dma((reps,)), dma((reps,)),
        ],
        compiler_params=pltpu.CompilerParams(
            collective_id=0, has_side_effects=True, vmem_limit_bytes=60 * 1024 * 1024
        ),
        name="tree_attention",
    )(parents, lengths, x, q, k, frozen, down.T, up, g)
    attended, query_grad, down_sum, up_sum = pl.pallas_call(
        finish,
        in_specs=[vmem, vmem, vmem],
        out_specs=[anywhere, anywhere, anywhere, anywhere],
        out_shape=[
            jax.ShapeDtypeStruct(q.shape, BF16),
            jax.ShapeDtypeStruct(q.shape, BF16),
            jax.ShapeDtypeStruct((rank, width), F32),
            jax.ShapeDtypeStruct((rank, up_width), F32),
        ],
        scratch_shapes=[
            v((rank, width), F32), v((rank, up_width), F32), dma((4,)),
        ],
        name="finish",
    )(*[pltpu.with_memory_space_constraint(a, pltpu.VMEM) for a in (attended, query_grad, result)])
    return attended[None], query_grad[None], down_sum.T, up_sum


def solution(mesh):
    rows = P(("groups", "rep"), "node", None)
    table = P(("groups", "rep"), None)
    return jax.shard_map(
        on_device,
        mesh=mesh,
        in_specs=(rows, rows, rows, rows, P(), P(), rows, table, table),
        out_specs=(rows, rows, P("groups", None), P("groups", None)),
        check_vma=False,
    )
```

```python
import functools
import math

import jax
import jax.numpy as jnp
from jax import lax
from jax.experimental import pallas as pl
from jax.experimental.pallas import tpu as pltpu
from jax.sharding import PartitionSpec as P

KEY_HEADS = 4
HEAD_SIZE = 128
PROMPT = 2
SPAN = 5
STEPS = 1 + PROMPT + SPAN
NEGATIVE = -1e30
F32 = jnp.float32
BF16 = jnp.bfloat16
NT = (((1,), (1,)), ((), ()))
NN = (((1,), (0,)), ((), ()))
TN = (((0,), (0,)), ((), ()))
MESH_ID = pl.DeviceIdType.MESH


def dot(a, b, dims):
    return lax.dot_general(a, b, dims, preferred_element_type=F32)


def reaches(slot, below):
    return (below > slot) & ((slot < PROMPT) | (below - slot <= SPAN))


def first_pair(own):
    return jnp.maximum((own + 2 * SPAN - SPAN) // 2 - SPAN, 1)


def pair_count(slots):
    most = 1
    for own in range(slots):
        most = max(most, own // 2 - max((own - SPAN) // 2, 1) + 2)
    return most


def peer(node, rep=None):
    target = {"node": node}
    if rep is not None:
        target["rep"] = rep
    return target


def kernel(
    slots, reps, factor,
    parents, lengths, x_ref, q_ref, k_ref, frozen_ref, down_ref, up_ref, g_ref,
    att_ref, qg_ref, result,
    xs, xcat, downs, qs, gs, fs, kbuf, vbuf, lowbuf, score, weight, tops, facs, acc, gup, gtr,
    lowsum, invs, proj, mine, landed, tbuf, upk, upland, parts, gathered,
    load_sem, k_recv, l_recv, v_recv, col_send, fwd_send, on_send, turn_send, l_col, l_fwd, l_on,
    x_recv, x_send, t_recv, t_send, u_recv, u_send, p_recv, p_send,
    r_recv, r_send, a_recv, a_send, b_recv, b_send,
):
    own, rep = lax.axis_index("node"), lax.axis_index("rep")
    heads = qs.shape[0]
    per = heads // KEY_HEADS
    block = qs.shape[1]
    rows = per * block
    width = xs.shape[1]
    half = width // reps
    scale = HEAD_SIZE ** -0.5
    pair = own // 2
    partner = own + 1 - 2 * lax.rem(own, 2)
    pairs = pair - first_pair(own) + 2

    barrier = pltpu.get_barrier_semaphore()
    for step in range(reps):
        other = lax.rem(rep + step, reps)

        def signal(t, carry):
            pl.semaphore_signal(
                barrier, inc=1, device_id=peer(lax.rem(own + t, slots), other),
                device_id_type=MESH_ID,
            )
            return carry

        lax.fori_loop(0 if step else 1, slots, signal, 0)

    def remote(src, dst, send, recv, node, r=None):
        return pltpu.make_async_remote_copy(
            src_ref=src, dst_ref=dst, send_sem=send, recv_sem=recv,
            device_id=peer(node, r), device_id_type=MESH_ID,
        )

    loads = [
        pltpu.make_async_copy(down_ref, downs, load_sem.at[1]),
        pltpu.make_async_copy(x_ref, xs, load_sem.at[2]),
        pltpu.make_async_copy(frozen_ref, fs, load_sem.at[3]),
        pltpu.make_async_copy(
            x_ref.at[:, pl.ds(pl.multiple_of(rep * half, 128), half)], xcat.at[rep], load_sem.at[0]
        ),
    ]
    def key_load(kk):
        return pltpu.make_async_copy(
            k_ref.at[:, pl.ds(pl.multiple_of(kk * HEAD_SIZE, HEAD_SIZE), HEAD_SIZE)],
            kbuf.at[own, kk], load_sem.at[4],
        )

    for kk in range(KEY_HEADS):
        key_load(kk).start()
    for c in loads:
        c.start()

    def head_copy(source, target, sem, i):
        return pltpu.make_async_copy(
            source.at[:, pl.ds(pl.multiple_of(i * HEAD_SIZE, HEAD_SIZE), HEAD_SIZE)],
            target.at[i], sem,
        )

    def all_of(buf, sem):
        return pltpu.make_async_copy(buf, buf, sem)

    def each(low, high, action):
        def body(i, carry):
            action(i)
            return carry

        lax.fori_loop(low, high, body, 0)

    each(0, heads, lambda i: head_copy(q_ref, qs, load_sem.at[5], i).start())
    each(0, heads, lambda i: head_copy(g_ref, gs, load_sem.at[6], i).start())

    chain = []
    current = own
    for _ in range(1, STEPS):
        parent = parents[0, jnp.maximum(current, 0)]
        current = jnp.where(current >= 0, parent, -1)
        chain.append(current)
    own_length = lengths[0, own]

    def limit(slot):
        found = slot == own
        for ancestor in chain:
            found = found | (slot == ancestor)
        return jnp.where(found, lengths[0, slot], 0)

    def unsent(slot):
        same = lax.rem(slot + own, 2) == 0
        lands = same & reaches(slot, 2 * pair) | reaches(slot, own)
        return jnp.logical_not(lands | (slot == own))

    def clear_slot(slot):
        @pl.when(unsent(slot))
        def _():
            kbuf[slot] = jnp.zeros(kbuf.shape[1:], BF16)
            vbuf[slot] = jnp.zeros(vbuf.shape[1:], BF16)
            lowbuf[slot] = jnp.zeros(lowbuf.shape[1:], BF16)

    each(0, slots, clear_slot)

    all_of(kbuf.at[own], load_sem.at[4]).wait()
    pl.semaphore_wait(barrier, slots * reps - 1)

    class Stream:
        def __init__(self, buf, col, fwd, on, recv, turns=KEY_HEADS):
            self.buf, self.col, self.fwd, self.on, self.recv = buf, col, fwd, on, recv
            self.turns = turns

        def move(self, slot, kk, send, node):
            block = self.buf.at[slot, kk]
            return remote(block, block, send, self.recv(slot, kk), node)

        def arrived(self, slot, kk):
            self.move(slot, kk, self.fwd.at[0], partner).wait_recv()

        def targets(self, across, column):
            @pl.when(reaches(own, partner))
            def _():
                across()

            for t in (2, 1):
                @pl.when((own + 2 * t < slots) & reaches(own, 2 * (pair + t)))
                def _():
                    column(t)

        def send(self, kk):
            self.targets(
                lambda: self.move(own, kk, self.fwd.at[0], partner).start(),
                lambda t: self.move(own, kk, self.col.at[t], own + 2 * t).start(),
            )

        def passing(self, kk, receive, onward, across):
            def body(t):
                slot = own - 2 * t

                @pl.when(reaches(slot, 2 * pair))
                def _():
                    receive(slot)

                    @pl.when((t >= 2) & (own + 2 < slots) & reaches(slot, 2 * pair + 2))
                    def _():
                        onward(slot, t)

                    crosses = reaches(slot, partner) & (
                        (t > 1) | (own > partner) | (kk < self.turns)
                    )

                    @pl.when(crosses)
                    def _():
                        across(slot, t)

            each(1, pair + 1, body)

        def turning(self, action):
            @pl.when((own > partner) & (own + 2 < slots) & reaches(partner, own + 2))
            def _():
                action()

        def forward(self, kk):
            if self.turns < KEY_HEADS:
                @pl.when((own > partner) & (kk >= self.turns))
                def _():
                    self.arrived(partner, kk)
                    self.turning(lambda: self.move(partner, kk, turn_send, own + 2).start())
            self.passing(
                kk,
                lambda slot: self.arrived(slot, kk),
                lambda slot, t: self.move(slot, kk, self.on.at[t], own + 2).start(),
                lambda slot, t: self.move(slot, kk, self.fwd.at[t], partner).start(),
            )

        def from_partner(self, t, kk):
            slot = partner - 2 * t

            @pl.when(reaches(slot, own) & ((t > 0) | (kk < self.turns)))
            def _():
                self.arrived(slot, kk)

    keys = Stream(
        kbuf, col_send, fwd_send, on_send, lambda slot, kk: k_recv.at[slot, kk], turns=4
    )
    values = Stream(
        vbuf, col_send, fwd_send, on_send, lambda slot, kk: v_recv.at[slot, kk], turns=0
    )
    lows = Stream(lowbuf, l_col, l_fwd, l_on, lambda slot, kk: l_recv.at[slot])
    each(0, KEY_HEADS, keys.send)

    def swap_x(r):
        return remote(
            x_ref.at[:, pl.ds(pl.multiple_of(r * half, 128), half)], xcat.at[rep],
            x_send.at[r], x_recv.at[rep], own, r,
        )

    def other_reps(action):
        for step in range(1, reps):
            action(lax.rem(rep + step, reps))

    other_reps(lambda r: swap_x(r).start())

    loads[0].wait()
    loads[1].wait()
    low = dot(downs[...], xs[...], NT).astype(BF16)
    lowbuf[own, 0] = low
    loads[2].wait()
    own_values = (fs[...].astype(F32) + dot(low, up_ref[...], TN)).astype(BF16)
    for kk in range(KEY_HEADS):
        vbuf[own, kk] = own_values[:, kk * HEAD_SIZE:(kk + 1) * HEAD_SIZE]
    lows.send(0)

    all_of(qs, load_sem.at[5]).wait()
    all_of(gs, load_sem.at[6]).wait()

    def stacked(buf, kk):
        return buf[pl.ds(kk * per, per)].reshape(rows, HEAD_SIZE)

    def pair_at(step):
        return jnp.where(step == pairs - 1, 0, pair - step)

    def two(buf, index, kk):
        return buf[pl.ds(2 * index, 2), kk].reshape(2 * block, HEAD_SIZE)

    for kk in range(KEY_HEADS):
        lanes = slice(kk * HEAD_SIZE, (kk + 1) * HEAD_SIZE)
        gup[kk] = dot(up_ref[:, lanes], stacked(gs, kk), NT)
        for i in range(per):
            at = slice(i * block, (i + 1) * block)
            gtr[kk, :, at] = gs[kk * per + i].astype(F32).T.astype(BF16)

    tune = scale * math.log2(math.e)
    rank = proj.shape[1]
    eights = 2 * block // 8

    def times(a, row):
        return (a.reshape(-1, 8, rows) * row[None]).reshape(a.shape)

    def eight(row):
        return jnp.broadcast_to(row, (8, rows))

    def scores(kk, step, mask, first):
        s = dot(two(kbuf, pair_at(step), kk), stacked(qs, kk), NT)
        s = jnp.where(mask, s, NEGATIVE).reshape(eights, 8, rows)
        most = eight(jnp.max(jnp.max(s, axis=0), axis=0, keepdims=True))
        if not first:
            most = jnp.maximum(most, tops[kk, step - 1])
        e = jnp.exp2((s - most[None]) * tune)
        score[kk, step] = e.reshape(2 * block, rows)
        weight[kk, step] = e.reshape(2 * block, rows).astype(BF16)
        tops[kk, step] = most
        facs[kk, step] = eight(jnp.sum(jnp.sum(e, axis=0), axis=0, keepdims=True))

    def seen(index):
        return limit(2 * index), limit(2 * index + 1)

    def own_pair(kk):
        keys.from_partner(0, kk)
        key = lax.broadcasted_iota(jnp.int32, (2 * block, block), 0)
        place = lax.rem(key, block)
        query = lax.broadcasted_iota(jnp.int32, (2 * block, block), 1)
        even, odd = seen(pair)
        here = jnp.where(key < block, 2 * pair, 2 * pair + 1) == own
        mask = (place < jnp.where(key < block, even, odd)) & (
            jnp.logical_not(here) | (place <= query)
        )
        scores(kk, 0, jnp.concatenate([mask] * per, axis=1), True)

    def other_pairs(kk):
        def body(t):
            keys.from_partner(t, kk)
            index = pair - t

            @pl.when((index == 0) | (index >= first_pair(own)))
            def _():
                even, odd = seen(index)
                key = lax.broadcasted_iota(jnp.int32, (2 * block, rows), 0)
                mask = lax.rem(key, block) < jnp.where(key < block, even, odd)
                scores(kk, jnp.where(index == 0, pairs - 1, t), mask, False)

        each(1, pair + 1, body)

    keys.forward(0)

    def arrive(kk):
        @pl.when(kk + 1 < KEY_HEADS)
        def _():
            keys.forward(kk + 1)

        @pl.when(kk == KEY_HEADS - 1)
        def _():
            lows.forward(0)

        own_pair(kk)

        @pl.when(kk == 0)
        def _():
            each(0, KEY_HEADS, values.send)

        other_pairs(kk)

    each(0, KEY_HEADS, arrive)
    values.forward(0)
    live = (
        lax.rem(lax.broadcasted_iota(jnp.int32, (8, rows), 1), block) < own_length
    ).astype(F32)

    def add(step, totals):
        out = []
        for kk in range(KEY_HEADS):
            fall = jnp.exp2((tops[kk, step] - tops[kk, pairs - 1]) * tune)
            out.append(totals[kk] + facs[kk, step] * fall)
            facs[kk, step] = fall
        return tuple(out)

    totals = lax.fori_loop(
        0, pairs, add, tuple(jnp.zeros((8, rows), F32) for _ in range(KEY_HEADS))
    )
    for kk in range(KEY_HEADS):
        invs[kk] = live / totals[kk]

    def scatter(source, target):
        return remote(
            proj.at[target], landed.at[source], p_send.at[target], p_recv.at[source], target
        )

    def project(i):
        step = pairs - 1 - i
        index = pair_at(step)
        turned = jnp.zeros((2 * rank, 2 * block), F32)
        for kk in range(KEY_HEADS):
            fac = facs[kk, step] * invs[kk]
            facs[kk, step] = fac
            side = times(gup[kk], fac)
            high = side.astype(BF16)
            sides = jnp.concatenate([high, (side - high.astype(F32)).astype(BF16)], axis=0)
            turned = turned + dot(sides, weight[kk, step], NT)
        turned = turned[:rank] + turned[rank:]
        for parity in range(2):
            slot = 2 * index + parity
            mine[parity] = turned[:, parity * block:(parity + 1) * block]
            proj[slot] = mine[parity].astype(BF16)

            @pl.when(reaches(slot, own))
            def _():
                scatter(own, slot).start()

    each(0, pairs, project)

    def ancestors(action):
        def body(t):
            @pl.when(reaches(t, own))
            def _():
                action(t)

        each(0, slots, body)

    def descendants(action):
        def body(t):
            @pl.when(reaches(own, t))
            def _():
                action(t)

        each(0, slots, body)

    values.forward(1)
    values.forward(2)
    each(0, pair + 1, lambda t: lows.from_partner(t, 0))

    for kk in range(KEY_HEADS):
        lowsum[kk] = jnp.zeros((rank, rows), F32)

    def low_weights(step):
        index = pair_at(step)
        low = jnp.concatenate([lowbuf[2 * index, 0], lowbuf[2 * index + 1, 0]], axis=1)
        for kk in range(KEY_HEADS):
            lowsum[kk] += times(dot(low, weight[kk, step], NN), facs[kk, step])

    each(0, pairs, low_weights)
    for kk in range(KEY_HEADS):
        total = lowsum[kk]
        high = total.astype(BF16)
        sides = jnp.concatenate([high, (total - high.astype(F32)).astype(BF16)], axis=0)
        out = dot(sides, stacked(gs, kk), NN)
        upk[kk] = out[:rank] + out[rank:]

    values.forward(3)
    share = KEY_HEADS // reps

    def swap_up(r):
        return remote(
            upk.at[pl.ds(r * share, share)], upland.at[rep], u_send.at[r], u_recv.at[rep], own, r
        )

    other_reps(lambda r: swap_up(r).start())

    descendants(lambda t: remote(
        proj.at[t], landed.at[t], p_send.at[t], p_recv.at[t], t
    ).wait_recv())
    total = mine[lax.rem(own, 2)]

    def add_landed(t):
        @pl.when(reaches(own, t))
        def _():
            mine[0] += landed[t].astype(F32)

    mine[0] = total
    each(0, slots, add_landed)
    tbuf[rep] = mine[0].astype(BF16)

    def swap_total(r):
        return remote(tbuf.at[rep], tbuf.at[rep], t_send.at[r], t_recv.at[rep], own, r)

    other_reps(lambda r: swap_total(r).start())
    loads[3].wait()

    def arrivals(r):
        remote(
            x_ref.at[:, pl.ds(0, half)], xcat.at[r], x_send.at[r], x_recv.at[r], own, r
        ).wait_recv()
        remote(tbuf.at[r], tbuf.at[r], t_send.at[r], t_recv.at[r], own, r).wait_recv()
        remote(
            upk.at[pl.ds(0, share)], upland.at[r], u_send.at[r], u_recv.at[r], own, r
        ).wait_recv()

    other_reps(arrivals)

    projected = jnp.concatenate([tbuf[r] for r in range(reps)], axis=1)
    ups = upk[pl.ds(rep * share, share)]
    for step in range(1, reps):
        ups = ups + upland[lax.rem(rep + step, reps)]
    upland[rep] = ups
    chunks, _, chunk = parts.shape
    for j in range(chunks):
        lo, hi = j * chunk, (j + 1) * chunk
        pieces = []
        if lo < half:
            end = min(hi, half)
            pieces.append(dot(projected, xcat[:, :, lo:end].reshape(reps * block, end - lo), NN))
        for h in range(share):
            if lo <= half + h * HEAD_SIZE < hi:
                pieces.append(upland[rep, h])
        filled = sum(p.shape[1] for p in pieces)
        if filled < chunk:
            pieces.append(jnp.zeros((rank, chunk - filled), F32))
        value = pieces[0] if len(pieces) == 1 else jnp.concatenate(pieces, axis=1)
        parts[j] = value.astype(BF16)

    def reduce_copy(source, node):
        return remote(
            parts.at[node], gathered.at[source], r_send, r_recv, node
        )

    def others(action):
        each(1, slots, lambda t: action(lax.rem(own + t, slots)))

    def owners(action):
        def body(node):
            @pl.when(node < chunks)
            def _():
                action(node)

        others(body)

    owners(lambda node: reduce_copy(own, node).start())

    def outputs(kk):
        each(0, pair + 1, lambda t: values.from_partner(t, kk))
        grad = stacked(gs, kk)
        acc[...] = jnp.zeros_like(acc)

        def attend(step):
            acc[...] += times(
                dot(two(vbuf, pair_at(step), kk), weight[kk, step], TN), facs[kk, step]
            )

        each(0, pairs, attend)
        out = acc[...]
        dots = (gtr[kk].astype(F32) * out).reshape(HEAD_SIZE // 8, 8, rows)
        dots = eight(jnp.sum(jnp.sum(dots, axis=0), axis=0, keepdims=True))
        for i in range(per):
            att_ref[:, pl.ds(pl.multiple_of((kk * per + i) * HEAD_SIZE, HEAD_SIZE), HEAD_SIZE)] = (
                acc[:, i * block:(i + 1) * block].T.astype(BF16)
            )
        acc[...] = jnp.zeros_like(acc)

        def back(step):
            index = pair_at(step)
            pressure = dot(two(vbuf, index, kk), grad, NT).reshape(eights, 8, rows)
            slopes = (pressure - dots[None]) * (facs[kk, step] * scale)[None]
            slopes = score[kk, step] * slopes.reshape(2 * block, rows)
            acc[...] += dot(two(kbuf, index, kk), slopes.astype(BF16), TN)

        each(0, pairs, back)
        for i in range(per):
            qg_ref[:, pl.ds(pl.multiple_of((kk * per + i) * HEAD_SIZE, HEAD_SIZE), HEAD_SIZE)] = (
                acc[:, i * block:(i + 1) * block].T.astype(BF16)
            )

    outputs_early = 2
    each(0, outputs_early, outputs)

    def gather_copy(node, owner):
        return remote(
            result.at[rep, owner], result.at[rep, owner], a_send, a_recv.at[owner], node
        )

    def swap_result(r, owner):
        return remote(
            result.at[rep, owner], result.at[rep, owner], b_send.at[r], b_recv.at[rep], own, r
        )

    @pl.when(own < chunks)
    def _():
        gathered[own] = parts[own]
        all_of(gathered.at[pl.ds(0, slots - 1)], r_recv).wait()
        acc = lax.fori_loop(
            0, slots, lambda t, a: a + gathered[t].astype(F32), jnp.zeros((rank, chunk), F32)
        )
        result[rep, own] = (acc * factor).astype(BF16)
        others(lambda node: gather_copy(node, own).start())
        other_reps(lambda r: swap_result(r, own).start())

    each(outputs_early, KEY_HEADS, outputs)

    def pass_on(owner):
        remote(
            result.at[rep, owner], result.at[rep, owner], a_send, a_recv.at[owner], owner
        ).wait_recv()
        other_reps(lambda r: swap_result(r, owner).start())

    owners(pass_on)

    other_reps(lambda r: all_of(result.at[r], b_recv.at[r]).wait())
    heads_of_two = kbuf.at[pl.ds(0, 2)]
    turned_heads = 2 * KEY_HEADS - keys.turns - values.turns
    turn_bytes = kbuf.at[0]

    def crossed(t):
        crossing = (t > 1) | (own > partner)

        @pl.when(crossing)
        def _():
            all_of(heads_of_two, fwd_send.at[t]).wait()

        if keys.turns + values.turns:
            @pl.when(jnp.logical_not(crossing))
            def _():
                all_of(kbuf.at[0, pl.ds(0, keys.turns + values.turns)], fwd_send.at[t]).wait()

    keys.targets(
        lambda: all_of(heads_of_two, fwd_send.at[0]).wait(),
        lambda t: all_of(heads_of_two, col_send.at[t]).wait(),
    )
    keys.passing(
        0,
        lambda slot: None,
        lambda slot, t: all_of(heads_of_two, on_send.at[t]).wait(),
        lambda slot, t: crossed(t),
    )
    if turned_heads:
        values.turning(
            lambda: all_of(turn_bytes, turn_send).wait()
        )
    lows.targets(
        lambda: all_of(lowbuf.at[0], l_fwd.at[0]).wait(),
        lambda t: all_of(lowbuf.at[0], l_col.at[t]).wait(),
    )
    lows.passing(
        0,
        lambda slot: None,
        lambda slot, t: all_of(lowbuf.at[0], l_on.at[t]).wait(),
        lambda slot, t: all_of(lowbuf.at[0], l_fwd.at[t]).wait(),
    )
    other_reps(lambda r: swap_x(r).wait_send())
    ancestors(lambda t: scatter(own, t).wait_send())
    other_reps(lambda r: swap_up(r).wait_send())
    other_reps(lambda r: swap_total(r).wait_send())

    @pl.when(own < chunks)
    def _():
        all_of(parts.at[pl.ds(0, chunks - 1)], r_send).wait()
        all_of(gathered.at[pl.ds(0, slots - 1)], a_send).wait()

    @pl.when(own >= chunks)
    def _():
        all_of(parts, r_send).wait()

    other_reps(lambda r: all_of(result.at[rep], b_send.at[r]).wait())


def finish(a_ref, b_ref, res, att_ref, qg_ref, down_ref, up_ref, down, up, sems):
    stores = [
        pltpu.make_async_copy(source, target, sems.at[i])
        for i, (source, target) in enumerate(
            [(a_ref, att_ref), (b_ref, qg_ref), (down, down_ref), (up, up_ref)]
        )
    ]
    for c in stores[:2]:
        c.start()
    reps, chunks, rank, chunk = res.shape
    half = down.shape[1] // reps
    up_half = up.shape[1] // reps
    for r in range(reps):
        for j in range(chunks):
            lo, hi = j * chunk, (j + 1) * chunk
            if lo < half:
                end = min(hi, half)
                down[:, r * half + lo:r * half + end] = res[r, j, :, :end - lo].astype(F32)
            if hi > half and lo < half + up_half:
                first, last = max(lo, half), min(hi, half + up_half)
                base = r * up_half - half
                up[:, base + first:base + last] = res[r, j, :, first - lo:last - lo].astype(F32)
    for c in stores[2:]:
        c.start()
    for c in stores:
        c.wait()


def on_device(x, q, k, frozen, down, up, g, parents, lengths):
    x, q, k, frozen, g = x[0], q[0], k[0], frozen[0], g[0]
    block, width = x.shape
    slots, reps = lax.axis_size("node"), lax.axis_size("rep")
    rank, up_width = up.shape
    heads = q.shape[1] // HEAD_SIZE
    rows = heads // KEY_HEADS * block
    pairs = pair_count(slots)
    tiles = -(-(width + up_width) // reps // 128)
    per = -(-tiles // slots)
    chunks = -(-tiles // per)
    chunk = per * 128
    factor = (slots * reps * block) ** -0.5
    anywhere = pl.BlockSpec(memory_space=pl.ANY)
    vmem = pl.BlockSpec(memory_space=pltpu.VMEM)
    smem = pl.BlockSpec(memory_space=pltpu.SMEM)
    dma = pltpu.SemaphoreType.DMA
    v = pltpu.VMEM
    share = KEY_HEADS // reps
    attended, query_grad, result = pl.pallas_call(
        functools.partial(kernel, slots, reps, factor),
        in_specs=[smem, smem, anywhere, anywhere, anywhere, anywhere, anywhere, vmem, anywhere],
        out_specs=[vmem, vmem, vmem],
        out_shape=[v(q.shape, BF16), v(q.shape, BF16), v((reps, chunks, rank, chunk), BF16)],
        scratch_shapes=[
            v(x.shape, BF16), v((reps, block, width // reps), BF16), v((rank, width), BF16),
            v((heads, block, HEAD_SIZE), BF16), v((heads, block, HEAD_SIZE), BF16),
            v(frozen.shape, BF16),
            v((slots, KEY_HEADS, block, HEAD_SIZE), BF16),
            v((slots, KEY_HEADS, block, HEAD_SIZE), BF16),
            v((slots, 1, rank, block), BF16),
            v((KEY_HEADS, pairs, 2 * block, rows), F32),
            v((KEY_HEADS, pairs, 2 * block, rows), BF16),
            v((KEY_HEADS, pairs, 8, rows), F32), v((KEY_HEADS, pairs, 8, rows), F32),
            v((HEAD_SIZE, rows), F32), v((KEY_HEADS, rank, rows), F32),
            v((KEY_HEADS, HEAD_SIZE, rows), BF16),
            v((KEY_HEADS, rank, rows), F32), v((KEY_HEADS, 8, rows), F32),
            v((slots, rank, block), BF16), v((2, rank, block), F32), v((slots, rank, block), BF16),
            v((reps, rank, block), BF16),
            v((KEY_HEADS, rank, HEAD_SIZE), F32), v((reps, share, rank, HEAD_SIZE), F32),
            v((chunks, rank, chunk), BF16), v((slots, rank, chunk), BF16),
            dma((7,)),
            dma((slots, KEY_HEADS)), dma((slots,)), dma((slots, KEY_HEADS)),
            dma((3,)), dma((slots // 2,)), dma((slots // 2,)), dma,
            dma((3,)), dma((slots // 2,)), dma((slots // 2,)),
            dma((reps,)), dma((reps,)), dma((reps,)), dma((reps,)), dma((reps,)), dma((reps,)),
            dma((slots,)), dma((slots,)), dma, dma, dma((slots,)), dma, dma((reps,)), dma((reps,)),
        ],
        compiler_params=pltpu.CompilerParams(
            collective_id=0, has_side_effects=True, vmem_limit_bytes=60 * 1024 * 1024
        ),
        name="tree_attention",
    )(parents, lengths, x, q, k, frozen, down.T, up, g)
    attended, query_grad, down_sum, up_sum = pl.pallas_call(
        finish,
        in_specs=[vmem, vmem, vmem],
        out_specs=[anywhere, anywhere, anywhere, anywhere],
        out_shape=[
            jax.ShapeDtypeStruct(q.shape, BF16),
            jax.ShapeDtypeStruct(q.shape, BF16),
            jax.ShapeDtypeStruct((rank, width), F32),
            jax.ShapeDtypeStruct((rank, up_width), F32),
        ],
        scratch_shapes=[
            v((rank, width), F32), v((rank, up_width), F32), dma((4,)),
        ],
        name="finish",
    )(*[pltpu.with_memory_space_constraint(a, pltpu.VMEM) for a in (attended, query_grad, result)])
    return attended[None], query_grad[None], down_sum.T, up_sum


def solution(mesh):
    rows = P(("groups", "rep"), "node", None)
    table = P(("groups", "rep"), None)
    return jax.shard_map(
        on_device,
        mesh=mesh,
        in_specs=(rows, rows, rows, rows, P(), P(), rows, table, table),
        out_specs=(rows, rows, P("groups", None), P("groups", None)),
        check_vma=False,
    )
```

```python
import functools
import math

import jax
import jax.numpy as jnp
from jax import lax
from jax.experimental import pallas as pl
from jax.experimental.pallas import tpu as pltpu
from jax.sharding import PartitionSpec as P

KEY_HEADS = 4
HEAD_SIZE = 128
PROMPT = 2
SPAN = 5
STEPS = 1 + PROMPT + SPAN
NEGATIVE = -1e30
F32 = jnp.float32
BF16 = jnp.bfloat16
NT = (((1,), (1,)), ((), ()))
NN = (((1,), (0,)), ((), ()))
TN = (((0,), (0,)), ((), ()))
MESH_ID = pl.DeviceIdType.MESH


def dot(a, b, dims):
    return lax.dot_general(a, b, dims, preferred_element_type=F32)


def reaches(slot, below):
    return (below > slot) & ((slot < PROMPT) | (below - slot <= SPAN))


def first_pair(own):
    return jnp.maximum((own + 2 * SPAN - SPAN) // 2 - SPAN, 1)


def pair_count(slots):
    most = 1
    for own in range(slots):
        most = max(most, own // 2 - max((own - SPAN) // 2, 1) + 2)
    return most


def peer(node, rep=None):
    target = {"node": node}
    if rep is not None:
        target["rep"] = rep
    return target


def kernel(
    slots, reps, factor,
    parents, lengths, x_ref, q_ref, k_ref, frozen_ref, down_ref, up_ref, g_ref,
    att_ref, qg_ref, result,
    xs, xcat, downs, qs, gs, fs, kbuf, vbuf, lowbuf, score, weight, tops, facs, acc, gup, gtr,
    lowsum, invs, proj, mine, landed, sums, upk, upland, parts, gathered,
    load_sem, k_recv, l_recv, v_recv, col_send, fwd_send, on_send, turn_send, l_col, l_fwd, l_on,
    x_recv, x_send, u_recv, u_send, p_recv, p_send,
    r_recv, r_send, a_recv, a_send, b_recv, b_send,
):
    own, rep = lax.axis_index("node"), lax.axis_index("rep")
    heads = qs.shape[0]
    per = heads // KEY_HEADS
    block = qs.shape[1]
    rows = per * block
    width = xs.shape[1]
    half = width // reps
    scale = HEAD_SIZE ** -0.5
    pair = own // 2
    partner = own + 1 - 2 * lax.rem(own, 2)
    pairs = pair - first_pair(own) + 2

    barrier = pltpu.get_barrier_semaphore()
    for step in range(reps):
        other = lax.rem(rep + step, reps)

        def signal(t, carry):
            pl.semaphore_signal(
                barrier, inc=1, device_id=peer(lax.rem(own + t, slots), other),
                device_id_type=MESH_ID,
            )
            return carry

        lax.fori_loop(0 if step else 1, slots, signal, 0)

    def remote(src, dst, send, recv, node, r=None):
        return pltpu.make_async_remote_copy(
            src_ref=src, dst_ref=dst, send_sem=send, recv_sem=recv,
            device_id=peer(node, r), device_id_type=MESH_ID,
        )

    loads = [
        pltpu.make_async_copy(down_ref, downs, load_sem.at[1]),
        pltpu.make_async_copy(x_ref, xs, load_sem.at[2]),
        pltpu.make_async_copy(frozen_ref, fs, load_sem.at[3]),
        pltpu.make_async_copy(
            x_ref.at[:, pl.ds(pl.multiple_of(rep * half, 128), half)], xcat.at[rep], load_sem.at[0]
        ),
    ]
    def key_load(kk):
        return pltpu.make_async_copy(
            k_ref.at[:, pl.ds(pl.multiple_of(kk * HEAD_SIZE, HEAD_SIZE), HEAD_SIZE)],
            kbuf.at[own, kk], load_sem.at[4],
        )

    for kk in range(KEY_HEADS):
        key_load(kk).start()
    for c in loads:
        c.start()

    def head_copy(source, target, sem, i):
        return pltpu.make_async_copy(
            source.at[:, pl.ds(pl.multiple_of(i * HEAD_SIZE, HEAD_SIZE), HEAD_SIZE)],
            target.at[i], sem,
        )

    def all_of(buf, sem):
        return pltpu.make_async_copy(buf, buf, sem)

    def each(low, high, action):
        def body(i, carry):
            action(i)
            return carry

        lax.fori_loop(low, high, body, 0)

    each(0, heads, lambda i: head_copy(q_ref, qs, load_sem.at[5], i).start())
    each(0, heads, lambda i: head_copy(g_ref, gs, load_sem.at[6], i).start())

    chain = []
    current = own
    for _ in range(1, STEPS):
        parent = parents[0, jnp.maximum(current, 0)]
        current = jnp.where(current >= 0, parent, -1)
        chain.append(current)
    own_length = lengths[0, own]

    def limit(slot):
        found = slot == own
        for ancestor in chain:
            found = found | (slot == ancestor)
        return jnp.where(found, lengths[0, slot], 0)

    def unsent(slot):
        same = lax.rem(slot + own, 2) == 0
        lands = same & reaches(slot, 2 * pair) | reaches(slot, own)
        return jnp.logical_not(lands | (slot == own))

    def clear_slot(slot):
        @pl.when(unsent(slot))
        def _():
            kbuf[slot] = jnp.zeros(kbuf.shape[1:], BF16)
            vbuf[slot] = jnp.zeros(vbuf.shape[1:], BF16)
            lowbuf[slot] = jnp.zeros(lowbuf.shape[1:], BF16)

    each(0, slots, clear_slot)

    all_of(kbuf.at[own], load_sem.at[4]).wait()
    pl.semaphore_wait(barrier, slots * reps - 1)

    class Stream:
        def __init__(self, buf, col, fwd, on, recv, turns=KEY_HEADS):
            self.buf, self.col, self.fwd, self.on, self.recv = buf, col, fwd, on, recv
            self.turns = turns

        def move(self, slot, kk, send, node):
            block = self.buf.at[slot, kk]
            return remote(block, block, send, self.recv(slot, kk), node)

        def arrived(self, slot, kk):
            self.move(slot, kk, self.fwd.at[0], partner).wait_recv()

        def targets(self, across, column):
            @pl.when(reaches(own, partner))
            def _():
                across()

            for t in (2, 1):
                @pl.when((own + 2 * t < slots) & reaches(own, 2 * (pair + t)))
                def _():
                    column(t)

        def send(self, kk):
            self.targets(
                lambda: self.move(own, kk, self.fwd.at[0], partner).start(),
                lambda t: self.move(own, kk, self.col.at[t], own + 2 * t).start(),
            )

        def passing(self, kk, receive, onward, across):
            def body(t):
                slot = own - 2 * t

                @pl.when(reaches(slot, 2 * pair))
                def _():
                    receive(slot)

                    @pl.when((t >= 2) & (own + 2 < slots) & reaches(slot, 2 * pair + 2))
                    def _():
                        onward(slot, t)

                    crosses = reaches(slot, partner) & (
                        (t > 1) | (own > partner) | (kk < self.turns)
                    )

                    @pl.when(crosses)
                    def _():
                        across(slot, t)

            each(1, pair + 1, body)

        def turning(self, action):
            @pl.when((own > partner) & (own + 2 < slots) & reaches(partner, own + 2))
            def _():
                action()

        def forward(self, kk):
            if self.turns < KEY_HEADS:
                @pl.when((own > partner) & (kk >= self.turns))
                def _():
                    self.arrived(partner, kk)
                    self.turning(lambda: self.move(partner, kk, turn_send, own + 2).start())
            self.passing(
                kk,
                lambda slot: self.arrived(slot, kk),
                lambda slot, t: self.move(slot, kk, self.on.at[t], own + 2).start(),
                lambda slot, t: self.move(slot, kk, self.fwd.at[t], partner).start(),
            )

        def from_partner(self, t, kk):
            slot = partner - 2 * t

            @pl.when(reaches(slot, own) & ((t > 0) | (kk < self.turns)))
            def _():
                self.arrived(slot, kk)

    keys = Stream(
        kbuf, col_send, fwd_send, on_send, lambda slot, kk: k_recv.at[slot, kk], turns=4
    )
    values = Stream(
        vbuf, col_send, fwd_send, on_send, lambda slot, kk: v_recv.at[slot, kk], turns=0
    )
    lows = Stream(lowbuf, l_col, l_fwd, l_on, lambda slot, kk: l_recv.at[slot])
    each(0, KEY_HEADS, keys.send)

    def swap_x(r):
        return remote(
            x_ref.at[:, pl.ds(pl.multiple_of(r * half, 128), half)], xcat.at[rep],
            x_send.at[r], x_recv.at[rep], own, r,
        )

    def other_reps(action):
        for step in range(1, reps):
            action(lax.rem(rep + step, reps))

    other_reps(lambda r: swap_x(r).start())

    loads[0].wait()
    loads[1].wait()
    low = dot(downs[...], xs[...], NT).astype(BF16)
    lowbuf[own, 0] = low
    loads[2].wait()
    own_values = (fs[...].astype(F32) + dot(low, up_ref[...], TN)).astype(BF16)
    for kk in range(KEY_HEADS):
        vbuf[own, kk] = own_values[:, kk * HEAD_SIZE:(kk + 1) * HEAD_SIZE]
    lows.send(0)
    each(0, KEY_HEADS, values.send)

    all_of(qs, load_sem.at[5]).wait()
    all_of(gs, load_sem.at[6]).wait()

    def stacked(buf, kk):
        return buf[pl.ds(kk * per, per)].reshape(rows, HEAD_SIZE)

    def pair_at(step):
        return jnp.where(step == pairs - 1, 0, pair - step)

    def two(buf, index, kk):
        return buf[pl.ds(2 * index, 2), kk].reshape(2 * block, HEAD_SIZE)

    for kk in range(KEY_HEADS):
        lanes = slice(kk * HEAD_SIZE, (kk + 1) * HEAD_SIZE)
        gup[kk] = dot(up_ref[:, lanes], stacked(gs, kk), NT)
        for i in range(per):
            at = slice(i * block, (i + 1) * block)
            gtr[kk, :, at] = gs[kk * per + i].astype(F32).T.astype(BF16)

    tune = scale * math.log2(math.e)
    rank = proj.shape[1]
    eights = 2 * block // 8

    def times(a, row):
        return (a.reshape(-1, 8, rows) * row[None]).reshape(a.shape)

    def eight(row):
        return jnp.broadcast_to(row, (8, rows))

    def scores(kk, step, mask, first):
        s = dot(two(kbuf, pair_at(step), kk), stacked(qs, kk), NT)
        s = jnp.where(mask, s, NEGATIVE).reshape(eights, 8, rows)
        most = eight(jnp.max(jnp.max(s, axis=0), axis=0, keepdims=True))
        if not first:
            most = jnp.maximum(most, tops[kk, step - 1])
        e = jnp.exp2((s - most[None]) * tune)
        score[kk, step] = e.reshape(2 * block, rows)
        weight[kk, step] = e.reshape(2 * block, rows).astype(BF16)
        tops[kk, step] = most
        facs[kk, step] = eight(jnp.sum(jnp.sum(e, axis=0), axis=0, keepdims=True))

    def seen(index):
        return limit(2 * index), limit(2 * index + 1)

    def own_pair(kk):
        keys.from_partner(0, kk)
        key = lax.broadcasted_iota(jnp.int32, (2 * block, block), 0)
        place = lax.rem(key, block)
        query = lax.broadcasted_iota(jnp.int32, (2 * block, block), 1)
        even, odd = seen(pair)
        here = jnp.where(key < block, 2 * pair, 2 * pair + 1) == own
        mask = (place < jnp.where(key < block, even, odd)) & (
            jnp.logical_not(here) | (place <= query)
        )
        scores(kk, 0, jnp.concatenate([mask] * per, axis=1), True)

    def other_pairs(kk):
        def body(t):
            keys.from_partner(t, kk)
            index = pair - t

            @pl.when((index == 0) | (index >= first_pair(own)))
            def _():
                even, odd = seen(index)
                key = lax.broadcasted_iota(jnp.int32, (2 * block, rows), 0)
                mask = lax.rem(key, block) < jnp.where(key < block, even, odd)
                scores(kk, jnp.where(index == 0, pairs - 1, t), mask, False)

        each(1, pair + 1, body)

    keys.forward(0)

    def arrive(kk):
        @pl.when(kk + 1 < KEY_HEADS)
        def _():
            keys.forward(kk + 1)

        @pl.when(kk == KEY_HEADS - 1)
        def _():
            lows.forward(0)

        own_pair(kk)

        other_pairs(kk)

    each(0, KEY_HEADS, arrive)
    values.forward(0)
    live = (
        lax.rem(lax.broadcasted_iota(jnp.int32, (8, rows), 1), block) < own_length
    ).astype(F32)

    def add(step, totals):
        out = []
        for kk in range(KEY_HEADS):
            fall = jnp.exp2((tops[kk, step] - tops[kk, pairs - 1]) * tune)
            out.append(totals[kk] + facs[kk, step] * fall)
            facs[kk, step] = fall
        return tuple(out)

    totals = lax.fori_loop(
        0, pairs, add, tuple(jnp.zeros((8, rows), F32) for _ in range(KEY_HEADS))
    )
    for kk in range(KEY_HEADS):
        invs[kk] = live / totals[kk]

    def scatter(source, target, r):
        return remote(
            proj.at[target], landed.at[rep, source], p_send.at[target], p_recv.at[rep, source],
            target, r,
        )

    def project(i):
        step = pairs - 1 - i
        index = pair_at(step)
        turned = jnp.zeros((2 * rank, 2 * block), F32)
        for kk in range(KEY_HEADS):
            fac = facs[kk, step] * invs[kk]
            facs[kk, step] = fac
            side = times(gup[kk], fac)
            high = side.astype(BF16)
            sides = jnp.concatenate([high, (side - high.astype(F32)).astype(BF16)], axis=0)
            turned = turned + dot(sides, weight[kk, step], NT)
        turned = turned[:rank] + turned[rank:]
        for parity in range(2):
            slot = 2 * index + parity
            mine[parity] = turned[:, parity * block:(parity + 1) * block]
            proj[slot] = mine[parity].astype(BF16)

            @pl.when(reaches(slot, own))
            def _():
                scatter(own, slot, rep).start()
                other_reps(lambda r: scatter(own, slot, r).start())

            @pl.when(slot == own)
            def _():
                other_reps(lambda r: scatter(own, own, r).start())

    each(0, pairs, project)
    values.forward(1)
    values.forward(2)
    values.forward(3)

    def ancestors(action):
        def body(t):
            @pl.when(reaches(t, own))
            def _():
                action(t)

        each(0, slots, body)

    each(0, pair + 1, lambda t: lows.from_partner(t, 0))

    for kk in range(KEY_HEADS):
        lowsum[kk] = jnp.zeros((rank, rows), F32)

    def low_weights(step):
        index = pair_at(step)
        low = jnp.concatenate([lowbuf[2 * index, 0], lowbuf[2 * index + 1, 0]], axis=1)
        for kk in range(KEY_HEADS):
            lowsum[kk] += times(dot(low, weight[kk, step], NN), facs[kk, step])

    each(0, pairs, low_weights)
    for kk in range(KEY_HEADS):
        total = lowsum[kk]
        high = total.astype(BF16)
        sides = jnp.concatenate([high, (total - high.astype(F32)).astype(BF16)], axis=0)
        out = dot(sides, stacked(gs, kk), NN)
        upk[kk] = out[:rank] + out[rank:]

    share = KEY_HEADS // reps

    def swap_up(r):
        return remote(
            upk.at[pl.ds(r * share, share)], upland.at[rep], u_send.at[r], u_recv.at[rep], own, r
        )

    other_reps(lambda r: swap_up(r).start())

    def land(r):
        sums[r] = jnp.where(r == rep, mine[lax.rem(own, 2)], 0.0)

        def body(t):
            @pl.when(reaches(own, t) | (t == own) & (r != rep))
            def _():
                remote(
                    proj.at[t], landed.at[r, t], p_send.at[t], p_recv.at[r, t], t, r
                ).wait_recv()
                sums[r] += landed[r, t].astype(F32)

        each(own, slots, body)

    each(0, reps, land)
    loads[3].wait()

    def arrivals(r):
        remote(
            x_ref.at[:, pl.ds(0, half)], xcat.at[r], x_send.at[r], x_recv.at[r], own, r
        ).wait_recv()
        remote(
            upk.at[pl.ds(0, share)], upland.at[r], u_send.at[r], u_recv.at[r], own, r
        ).wait_recv()

    other_reps(arrivals)

    projected = jnp.concatenate([sums[r] for r in range(reps)], axis=1).astype(BF16)
    ups = upk[pl.ds(rep * share, share)]
    for step in range(1, reps):
        ups = ups + upland[lax.rem(rep + step, reps)]
    upland[rep] = ups
    chunks, _, chunk = parts.shape
    for j in range(chunks):
        lo, hi = j * chunk, (j + 1) * chunk
        pieces = []
        if lo < half:
            end = min(hi, half)
            pieces.append(dot(projected, xcat[:, :, lo:end].reshape(reps * block, end - lo), NN))
        for h in range(share):
            if lo <= half + h * HEAD_SIZE < hi:
                pieces.append(upland[rep, h])
        filled = sum(p.shape[1] for p in pieces)
        if filled < chunk:
            pieces.append(jnp.zeros((rank, chunk - filled), F32))
        value = pieces[0] if len(pieces) == 1 else jnp.concatenate(pieces, axis=1)
        parts[j] = value.astype(BF16)

    def reduce_copy(source, node):
        return remote(
            parts.at[node], gathered.at[source], r_send, r_recv, node
        )

    def others(action):
        each(1, slots, lambda t: action(lax.rem(own + t, slots)))

    def owners(action):
        def body(node):
            @pl.when(node < chunks)
            def _():
                action(node)

        others(body)

    owners(lambda node: reduce_copy(own, node).start())

    def outputs(kk):
        each(0, pair + 1, lambda t: values.from_partner(t, kk))
        grad = stacked(gs, kk)
        acc[...] = jnp.zeros_like(acc)

        def attend(step):
            acc[...] += times(
                dot(two(vbuf, pair_at(step), kk), weight[kk, step], TN), facs[kk, step]
            )

        each(0, pairs, attend)
        out = acc[...]
        dots = (gtr[kk].astype(F32) * out).reshape(HEAD_SIZE // 8, 8, rows)
        dots = eight(jnp.sum(jnp.sum(dots, axis=0), axis=0, keepdims=True))
        for i in range(per):
            att_ref[:, pl.ds(pl.multiple_of((kk * per + i) * HEAD_SIZE, HEAD_SIZE), HEAD_SIZE)] = (
                acc[:, i * block:(i + 1) * block].T.astype(BF16)
            )
        acc[...] = jnp.zeros_like(acc)

        def back(step):
            index = pair_at(step)
            pressure = dot(two(vbuf, index, kk), grad, NT).reshape(eights, 8, rows)
            slopes = (pressure - dots[None]) * (facs[kk, step] * scale)[None]
            slopes = score[kk, step] * slopes.reshape(2 * block, rows)
            acc[...] += dot(two(kbuf, index, kk), slopes.astype(BF16), TN)

        each(0, pairs, back)
        for i in range(per):
            qg_ref[:, pl.ds(pl.multiple_of((kk * per + i) * HEAD_SIZE, HEAD_SIZE), HEAD_SIZE)] = (
                acc[:, i * block:(i + 1) * block].T.astype(BF16)
            )

    outputs_early = 2
    each(0, outputs_early, outputs)

    def gather_copy(node, owner):
        return remote(
            result.at[rep, owner], result.at[rep, owner], a_send, a_recv.at[owner], node
        )

    def swap_result(r, owner):
        return remote(
            result.at[rep, owner], result.at[rep, owner], b_send.at[r], b_recv.at[rep], own, r
        )

    @pl.when(own < chunks)
    def _():
        gathered[own] = parts[own]
        all_of(gathered.at[pl.ds(0, slots - 1)], r_recv).wait()
        acc = jnp.sum(gathered[...].astype(F32), axis=0)
        result[rep, own] = (acc * factor).astype(BF16)
        others(lambda node: gather_copy(node, own).start())
        other_reps(lambda r: swap_result(r, own).start())

    each(outputs_early, KEY_HEADS, outputs)

    def pass_on(owner):
        remote(
            result.at[rep, owner], result.at[rep, owner], a_send, a_recv.at[owner], owner
        ).wait_recv()
        other_reps(lambda r: swap_result(r, owner).start())

    owners(pass_on)

    other_reps(lambda r: all_of(result.at[r], b_recv.at[r]).wait())
    heads_of_two = kbuf.at[pl.ds(0, 2)]
    turned_heads = 2 * KEY_HEADS - keys.turns - values.turns
    turn_bytes = kbuf.at[0]

    def crossed(t):
        crossing = (t > 1) | (own > partner)

        @pl.when(crossing)
        def _():
            all_of(heads_of_two, fwd_send.at[t]).wait()

        if keys.turns + values.turns:
            @pl.when(jnp.logical_not(crossing))
            def _():
                all_of(kbuf.at[0, pl.ds(0, keys.turns + values.turns)], fwd_send.at[t]).wait()

    keys.targets(
        lambda: all_of(heads_of_two, fwd_send.at[0]).wait(),
        lambda t: all_of(heads_of_two, col_send.at[t]).wait(),
    )
    keys.passing(
        0,
        lambda slot: None,
        lambda slot, t: all_of(heads_of_two, on_send.at[t]).wait(),
        lambda slot, t: crossed(t),
    )
    if turned_heads:
        values.turning(
            lambda: all_of(turn_bytes, turn_send).wait()
        )
    lows.targets(
        lambda: all_of(lowbuf.at[0], l_fwd.at[0]).wait(),
        lambda t: all_of(lowbuf.at[0], l_col.at[t]).wait(),
    )
    lows.passing(
        0,
        lambda slot: None,
        lambda slot, t: all_of(lowbuf.at[0], l_on.at[t]).wait(),
        lambda slot, t: all_of(lowbuf.at[0], l_fwd.at[t]).wait(),
    )
    other_reps(lambda r: swap_x(r).wait_send())
    ancestors(lambda t: all_of(proj.at[pl.ds(0, reps)], p_send.at[t]).wait())
    all_of(proj.at[pl.ds(0, reps - 1)], p_send.at[own]).wait()
    other_reps(lambda r: swap_up(r).wait_send())

    @pl.when(own < chunks)
    def _():
        all_of(parts.at[pl.ds(0, chunks - 1)], r_send).wait()
        all_of(gathered.at[pl.ds(0, slots - 1)], a_send).wait()

    @pl.when(own >= chunks)
    def _():
        all_of(parts, r_send).wait()

    other_reps(lambda r: all_of(result.at[rep], b_send.at[r]).wait())


def finish(a_ref, b_ref, res, att_ref, qg_ref, down_ref, up_ref, down, up, sems):
    stores = [
        pltpu.make_async_copy(source, target, sems.at[i])
        for i, (source, target) in enumerate(
            [(a_ref, att_ref), (b_ref, qg_ref), (down, down_ref), (up, up_ref)]
        )
    ]
    for c in stores[:2]:
        c.start()
    reps, chunks, rank, chunk = res.shape
    half = down.shape[1] // reps
    up_half = up.shape[1] // reps
    for r in range(reps):
        for j in range(chunks):
            lo, hi = j * chunk, (j + 1) * chunk
            if lo < half:
                end = min(hi, half)
                down[:, r * half + lo:r * half + end] = res[r, j, :, :end - lo].astype(F32)
            if hi > half and lo < half + up_half:
                first, last = max(lo, half), min(hi, half + up_half)
                base = r * up_half - half
                up[:, base + first:base + last] = res[r, j, :, first - lo:last - lo].astype(F32)
    for c in stores[2:]:
        c.start()
    for c in stores:
        c.wait()


def on_device(x, q, k, frozen, down, up, g, parents, lengths):
    x, q, k, frozen, g = x[0], q[0], k[0], frozen[0], g[0]
    block, width = x.shape
    slots, reps = lax.axis_size("node"), lax.axis_size("rep")
    rank, up_width = up.shape
    heads = q.shape[1] // HEAD_SIZE
    rows = heads // KEY_HEADS * block
    pairs = pair_count(slots)
    tiles = -(-(width + up_width) // reps // 128)
    per = -(-tiles // slots)
    chunks = -(-tiles // per)
    chunk = per * 128
    factor = (slots * reps * block) ** -0.5
    anywhere = pl.BlockSpec(memory_space=pl.ANY)
    vmem = pl.BlockSpec(memory_space=pltpu.VMEM)
    smem = pl.BlockSpec(memory_space=pltpu.SMEM)
    dma = pltpu.SemaphoreType.DMA
    v = pltpu.VMEM
    share = KEY_HEADS // reps
    attended, query_grad, result = pl.pallas_call(
        functools.partial(kernel, slots, reps, factor),
        in_specs=[smem, smem, anywhere, anywhere, anywhere, anywhere, anywhere, vmem, anywhere],
        out_specs=[vmem, vmem, vmem],
        out_shape=[v(q.shape, BF16), v(q.shape, BF16), v((reps, chunks, rank, chunk), BF16)],
        scratch_shapes=[
            v(x.shape, BF16), v((reps, block, width // reps), BF16), v((rank, width), BF16),
            v((heads, block, HEAD_SIZE), BF16), v((heads, block, HEAD_SIZE), BF16),
            v(frozen.shape, BF16),
            v((slots, KEY_HEADS, block, HEAD_SIZE), BF16),
            v((slots, KEY_HEADS, block, HEAD_SIZE), BF16),
            v((slots, 1, rank, block), BF16),
            v((KEY_HEADS, pairs, 2 * block, rows), F32),
            v((KEY_HEADS, pairs, 2 * block, rows), BF16),
            v((KEY_HEADS, pairs, 8, rows), F32), v((KEY_HEADS, pairs, 8, rows), F32),
            v((HEAD_SIZE, rows), F32), v((KEY_HEADS, rank, rows), F32),
            v((KEY_HEADS, HEAD_SIZE, rows), BF16),
            v((KEY_HEADS, rank, rows), F32), v((KEY_HEADS, 8, rows), F32),
            v((slots, rank, block), BF16), v((2, rank, block), F32),
            v((reps, slots, rank, block), BF16), v((reps, rank, block), F32),
            v((KEY_HEADS, rank, HEAD_SIZE), F32), v((reps, share, rank, HEAD_SIZE), F32),
            v((chunks, rank, chunk), BF16), v((slots, rank, chunk), BF16),
            dma((7,)),
            dma((slots, KEY_HEADS)), dma((slots,)), dma((slots, KEY_HEADS)),
            dma((3,)), dma((slots // 2,)), dma((slots // 2,)), dma,
            dma((3,)), dma((slots // 2,)), dma((slots // 2,)),
            dma((reps,)), dma((reps,)), dma((reps,)), dma((reps,)),
            dma((reps, slots)), dma((slots,)), dma, dma, dma((slots,)), dma, dma((reps,)), dma((reps,)),
        ],
        compiler_params=pltpu.CompilerParams(
            collective_id=0, has_side_effects=True, vmem_limit_bytes=60 * 1024 * 1024
        ),
        name="tree_attention",
    )(parents, lengths, x, q, k, frozen, down.T, up, g)
    attended, query_grad, down_sum, up_sum = pl.pallas_call(
        finish,
        in_specs=[vmem, vmem, vmem],
        out_specs=[anywhere, anywhere, anywhere, anywhere],
        out_shape=[
            jax.ShapeDtypeStruct(q.shape, BF16),
            jax.ShapeDtypeStruct(q.shape, BF16),
            jax.ShapeDtypeStruct((rank, width), F32),
            jax.ShapeDtypeStruct((rank, up_width), F32),
        ],
        scratch_shapes=[
            v((rank, width), F32), v((rank, up_width), F32), dma((4,)),
        ],
        name="finish",
    )(*[pltpu.with_memory_space_constraint(a, pltpu.VMEM) for a in (attended, query_grad, result)])
    return attended[None], query_grad[None], down_sum.T, up_sum


def solution(mesh):
    rows = P(("groups", "rep"), "node", None)
    table = P(("groups", "rep"), None)
    return jax.shard_map(
        on_device,
        mesh=mesh,
        in_specs=(rows, rows, rows, rows, P(), P(), rows, table, table),
        out_specs=(rows, rows, P("groups", None), P("groups", None)),
        check_vma=False,
    )
```

```python
import functools
import math

import jax
import jax.numpy as jnp
from jax import lax
from jax.experimental import pallas as pl
from jax.experimental.pallas import tpu as pltpu
from jax.sharding import PartitionSpec as P

KEY_HEADS = 4
HEAD_SIZE = 128
PROMPT = 2
SPAN = 5
STEPS = 1 + PROMPT + SPAN
NEGATIVE = -1e30
F32 = jnp.float32
BF16 = jnp.bfloat16
NT = (((1,), (1,)), ((), ()))
NN = (((1,), (0,)), ((), ()))
TN = (((0,), (0,)), ((), ()))
MESH_ID = pl.DeviceIdType.MESH


def dot(a, b, dims):
    return lax.dot_general(a, b, dims, preferred_element_type=F32)


def reaches(slot, below):
    return (below > slot) & ((slot < PROMPT) | (below - slot <= SPAN))


def first_pair(own):
    return jnp.maximum((own + 2 * SPAN - SPAN) // 2 - SPAN, 1)


def pair_count(slots):
    most = 1
    for own in range(slots):
        most = max(most, own // 2 - max((own - SPAN) // 2, 1) + 2)
    return most


def peer(node, rep=None):
    target = {"node": node}
    if rep is not None:
        target["rep"] = rep
    return target


def kernel(
    slots, reps, factor,
    parents, lengths, x_ref, q_ref, k_ref, frozen_ref, down_ref, up_ref, g_ref,
    att_ref, qg_ref, result,
    xs, xcat, downs, qs, gs, fs, kbuf, vbuf, lowbuf, score, weight, tops, facs, acc, gup, gtr,
    lowsum, invs, proj, mine, landed, sums, upk, upland, parts, gathered,
    load_sem, k_recv, l_recv, v_recv, col_send, fwd_send, on_send, turn_send, l_col, l_fwd, l_on,
    x_recv, x_send, u_recv, u_send, p_recv, p_send,
    r_recv, r_send, a_recv, a_send, b_recv, b_send,
):
    own, rep = lax.axis_index("node"), lax.axis_index("rep")
    heads = qs.shape[0]
    per = heads // KEY_HEADS
    block = qs.shape[1]
    rows = per * block
    width = xs.shape[1]
    half = width // reps
    scale = HEAD_SIZE ** -0.5
    pair = own // 2
    partner = own + 1 - 2 * lax.rem(own, 2)
    pairs = pair - first_pair(own) + 2

    barrier = pltpu.get_barrier_semaphore()
    for step in range(reps):
        other = lax.rem(rep + step, reps)

        def signal(t, carry):
            pl.semaphore_signal(
                barrier, inc=1, device_id=peer(lax.rem(own + t, slots), other),
                device_id_type=MESH_ID,
            )
            return carry

        lax.fori_loop(0 if step else 1, slots, signal, 0)

    def remote(src, dst, send, recv, node, r=None):
        return pltpu.make_async_remote_copy(
            src_ref=src, dst_ref=dst, send_sem=send, recv_sem=recv,
            device_id=peer(node, r), device_id_type=MESH_ID,
        )

    loads = [
        pltpu.make_async_copy(down_ref, downs, load_sem.at[1]),
        pltpu.make_async_copy(x_ref, xs, load_sem.at[2]),
        pltpu.make_async_copy(frozen_ref, fs, load_sem.at[3]),
        pltpu.make_async_copy(
            x_ref.at[:, pl.ds(pl.multiple_of(rep * half, 128), half)], xcat.at[rep], load_sem.at[0]
        ),
    ]
    def key_load(kk):
        return pltpu.make_async_copy(
            k_ref.at[:, pl.ds(pl.multiple_of(kk * HEAD_SIZE, HEAD_SIZE), HEAD_SIZE)],
            kbuf.at[own, kk], load_sem.at[4],
        )

    for kk in range(KEY_HEADS):
        key_load(kk).start()
    for c in loads:
        c.start()

    def head_copy(source, target, sem, i):
        return pltpu.make_async_copy(
            source.at[:, pl.ds(pl.multiple_of(i * HEAD_SIZE, HEAD_SIZE), HEAD_SIZE)],
            target.at[i], sem,
        )

    def all_of(buf, sem):
        return pltpu.make_async_copy(buf, buf, sem)

    def each(low, high, action):
        def body(i, carry):
            action(i)
            return carry

        lax.fori_loop(low, high, body, 0)

    each(0, heads, lambda i: head_copy(q_ref, qs, load_sem.at[5], i).start())
    each(0, heads, lambda i: head_copy(g_ref, gs, load_sem.at[6], i).start())

    chain = []
    current = own
    for _ in range(1, STEPS):
        parent = parents[0, jnp.maximum(current, 0)]
        current = jnp.where(current >= 0, parent, -1)
        chain.append(current)
    own_length = lengths[0, own]

    def limit(slot):
        found = slot == own
        for ancestor in chain:
            found = found | (slot == ancestor)
        return jnp.where(found, lengths[0, slot], 0)

    def unsent(slot):
        same = lax.rem(slot + own, 2) == 0
        lands = same & reaches(slot, 2 * pair) | reaches(slot, own)
        return jnp.logical_not(lands | (slot == own))

    def clear_slot(slot):
        @pl.when(unsent(slot))
        def _():
            kbuf[slot] = jnp.zeros(kbuf.shape[1:], BF16)
            vbuf[slot] = jnp.zeros(vbuf.shape[1:], BF16)
            lowbuf[slot] = jnp.zeros(lowbuf.shape[1:], BF16)

    each(0, slots, clear_slot)

    all_of(kbuf.at[own], load_sem.at[4]).wait()
    pl.semaphore_wait(barrier, slots * reps - 1)

    class Stream:
        def __init__(self, buf, col, fwd, on, recv, turns=KEY_HEADS):
            self.buf, self.col, self.fwd, self.on, self.recv = buf, col, fwd, on, recv
            self.turns = turns

        def move(self, slot, kk, send, node):
            block = self.buf.at[slot, kk]
            return remote(block, block, send, self.recv(slot, kk), node)

        def arrived(self, slot, kk):
            self.move(slot, kk, self.fwd.at[0], partner).wait_recv()

        def targets(self, across, column):
            @pl.when(reaches(own, partner))
            def _():
                across()

            for t in (1, 2):
                @pl.when((own + 2 * t < slots) & reaches(own, 2 * (pair + t)))
                def _():
                    column(t)

        def send(self, kk):
            self.targets(
                lambda: self.move(own, kk, self.fwd.at[0], partner).start(),
                lambda t: self.move(own, kk, self.col.at[t], own + 2 * t).start(),
            )

        def passing(self, kk, receive, onward, across):
            def body(t):
                slot = own - 2 * t

                @pl.when(reaches(slot, 2 * pair))
                def _():
                    receive(slot)

                    @pl.when((t >= 2) & (own + 2 < slots) & reaches(slot, 2 * pair + 2))
                    def _():
                        onward(slot, t)

                    crosses = reaches(slot, partner) & (
                        (t > 1) | (own > partner) | (kk < self.turns)
                    )

                    @pl.when(crosses)
                    def _():
                        across(slot, t)

            each(1, pair + 1, body)

        def turning(self, action):
            @pl.when((own > partner) & (own + 2 < slots) & reaches(partner, own + 2))
            def _():
                action()

        def forward(self, kk):
            if self.turns < KEY_HEADS:
                @pl.when((own > partner) & (kk >= self.turns))
                def _():
                    self.arrived(partner, kk)
                    self.turning(lambda: self.move(partner, kk, turn_send, own + 2).start())
            self.passing(
                kk,
                lambda slot: self.arrived(slot, kk),
                lambda slot, t: self.move(slot, kk, self.on.at[t], own + 2).start(),
                lambda slot, t: self.move(slot, kk, self.fwd.at[t], partner).start(),
            )

        def from_partner(self, t, kk):
            slot = partner - 2 * t

            @pl.when(reaches(slot, own) & ((t > 0) | (kk < self.turns)))
            def _():
                self.arrived(slot, kk)

    keys = Stream(
        kbuf, col_send, fwd_send, on_send, lambda slot, kk: k_recv.at[slot, kk], turns=4
    )
    values = Stream(
        vbuf, col_send, fwd_send, on_send, lambda slot, kk: v_recv.at[slot, kk], turns=0
    )
    lows = Stream(lowbuf, l_col, l_fwd, l_on, lambda slot, kk: l_recv.at[slot])
    each(0, KEY_HEADS, keys.send)

    def swap_x(r):
        return remote(
            x_ref.at[:, pl.ds(pl.multiple_of(r * half, 128), half)], xcat.at[rep],
            x_send.at[r], x_recv.at[rep], own, r,
        )

    def other_reps(action):
        for step in range(1, reps):
            action(lax.rem(rep + step, reps))

    other_reps(lambda r: swap_x(r).start())

    loads[0].wait()
    loads[1].wait()
    low = dot(downs[...], xs[...], NT).astype(BF16)
    lowbuf[own, 0] = low
    loads[2].wait()
    own_values = (fs[...].astype(F32) + dot(low, up_ref[...], TN)).astype(BF16)
    for kk in range(KEY_HEADS):
        vbuf[own, kk] = own_values[:, kk * HEAD_SIZE:(kk + 1) * HEAD_SIZE]
    lows.send(0)
    each(0, KEY_HEADS, values.send)

    all_of(qs, load_sem.at[5]).wait()
    all_of(gs, load_sem.at[6]).wait()

    def stacked(buf, kk):
        return buf[pl.ds(kk * per, per)].reshape(rows, HEAD_SIZE)

    def pair_at(step):
        return jnp.where(step == pairs - 1, 0, pair - step)

    def two(buf, index, kk):
        return buf[pl.ds(2 * index, 2), kk].reshape(2 * block, HEAD_SIZE)

    for kk in range(KEY_HEADS):
        lanes = slice(kk * HEAD_SIZE, (kk + 1) * HEAD_SIZE)
        gup[kk] = dot(up_ref[:, lanes], stacked(gs, kk), NT)
        for i in range(per):
            at = slice(i * block, (i + 1) * block)
            gtr[kk, :, at] = gs[kk * per + i].astype(F32).T.astype(BF16)

    tune = scale * math.log2(math.e)
    rank = proj.shape[1]
    eights = 2 * block // 8

    def times(a, row):
        return (a.reshape(-1, 8, rows) * row[None]).reshape(a.shape)

    def eight(row):
        return jnp.broadcast_to(row, (8, rows))

    def scores(kk, step, mask, first):
        s = dot(two(kbuf, pair_at(step), kk), stacked(qs, kk), NT)
        s = jnp.where(mask, s, NEGATIVE).reshape(eights, 8, rows)
        most = eight(jnp.max(jnp.max(s, axis=0), axis=0, keepdims=True))
        if not first:
            most = jnp.maximum(most, tops[kk, step - 1])
        e = jnp.exp2((s - most[None]) * tune)
        score[kk, step] = e.reshape(2 * block, rows)
        weight[kk, step] = e.reshape(2 * block, rows).astype(BF16)
        tops[kk, step] = most
        facs[kk, step] = eight(jnp.sum(jnp.sum(e, axis=0), axis=0, keepdims=True))

    def seen(index):
        return limit(2 * index), limit(2 * index + 1)

    def own_pair(kk):
        keys.from_partner(0, kk)
        key = lax.broadcasted_iota(jnp.int32, (2 * block, block), 0)
        place = lax.rem(key, block)
        query = lax.broadcasted_iota(jnp.int32, (2 * block, block), 1)
        even, odd = seen(pair)
        here = jnp.where(key < block, 2 * pair, 2 * pair + 1) == own
        mask = (place < jnp.where(key < block, even, odd)) & (
            jnp.logical_not(here) | (place <= query)
        )
        scores(kk, 0, jnp.concatenate([mask] * per, axis=1), True)

    def other_pairs(kk):
        def body(t):
            keys.from_partner(t, kk)
            index = pair - t

            @pl.when((index == 0) | (index >= first_pair(own)))
            def _():
                even, odd = seen(index)
                key = lax.broadcasted_iota(jnp.int32, (2 * block, rows), 0)
                mask = lax.rem(key, block) < jnp.where(key < block, even, odd)
                scores(kk, jnp.where(index == 0, pairs - 1, t), mask, False)

        each(1, pair + 1, body)

    keys.forward(0)

    def arrive(kk):
        @pl.when(kk + 1 < KEY_HEADS)
        def _():
            keys.forward(kk + 1)

        @pl.when(kk == KEY_HEADS - 1)
        def _():
            lows.forward(0)

        own_pair(kk)

        other_pairs(kk)

    each(0, KEY_HEADS, arrive)
    values.forward(0)
    live = (
        lax.rem(lax.broadcasted_iota(jnp.int32, (8, rows), 1), block) < own_length
    ).astype(F32)

    def add(step, totals):
        out = []
        for kk in range(KEY_HEADS):
            fall = jnp.exp2((tops[kk, step] - tops[kk, pairs - 1]) * tune)
            out.append(totals[kk] + facs[kk, step] * fall)
            facs[kk, step] = fall
        return tuple(out)

    totals = lax.fori_loop(
        0, pairs, add, tuple(jnp.zeros((8, rows), F32) for _ in range(KEY_HEADS))
    )
    for kk in range(KEY_HEADS):
        invs[kk] = live / totals[kk]

    def scatter(source, target, r):
        return remote(
            proj.at[target], landed.at[rep, source], p_send.at[target], p_recv.at[rep, source],
            target, r,
        )

    def project(i):
        step = pairs - 1 - i
        index = pair_at(step)
        turned = jnp.zeros((2 * rank, 2 * block), F32)
        for kk in range(KEY_HEADS):
            fac = facs[kk, step] * invs[kk]
            facs[kk, step] = fac
            side = times(gup[kk], fac)
            high = side.astype(BF16)
            sides = jnp.concatenate([high, (side - high.astype(F32)).astype(BF16)], axis=0)
            turned = turned + dot(sides, weight[kk, step], NT)
        turned = turned[:rank] + turned[rank:]
        for parity in range(2):
            slot = 2 * index + parity
            mine[parity] = turned[:, parity * block:(parity + 1) * block]
            proj[slot] = mine[parity].astype(BF16)

            @pl.when(reaches(slot, own))
            def _():
                scatter(own, slot, rep).start()
                other_reps(lambda r: scatter(own, slot, r).start())

            @pl.when(slot == own)
            def _():
                other_reps(lambda r: scatter(own, own, r).start())

    each(0, pairs, project)
    values.forward(1)
    values.forward(2)
    values.forward(3)

    def ancestors(action):
        def body(t):
            @pl.when(reaches(t, own))
            def _():
                action(t)

        each(0, slots, body)

    each(0, pair + 1, lambda t: lows.from_partner(t, 0))

    for kk in range(KEY_HEADS):
        lowsum[kk] = jnp.zeros((rank, rows), F32)

    def low_weights(step):
        index = pair_at(step)
        low = jnp.concatenate([lowbuf[2 * index, 0], lowbuf[2 * index + 1, 0]], axis=1)
        for kk in range(KEY_HEADS):
            lowsum[kk] += times(dot(low, weight[kk, step], NN), facs[kk, step])

    each(0, pairs, low_weights)
    for kk in range(KEY_HEADS):
        total = lowsum[kk]
        high = total.astype(BF16)
        sides = jnp.concatenate([high, (total - high.astype(F32)).astype(BF16)], axis=0)
        out = dot(sides, stacked(gs, kk), NN)
        upk[kk] = out[:rank] + out[rank:]

    share = KEY_HEADS // reps

    def swap_up(r):
        return remote(
            upk.at[pl.ds(r * share, share)], upland.at[rep], u_send.at[r], u_recv.at[rep], own, r
        )

    other_reps(lambda r: swap_up(r).start())

    def land(r):
        sums[r] = jnp.where(r == rep, mine[lax.rem(own, 2)], 0.0)

        def body(t):
            @pl.when(reaches(own, t) | (t == own) & (r != rep))
            def _():
                remote(
                    proj.at[t], landed.at[r, t], p_send.at[t], p_recv.at[r, t], t, r
                ).wait_recv()
                sums[r] += landed[r, t].astype(F32)

        each(own, slots, body)

    each(0, reps, land)
    loads[3].wait()

    def arrivals(r):
        remote(
            x_ref.at[:, pl.ds(0, half)], xcat.at[r], x_send.at[r], x_recv.at[r], own, r
        ).wait_recv()
        remote(
            upk.at[pl.ds(0, share)], upland.at[r], u_send.at[r], u_recv.at[r], own, r
        ).wait_recv()

    other_reps(arrivals)

    projected = jnp.concatenate([sums[r] for r in range(reps)], axis=1).astype(BF16)
    ups = upk[pl.ds(rep * share, share)]
    for step in range(1, reps):
        ups = ups + upland[lax.rem(rep + step, reps)]
    upland[rep] = ups
    chunks, _, chunk = parts.shape
    for j in range(chunks):
        lo, hi = j * chunk, (j + 1) * chunk
        pieces = []
        if lo < half:
            end = min(hi, half)
            pieces.append(dot(projected, xcat[:, :, lo:end].reshape(reps * block, end - lo), NN))
        for h in range(share):
            if lo <= half + h * HEAD_SIZE < hi:
                pieces.append(upland[rep, h])
        filled = sum(p.shape[1] for p in pieces)
        if filled < chunk:
            pieces.append(jnp.zeros((rank, chunk - filled), F32))
        value = pieces[0] if len(pieces) == 1 else jnp.concatenate(pieces, axis=1)
        parts[j] = value.astype(BF16)

    def reduce_copy(source, node):
        return remote(
            parts.at[node], gathered.at[source], r_send, r_recv, node
        )

    def others(action):
        each(1, slots, lambda t: action(lax.rem(own + t, slots)))

    def owners(action):
        def body(node):
            @pl.when(node < chunks)
            def _():
                action(node)

        others(body)

    owners(lambda node: reduce_copy(own, node).start())

    def outputs(kk):
        each(0, pair + 1, lambda t: values.from_partner(t, kk))
        grad = stacked(gs, kk)
        acc[...] = jnp.zeros_like(acc)

        def attend(step):
            acc[...] += times(
                dot(two(vbuf, pair_at(step), kk), weight[kk, step], TN), facs[kk, step]
            )

        each(0, pairs, attend)
        out = acc[...]
        dots = (gtr[kk].astype(F32) * out).reshape(HEAD_SIZE // 8, 8, rows)
        dots = eight(jnp.sum(jnp.sum(dots, axis=0), axis=0, keepdims=True))
        for i in range(per):
            att_ref[:, pl.ds(pl.multiple_of((kk * per + i) * HEAD_SIZE, HEAD_SIZE), HEAD_SIZE)] = (
                acc[:, i * block:(i + 1) * block].T.astype(BF16)
            )
        acc[...] = jnp.zeros_like(acc)

        def back(step):
            index = pair_at(step)
            pressure = dot(two(vbuf, index, kk), grad, NT).reshape(eights, 8, rows)
            slopes = (pressure - dots[None]) * (facs[kk, step] * scale)[None]
            slopes = score[kk, step] * slopes.reshape(2 * block, rows)
            acc[...] += dot(two(kbuf, index, kk), slopes.astype(BF16), TN)

        each(0, pairs, back)
        for i in range(per):
            qg_ref[:, pl.ds(pl.multiple_of((kk * per + i) * HEAD_SIZE, HEAD_SIZE), HEAD_SIZE)] = (
                acc[:, i * block:(i + 1) * block].T.astype(BF16)
            )

    outputs_early = 2
    each(0, outputs_early, outputs)

    def gather_copy(node, owner):
        return remote(
            result.at[rep, owner], result.at[rep, owner], a_send, a_recv.at[owner], node
        )

    def swap_result(r, owner):
        return remote(
            result.at[rep, owner], result.at[rep, owner], b_send.at[r], b_recv.at[rep], own, r
        )

    @pl.when(own < chunks)
    def _():
        gathered[own] = parts[own]
        all_of(gathered.at[pl.ds(0, slots - 1)], r_recv).wait()
        acc = jnp.sum(gathered[...].astype(F32), axis=0)
        result[rep, own] = (acc * factor).astype(BF16)
        others(lambda node: gather_copy(node, own).start())
        other_reps(lambda r: swap_result(r, own).start())

    each(outputs_early, KEY_HEADS, outputs)

    def pass_on(owner):
        remote(
            result.at[rep, owner], result.at[rep, owner], a_send, a_recv.at[owner], owner
        ).wait_recv()
        other_reps(lambda r: swap_result(r, owner).start())

    owners(pass_on)

    other_reps(lambda r: all_of(result.at[r], b_recv.at[r]).wait())
    heads_of_two = kbuf.at[pl.ds(0, 2)]
    turned_heads = 2 * KEY_HEADS - keys.turns - values.turns
    turn_bytes = kbuf.at[0]

    def crossed(t):
        crossing = (t > 1) | (own > partner)

        @pl.when(crossing)
        def _():
            all_of(heads_of_two, fwd_send.at[t]).wait()

        if keys.turns + values.turns:
            @pl.when(jnp.logical_not(crossing))
            def _():
                all_of(kbuf.at[0, pl.ds(0, keys.turns + values.turns)], fwd_send.at[t]).wait()

    keys.targets(
        lambda: all_of(heads_of_two, fwd_send.at[0]).wait(),
        lambda t: all_of(heads_of_two, col_send.at[t]).wait(),
    )
    keys.passing(
        0,
        lambda slot: None,
        lambda slot, t: all_of(heads_of_two, on_send.at[t]).wait(),
        lambda slot, t: crossed(t),
    )
    if turned_heads:
        values.turning(
            lambda: all_of(turn_bytes, turn_send).wait()
        )
    lows.targets(
        lambda: all_of(lowbuf.at[0], l_fwd.at[0]).wait(),
        lambda t: all_of(lowbuf.at[0], l_col.at[t]).wait(),
    )
    lows.passing(
        0,
        lambda slot: None,
        lambda slot, t: all_of(lowbuf.at[0], l_on.at[t]).wait(),
        lambda slot, t: all_of(lowbuf.at[0], l_fwd.at[t]).wait(),
    )
    other_reps(lambda r: swap_x(r).wait_send())
    ancestors(lambda t: all_of(proj.at[pl.ds(0, reps)], p_send.at[t]).wait())
    all_of(proj.at[pl.ds(0, reps - 1)], p_send.at[own]).wait()
    other_reps(lambda r: swap_up(r).wait_send())

    @pl.when(own < chunks)
    def _():
        all_of(parts.at[pl.ds(0, chunks - 1)], r_send).wait()
        all_of(gathered.at[pl.ds(0, slots - 1)], a_send).wait()

    @pl.when(own >= chunks)
    def _():
        all_of(parts, r_send).wait()

    other_reps(lambda r: all_of(result.at[rep], b_send.at[r]).wait())


def finish(a_ref, b_ref, res, att_ref, qg_ref, down_ref, up_ref, down, up, sems):
    stores = [
        pltpu.make_async_copy(source, target, sems.at[i])
        for i, (source, target) in enumerate(
            [(a_ref, att_ref), (b_ref, qg_ref), (down, down_ref), (up, up_ref)]
        )
    ]
    for c in stores[:2]:
        c.start()
    reps, chunks, rank, chunk = res.shape
    half = down.shape[1] // reps
    up_half = up.shape[1] // reps
    for r in range(reps):
        for j in range(chunks):
            lo, hi = j * chunk, (j + 1) * chunk
            if lo < half:
                end = min(hi, half)
                down[:, r * half + lo:r * half + end] = res[r, j, :, :end - lo].astype(F32)
            if hi > half and lo < half + up_half:
                first, last = max(lo, half), min(hi, half + up_half)
                base = r * up_half - half
                up[:, base + first:base + last] = res[r, j, :, first - lo:last - lo].astype(F32)
    for c in stores[2:]:
        c.start()
    for c in stores:
        c.wait()


def on_device(x, q, k, frozen, down, up, g, parents, lengths):
    x, q, k, frozen, g = x[0], q[0], k[0], frozen[0], g[0]
    block, width = x.shape
    slots, reps = lax.axis_size("node"), lax.axis_size("rep")
    rank, up_width = up.shape
    heads = q.shape[1] // HEAD_SIZE
    rows = heads // KEY_HEADS * block
    pairs = pair_count(slots)
    tiles = -(-(width + up_width) // reps // 128)
    per = -(-tiles // slots)
    chunks = -(-tiles // per)
    chunk = per * 128
    factor = (slots * reps * block) ** -0.5
    anywhere = pl.BlockSpec(memory_space=pl.ANY)
    vmem = pl.BlockSpec(memory_space=pltpu.VMEM)
    smem = pl.BlockSpec(memory_space=pltpu.SMEM)
    dma = pltpu.SemaphoreType.DMA
    v = pltpu.VMEM
    share = KEY_HEADS // reps
    attended, query_grad, result = pl.pallas_call(
        functools.partial(kernel, slots, reps, factor),
        in_specs=[smem, smem, anywhere, anywhere, anywhere, anywhere, anywhere, vmem, anywhere],
        out_specs=[vmem, vmem, vmem],
        out_shape=[v(q.shape, BF16), v(q.shape, BF16), v((reps, chunks, rank, chunk), BF16)],
        scratch_shapes=[
            v(x.shape, BF16), v((reps, block, width // reps), BF16), v((rank, width), BF16),
            v((heads, block, HEAD_SIZE), BF16), v((heads, block, HEAD_SIZE), BF16),
            v(frozen.shape, BF16),
            v((slots, KEY_HEADS, block, HEAD_SIZE), BF16),
            v((slots, KEY_HEADS, block, HEAD_SIZE), BF16),
            v((slots, 1, rank, block), BF16),
            v((KEY_HEADS, pairs, 2 * block, rows), F32),
            v((KEY_HEADS, pairs, 2 * block, rows), BF16),
            v((KEY_HEADS, pairs, 8, rows), F32), v((KEY_HEADS, pairs, 8, rows), F32),
            v((HEAD_SIZE, rows), F32), v((KEY_HEADS, rank, rows), F32),
            v((KEY_HEADS, HEAD_SIZE, rows), BF16),
            v((KEY_HEADS, rank, rows), F32), v((KEY_HEADS, 8, rows), F32),
            v((slots, rank, block), BF16), v((2, rank, block), F32),
            v((reps, slots, rank, block), BF16), v((reps, rank, block), F32),
            v((KEY_HEADS, rank, HEAD_SIZE), F32), v((reps, share, rank, HEAD_SIZE), F32),
            v((chunks, rank, chunk), BF16), v((slots, rank, chunk), BF16),
            dma((7,)),
            dma((slots, KEY_HEADS)), dma((slots,)), dma((slots, KEY_HEADS)),
            dma((3,)), dma((slots // 2,)), dma((slots // 2,)), dma,
            dma((3,)), dma((slots // 2,)), dma((slots // 2,)),
            dma((reps,)), dma((reps,)), dma((reps,)), dma((reps,)),
            dma((reps, slots)), dma((slots,)), dma, dma, dma((slots,)), dma, dma((reps,)), dma((reps,)),
        ],
        compiler_params=pltpu.CompilerParams(
            collective_id=0, has_side_effects=True, vmem_limit_bytes=60 * 1024 * 1024
        ),
        name="tree_attention",
    )(parents, lengths, x, q, k, frozen, down.T, up, g)
    attended, query_grad, down_sum, up_sum = pl.pallas_call(
        finish,
        in_specs=[vmem, vmem, vmem],
        out_specs=[anywhere, anywhere, anywhere, anywhere],
        out_shape=[
            jax.ShapeDtypeStruct(q.shape, BF16),
            jax.ShapeDtypeStruct(q.shape, BF16),
            jax.ShapeDtypeStruct((rank, width), F32),
            jax.ShapeDtypeStruct((rank, up_width), F32),
        ],
        scratch_shapes=[
            v((rank, width), F32), v((rank, up_width), F32), dma((4,)),
        ],
        name="finish",
    )(*[pltpu.with_memory_space_constraint(a, pltpu.VMEM) for a in (attended, query_grad, result)])
    return attended[None], query_grad[None], down_sum.T, up_sum


def solution(mesh):
    rows = P(("groups", "rep"), "node", None)
    table = P(("groups", "rep"), None)
    return jax.shard_map(
        on_device,
        mesh=mesh,
        in_specs=(rows, rows, rows, rows, P(), P(), rows, table, table),
        out_specs=(rows, rows, P("groups", None), P("groups", None)),
        check_vma=False,
    )
```

```python
import functools
import math

import jax
import jax.numpy as jnp
from jax import lax
from jax.experimental import pallas as pl
from jax.experimental.pallas import tpu as pltpu
from jax.sharding import PartitionSpec as P

KEY_HEADS = 4
HEAD_SIZE = 128
PROMPT = 2
SPAN = 5
STEPS = 1 + PROMPT + SPAN
NEGATIVE = -1e30
F32 = jnp.float32
BF16 = jnp.bfloat16
NT = (((1,), (1,)), ((), ()))
NN = (((1,), (0,)), ((), ()))
TN = (((0,), (0,)), ((), ()))
MESH_ID = pl.DeviceIdType.MESH


def dot(a, b, dims):
    return lax.dot_general(a, b, dims, preferred_element_type=F32)


def reaches(slot, below):
    return (below > slot) & ((slot < PROMPT) | (below - slot <= SPAN))


def first_pair(own):
    return jnp.maximum((own + 2 * SPAN - SPAN) // 2 - SPAN, 1)


def pair_count(slots):
    most = 1
    for own in range(slots):
        most = max(most, own // 2 - max((own - SPAN) // 2, 1) + 2)
    return most


def peer(node, rep=None):
    target = {"node": node}
    if rep is not None:
        target["rep"] = rep
    return target


def kernel(
    slots, reps, factor,
    parents, lengths, x_ref, q_ref, k_ref, frozen_ref, down_ref, up_ref, g_ref,
    att_ref, qg_ref, result,
    xs, xcat, downs, qs, gs, fs, kbuf, vbuf, lowbuf, score, weight, tops, facs, acc, gup, gtr,
    lowsum, invs, proj, mine, landed, sums, upk, upland, parts, gathered,
    load_sem, k_recv, l_recv, v_recv, col_send, fwd_send, on_send, turn_send, l_col, l_fwd, l_on,
    x_recv, x_send, u_recv, u_send, p_recv, p_send,
    r_recv, r_send, a_recv, a_send, b_recv, b_send,
):
    own, rep = lax.axis_index("node"), lax.axis_index("rep")
    heads = qs.shape[0]
    per = heads // KEY_HEADS
    block = qs.shape[1]
    rows = per * block
    width = xs.shape[1]
    half = width // reps
    scale = HEAD_SIZE ** -0.5
    pair = own // 2
    partner = own + 1 - 2 * lax.rem(own, 2)
    pairs = pair - first_pair(own) + 2

    barrier = pltpu.get_barrier_semaphore()
    for step in range(reps):
        other = lax.rem(rep + step, reps)

        def signal(t, carry):
            pl.semaphore_signal(
                barrier, inc=1, device_id=peer(lax.rem(own + t, slots), other),
                device_id_type=MESH_ID,
            )
            return carry

        lax.fori_loop(0 if step else 1, slots, signal, 0)

    def remote(src, dst, send, recv, node, r=None):
        return pltpu.make_async_remote_copy(
            src_ref=src, dst_ref=dst, send_sem=send, recv_sem=recv,
            device_id=peer(node, r), device_id_type=MESH_ID,
        )

    loads = [
        pltpu.make_async_copy(down_ref, downs, load_sem.at[1]),
        pltpu.make_async_copy(x_ref, xs, load_sem.at[2]),
        pltpu.make_async_copy(frozen_ref, fs, load_sem.at[3]),
        pltpu.make_async_copy(
            x_ref.at[:, pl.ds(pl.multiple_of(rep * half, 128), half)], xcat.at[rep], load_sem.at[0]
        ),
    ]
    def key_load(kk):
        return pltpu.make_async_copy(
            k_ref.at[:, pl.ds(pl.multiple_of(kk * HEAD_SIZE, HEAD_SIZE), HEAD_SIZE)],
            kbuf.at[own, kk], load_sem.at[4],
        )

    for kk in range(KEY_HEADS):
        key_load(kk).start()
    for c in loads:
        c.start()

    def head_copy(source, target, sem, i):
        return pltpu.make_async_copy(
            source.at[:, pl.ds(pl.multiple_of(i * HEAD_SIZE, HEAD_SIZE), HEAD_SIZE)],
            target.at[i], sem,
        )

    def all_of(buf, sem):
        return pltpu.make_async_copy(buf, buf, sem)

    def each(low, high, action):
        def body(i, carry):
            action(i)
            return carry

        lax.fori_loop(low, high, body, 0)

    each(0, heads, lambda i: head_copy(q_ref, qs, load_sem.at[5], i).start())
    each(0, heads, lambda i: head_copy(g_ref, gs, load_sem.at[6], i).start())

    chain = []
    current = own
    for _ in range(1, STEPS):
        parent = parents[0, jnp.maximum(current, 0)]
        current = jnp.where(current >= 0, parent, -1)
        chain.append(current)
    own_length = lengths[0, own]

    def limit(slot):
        found = slot == own
        for ancestor in chain:
            found = found | (slot == ancestor)
        return jnp.where(found, lengths[0, slot], 0)

    def unsent(slot):
        same = lax.rem(slot + own, 2) == 0
        lands = same & reaches(slot, 2 * pair) | reaches(slot, own)
        return jnp.logical_not(lands | (slot == own))

    def clear_slot(slot):
        @pl.when(unsent(slot))
        def _():
            kbuf[slot] = jnp.zeros(kbuf.shape[1:], BF16)
            vbuf[slot] = jnp.zeros(vbuf.shape[1:], BF16)
            lowbuf[slot] = jnp.zeros(lowbuf.shape[1:], BF16)

    each(0, slots, clear_slot)

    all_of(kbuf.at[own], load_sem.at[4]).wait()
    pl.semaphore_wait(barrier, slots * reps - 1)

    class Stream:
        def __init__(self, buf, col, fwd, on, recv, turns=KEY_HEADS):
            self.buf, self.col, self.fwd, self.on, self.recv = buf, col, fwd, on, recv
            self.turns = turns

        def move(self, slot, kk, send, node):
            block = self.buf.at[slot, kk]
            return remote(block, block, send, self.recv(slot, kk), node)

        def arrived(self, slot, kk):
            self.move(slot, kk, self.fwd.at[0], partner).wait_recv()

        def targets(self, across, column):
            @pl.when(reaches(own, partner))
            def _():
                across()

            for t in (1, 2):
                @pl.when((own + 2 * t < slots) & reaches(own, 2 * (pair + t)))
                def _():
                    column(t)

        def send(self, kk):
            self.targets(
                lambda: self.move(own, kk, self.fwd.at[0], partner).start(),
                lambda t: self.move(own, kk, self.col.at[t], own + 2 * t).start(),
            )

        def passing(self, kk, receive, onward, across):
            def body(t):
                slot = own - 2 * t

                @pl.when(reaches(slot, 2 * pair))
                def _():
                    receive(slot)

                    @pl.when((t >= 2) & (own + 2 < slots) & reaches(slot, 2 * pair + 2))
                    def _():
                        onward(slot, t)

                    crosses = reaches(slot, partner) & (
                        (t > 1) | (own > partner) | (kk < self.turns)
                    )

                    @pl.when(crosses)
                    def _():
                        across(slot, t)

            each(1, pair + 1, body)

        def turning(self, action):
            @pl.when((own > partner) & (own + 2 < slots) & reaches(partner, own + 2))
            def _():
                action()

        def forward(self, kk):
            if self.turns < KEY_HEADS:
                @pl.when((own > partner) & (kk >= self.turns))
                def _():
                    self.arrived(partner, kk)
                    self.turning(lambda: self.move(partner, kk, turn_send, own + 2).start())
            self.passing(
                kk,
                lambda slot: self.arrived(slot, kk),
                lambda slot, t: self.move(slot, kk, self.on.at[t], own + 2).start(),
                lambda slot, t: self.move(slot, kk, self.fwd.at[t], partner).start(),
            )

        def from_partner(self, t, kk):
            slot = partner - 2 * t

            @pl.when(reaches(slot, own) & ((t > 0) | (kk < self.turns)))
            def _():
                self.arrived(slot, kk)

    keys = Stream(
        kbuf, col_send, fwd_send, on_send, lambda slot, kk: k_recv.at[slot, kk], turns=4
    )
    values = Stream(
        vbuf, col_send, fwd_send, on_send, lambda slot, kk: v_recv.at[slot, kk], turns=0
    )
    lows = Stream(lowbuf, l_col, l_fwd, l_on, lambda slot, kk: l_recv.at[slot])
    each(0, KEY_HEADS, keys.send)

    def swap_x(r):
        return remote(
            x_ref.at[:, pl.ds(pl.multiple_of(r * half, 128), half)], xcat.at[rep],
            x_send.at[r], x_recv.at[rep], own, r,
        )

    def other_reps(action):
        for step in range(1, reps):
            action(lax.rem(rep + step, reps))

    other_reps(lambda r: swap_x(r).start())

    loads[0].wait()
    loads[1].wait()
    low = dot(downs[...], xs[...], NT).astype(BF16)
    lowbuf[own, 0] = low
    loads[2].wait()
    own_values = (fs[...].astype(F32) + dot(low, up_ref[...], TN)).astype(BF16)
    for kk in range(KEY_HEADS):
        vbuf[own, kk] = own_values[:, kk * HEAD_SIZE:(kk + 1) * HEAD_SIZE]
    lows.send(0)
    each(0, KEY_HEADS, values.send)

    all_of(qs, load_sem.at[5]).wait()
    all_of(gs, load_sem.at[6]).wait()

    def stacked(buf, kk):
        return buf[pl.ds(kk * per, per)].reshape(rows, HEAD_SIZE)

    def pair_at(step):
        return jnp.where(step == pairs - 1, 0, pair - step)

    def two(buf, index, kk):
        return buf[pl.ds(2 * index, 2), kk].reshape(2 * block, HEAD_SIZE)

    for kk in range(KEY_HEADS):
        lanes = slice(kk * HEAD_SIZE, (kk + 1) * HEAD_SIZE)
        gup[kk] = dot(up_ref[:, lanes], stacked(gs, kk), NT)
        for i in range(per):
            at = slice(i * block, (i + 1) * block)
            gtr[kk, :, at] = gs[kk * per + i].astype(F32).T.astype(BF16)

    tune = scale * math.log2(math.e)
    rank = proj.shape[1]
    eights = 2 * block // 8

    def times(a, row):
        return (a.reshape(-1, 8, rows) * row[None]).reshape(a.shape)

    def eight(row):
        return jnp.broadcast_to(row, (8, rows))

    def scores(kk, step, mask, first):
        s = dot(two(kbuf, pair_at(step), kk), stacked(qs, kk), NT)
        s = jnp.where(mask, s, NEGATIVE).reshape(eights, 8, rows)
        most = eight(jnp.max(jnp.max(s, axis=0), axis=0, keepdims=True))
        if not first:
            most = jnp.maximum(most, tops[kk, step - 1])
        e = jnp.exp2((s - most[None]) * tune)
        score[kk, step] = e.reshape(2 * block, rows)
        weight[kk, step] = e.reshape(2 * block, rows).astype(BF16)
        tops[kk, step] = most
        facs[kk, step] = eight(jnp.sum(jnp.sum(e, axis=0), axis=0, keepdims=True))

    def seen(index):
        return limit(2 * index), limit(2 * index + 1)

    def own_pair(kk):
        keys.from_partner(0, kk)
        key = lax.broadcasted_iota(jnp.int32, (2 * block, block), 0)
        place = lax.rem(key, block)
        query = lax.broadcasted_iota(jnp.int32, (2 * block, block), 1)
        even, odd = seen(pair)
        here = jnp.where(key < block, 2 * pair, 2 * pair + 1) == own
        mask = (place < jnp.where(key < block, even, odd)) & (
            jnp.logical_not(here) | (place <= query)
        )
        scores(kk, 0, jnp.concatenate([mask] * per, axis=1), True)

    def other_pairs(kk):
        def body(t):
            keys.from_partner(t, kk)
            index = pair - t

            @pl.when((index == 0) | (index >= first_pair(own)))
            def _():
                even, odd = seen(index)
                key = lax.broadcasted_iota(jnp.int32, (2 * block, rows), 0)
                mask = lax.rem(key, block) < jnp.where(key < block, even, odd)
                scores(kk, jnp.where(index == 0, pairs - 1, t), mask, False)

        each(1, pair + 1, body)

    keys.forward(0)

    def arrive(kk):
        @pl.when(kk + 1 < KEY_HEADS)
        def _():
            keys.forward(kk + 1)

        @pl.when(kk == KEY_HEADS - 1)
        def _():
            lows.forward(0)

        own_pair(kk)

        other_pairs(kk)

    each(0, KEY_HEADS, arrive)
    values.forward(0)
    live = (
        lax.rem(lax.broadcasted_iota(jnp.int32, (8, rows), 1), block) < own_length
    ).astype(F32)

    def add(step, totals):
        out = []
        for kk in range(KEY_HEADS):
            fall = jnp.exp2((tops[kk, step] - tops[kk, pairs - 1]) * tune)
            out.append(totals[kk] + facs[kk, step] * fall)
            facs[kk, step] = fall
        return tuple(out)

    totals = lax.fori_loop(
        0, pairs, add, tuple(jnp.zeros((8, rows), F32) for _ in range(KEY_HEADS))
    )
    for kk in range(KEY_HEADS):
        invs[kk] = live / totals[kk]

    def scatter(source, target, r):
        return remote(
            proj.at[target], landed.at[rep, source], p_send.at[target], p_recv.at[rep, source],
            target, r,
        )

    def project(i):
        step = pairs - 1 - i
        index = pair_at(step)
        turned = jnp.zeros((2 * rank, 2 * block), F32)
        for kk in range(KEY_HEADS):
            fac = facs[kk, step] * invs[kk]
            facs[kk, step] = fac
            side = times(gup[kk], fac)
            high = side.astype(BF16)
            sides = jnp.concatenate([high, (side - high.astype(F32)).astype(BF16)], axis=0)
            turned = turned + dot(sides, weight[kk, step], NT)
        turned = turned[:rank] + turned[rank:]
        for parity in range(2):
            slot = 2 * index + parity
            mine[parity] = turned[:, parity * block:(parity + 1) * block]
            proj[slot] = mine[parity].astype(BF16)

            @pl.when(reaches(slot, own))
            def _():
                scatter(own, slot, rep).start()
                other_reps(lambda r: scatter(own, slot, r).start())

            @pl.when(slot == own)
            def _():
                other_reps(lambda r: scatter(own, own, r).start())

    each(0, pairs, project)
    values.forward(1)
    values.forward(2)
    values.forward(3)

    def ancestors(action):
        def body(t):
            @pl.when(reaches(t, own))
            def _():
                action(t)

        each(0, slots, body)

    each(0, pair + 1, lambda t: lows.from_partner(t, 0))

    for kk in range(KEY_HEADS):
        lowsum[kk] = jnp.zeros((rank, rows), F32)

    def low_weights(step):
        index = pair_at(step)
        low = jnp.concatenate([lowbuf[2 * index, 0], lowbuf[2 * index + 1, 0]], axis=1)
        for kk in range(KEY_HEADS):
            lowsum[kk] += times(dot(low, weight[kk, step], NN), facs[kk, step])

    each(0, pairs, low_weights)
    for kk in range(KEY_HEADS):
        total = lowsum[kk]
        high = total.astype(BF16)
        sides = jnp.concatenate([high, (total - high.astype(F32)).astype(BF16)], axis=0)
        out = dot(sides, stacked(gs, kk), NN)
        upk[kk] = out[:rank] + out[rank:]

    share = KEY_HEADS // reps

    def swap_up(r):
        return remote(
            upk.at[pl.ds(r * share, share)], upland.at[rep], u_send.at[r], u_recv.at[rep], own, r
        )

    other_reps(lambda r: swap_up(r).start())

    def land(r):
        sums[r] = jnp.where(r == rep, mine[lax.rem(own, 2)], 0.0)

        def body(t):
            @pl.when(reaches(own, t) | (t == own) & (r != rep))
            def _():
                remote(
                    proj.at[t], landed.at[r, t], p_send.at[t], p_recv.at[r, t], t, r
                ).wait_recv()
                sums[r] += landed[r, t].astype(F32)

        each(own, slots, body)

    each(0, reps, land)
    loads[3].wait()

    def arrivals(r):
        remote(
            x_ref.at[:, pl.ds(0, half)], xcat.at[r], x_send.at[r], x_recv.at[r], own, r
        ).wait_recv()
        remote(
            upk.at[pl.ds(0, share)], upland.at[r], u_send.at[r], u_recv.at[r], own, r
        ).wait_recv()

    other_reps(arrivals)

    projected = jnp.concatenate([sums[r] for r in range(reps)], axis=1).astype(BF16)
    ups = upk[pl.ds(rep * share, share)]
    for step in range(1, reps):
        ups = ups + upland[lax.rem(rep + step, reps)]
    upland[rep] = ups
    chunks, _, chunk = parts.shape
    for j in range(chunks):
        lo, hi = j * chunk, (j + 1) * chunk
        pieces = []
        if lo < half:
            end = min(hi, half)
            pieces.append(dot(projected, xcat[:, :, lo:end].reshape(reps * block, end - lo), NN))
        for h in range(share):
            if lo <= half + h * HEAD_SIZE < hi:
                pieces.append(upland[rep, h])
        filled = sum(p.shape[1] for p in pieces)
        if filled < chunk:
            pieces.append(jnp.zeros((rank, chunk - filled), F32))
        value = pieces[0] if len(pieces) == 1 else jnp.concatenate(pieces, axis=1)
        parts[j] = value.astype(BF16)

    def reduce_copy(source, node):
        return remote(
            parts.at[node], gathered.at[source], r_send, r_recv, node
        )

    def others(action):
        if slots <= 8:
            for t in range(1, slots):
                action(lax.rem(own + t, slots))
        else:
            each(1, slots, lambda t: action(lax.rem(own + t, slots)))

    def owners(action):
        def body(node):
            @pl.when(node < chunks)
            def _():
                action(node)

        others(body)

    owners(lambda node: reduce_copy(own, node).start())

    def outputs(kk):
        each(0, pair + 1, lambda t: values.from_partner(t, kk))
        grad = stacked(gs, kk)
        acc[...] = jnp.zeros_like(acc)

        def attend(step):
            acc[...] += times(
                dot(two(vbuf, pair_at(step), kk), weight[kk, step], TN), facs[kk, step]
            )

        each(0, pairs, attend)
        out = acc[...]
        dots = (gtr[kk].astype(F32) * out).reshape(HEAD_SIZE // 8, 8, rows)
        dots = eight(jnp.sum(jnp.sum(dots, axis=0), axis=0, keepdims=True))
        for i in range(per):
            att_ref[:, pl.ds(pl.multiple_of((kk * per + i) * HEAD_SIZE, HEAD_SIZE), HEAD_SIZE)] = (
                acc[:, i * block:(i + 1) * block].T.astype(BF16)
            )
        acc[...] = jnp.zeros_like(acc)

        def back(step):
            index = pair_at(step)
            pressure = dot(two(vbuf, index, kk), grad, NT).reshape(eights, 8, rows)
            slopes = (pressure - dots[None]) * (facs[kk, step] * scale)[None]
            slopes = score[kk, step] * slopes.reshape(2 * block, rows)
            acc[...] += dot(two(kbuf, index, kk), slopes.astype(BF16), TN)

        each(0, pairs, back)
        for i in range(per):
            qg_ref[:, pl.ds(pl.multiple_of((kk * per + i) * HEAD_SIZE, HEAD_SIZE), HEAD_SIZE)] = (
                acc[:, i * block:(i + 1) * block].T.astype(BF16)
            )

    outputs_early = 2
    each(0, outputs_early, outputs)

    def gather_copy(node, owner):
        return remote(
            result.at[rep, owner], result.at[rep, owner], a_send, a_recv.at[owner], node
        )

    def swap_result(r, owner):
        return remote(
            result.at[rep, owner], result.at[rep, owner], b_send.at[r], b_recv.at[rep], own, r
        )

    @pl.when(own < chunks)
    def _():
        gathered[own] = parts[own]
        all_of(gathered.at[pl.ds(0, slots - 1)], r_recv).wait()
        acc = jnp.sum(gathered[...].astype(F32), axis=0)
        result[rep, own] = (acc * factor).astype(BF16)
        others(lambda node: gather_copy(node, own).start())
        other_reps(lambda r: swap_result(r, own).start())

    each(outputs_early, KEY_HEADS, outputs)

    def pass_on(owner):
        remote(
            result.at[rep, owner], result.at[rep, owner], a_send, a_recv.at[owner], owner
        ).wait_recv()
        other_reps(lambda r: swap_result(r, owner).start())

    owners(pass_on)

    other_reps(lambda r: all_of(result.at[r], b_recv.at[r]).wait())
    heads_of_two = kbuf.at[pl.ds(0, 2)]
    turned_heads = 2 * KEY_HEADS - keys.turns - values.turns
    turn_bytes = kbuf.at[0]

    def crossed(t):
        crossing = (t > 1) | (own > partner)

        @pl.when(crossing)
        def _():
            all_of(heads_of_two, fwd_send.at[t]).wait()

        if keys.turns + values.turns:
            @pl.when(jnp.logical_not(crossing))
            def _():
                all_of(kbuf.at[0, pl.ds(0, keys.turns + values.turns)], fwd_send.at[t]).wait()

    keys.targets(
        lambda: all_of(heads_of_two, fwd_send.at[0]).wait(),
        lambda t: all_of(heads_of_two, col_send.at[t]).wait(),
    )
    keys.passing(
        0,
        lambda slot: None,
        lambda slot, t: all_of(heads_of_two, on_send.at[t]).wait(),
        lambda slot, t: crossed(t),
    )
    if turned_heads:
        values.turning(
            lambda: all_of(turn_bytes, turn_send).wait()
        )
    lows.targets(
        lambda: all_of(lowbuf.at[0], l_fwd.at[0]).wait(),
        lambda t: all_of(lowbuf.at[0], l_col.at[t]).wait(),
    )
    lows.passing(
        0,
        lambda slot: None,
        lambda slot, t: all_of(lowbuf.at[0], l_on.at[t]).wait(),
        lambda slot, t: all_of(lowbuf.at[0], l_fwd.at[t]).wait(),
    )
    other_reps(lambda r: swap_x(r).wait_send())
    ancestors(lambda t: all_of(proj.at[pl.ds(0, reps)], p_send.at[t]).wait())
    all_of(proj.at[pl.ds(0, reps - 1)], p_send.at[own]).wait()
    other_reps(lambda r: swap_up(r).wait_send())

    @pl.when(own < chunks)
    def _():
        all_of(parts.at[pl.ds(0, chunks - 1)], r_send).wait()
        all_of(gathered.at[pl.ds(0, slots - 1)], a_send).wait()

    @pl.when(own >= chunks)
    def _():
        all_of(parts, r_send).wait()

    other_reps(lambda r: all_of(result.at[rep], b_send.at[r]).wait())


def finish(a_ref, b_ref, res, att_ref, qg_ref, down_ref, up_ref, down, up, sems):
    stores = [
        pltpu.make_async_copy(source, target, sems.at[i])
        for i, (source, target) in enumerate(
            [(a_ref, att_ref), (b_ref, qg_ref), (down, down_ref), (up, up_ref)]
        )
    ]
    for c in stores[:2]:
        c.start()
    reps, chunks, rank, chunk = res.shape
    half = down.shape[1] // reps
    up_half = up.shape[1] // reps
    for r in range(reps):
        for j in range(chunks):
            lo, hi = j * chunk, (j + 1) * chunk
            if lo < half:
                end = min(hi, half)
                down[:, r * half + lo:r * half + end] = res[r, j, :, :end - lo].astype(F32)
            if hi > half and lo < half + up_half:
                first, last = max(lo, half), min(hi, half + up_half)
                base = r * up_half - half
                up[:, base + first:base + last] = res[r, j, :, first - lo:last - lo].astype(F32)
    for c in stores[2:]:
        c.start()
    for c in stores:
        c.wait()


def on_device(x, q, k, frozen, down, up, g, parents, lengths):
    x, q, k, frozen, g = x[0], q[0], k[0], frozen[0], g[0]
    block, width = x.shape
    slots, reps = lax.axis_size("node"), lax.axis_size("rep")
    rank, up_width = up.shape
    heads = q.shape[1] // HEAD_SIZE
    rows = heads // KEY_HEADS * block
    pairs = pair_count(slots)
    tiles = -(-(width + up_width) // reps // 128)
    per = -(-tiles // slots)
    chunks = -(-tiles // per)
    chunk = per * 128
    factor = (slots * reps * block) ** -0.5
    anywhere = pl.BlockSpec(memory_space=pl.ANY)
    vmem = pl.BlockSpec(memory_space=pltpu.VMEM)
    smem = pl.BlockSpec(memory_space=pltpu.SMEM)
    dma = pltpu.SemaphoreType.DMA
    v = pltpu.VMEM
    share = KEY_HEADS // reps
    attended, query_grad, result = pl.pallas_call(
        functools.partial(kernel, slots, reps, factor),
        in_specs=[smem, smem, anywhere, anywhere, anywhere, anywhere, anywhere, vmem, anywhere],
        out_specs=[vmem, vmem, vmem],
        out_shape=[v(q.shape, BF16), v(q.shape, BF16), v((reps, chunks, rank, chunk), BF16)],
        scratch_shapes=[
            v(x.shape, BF16), v((reps, block, width // reps), BF16), v((rank, width), BF16),
            v((heads, block, HEAD_SIZE), BF16), v((heads, block, HEAD_SIZE), BF16),
            v(frozen.shape, BF16),
            v((slots, KEY_HEADS, block, HEAD_SIZE), BF16),
            v((slots, KEY_HEADS, block, HEAD_SIZE), BF16),
            v((slots, 1, rank, block), BF16),
            v((KEY_HEADS, pairs, 2 * block, rows), F32),
            v((KEY_HEADS, pairs, 2 * block, rows), BF16),
            v((KEY_HEADS, pairs, 8, rows), F32), v((KEY_HEADS, pairs, 8, rows), F32),
            v((HEAD_SIZE, rows), F32), v((KEY_HEADS, rank, rows), F32),
            v((KEY_HEADS, HEAD_SIZE, rows), BF16),
            v((KEY_HEADS, rank, rows), F32), v((KEY_HEADS, 8, rows), F32),
            v((slots, rank, block), BF16), v((2, rank, block), F32),
            v((reps, slots, rank, block), BF16), v((reps, rank, block), F32),
            v((KEY_HEADS, rank, HEAD_SIZE), F32), v((reps, share, rank, HEAD_SIZE), F32),
            v((chunks, rank, chunk), BF16), v((slots, rank, chunk), BF16),
            dma((7,)),
            dma((slots, KEY_HEADS)), dma((slots,)), dma((slots, KEY_HEADS)),
            dma((3,)), dma((slots // 2,)), dma((slots // 2,)), dma,
            dma((3,)), dma((slots // 2,)), dma((slots // 2,)),
            dma((reps,)), dma((reps,)), dma((reps,)), dma((reps,)),
            dma((reps, slots)), dma((slots,)), dma, dma, dma((slots,)), dma, dma((reps,)), dma((reps,)),
        ],
        compiler_params=pltpu.CompilerParams(
            collective_id=0, has_side_effects=True, vmem_limit_bytes=60 * 1024 * 1024
        ),
        name="tree_attention",
    )(parents, lengths, x, q, k, frozen, down.T, up, g)
    attended, query_grad, down_sum, up_sum = pl.pallas_call(
        finish,
        in_specs=[vmem, vmem, vmem],
        out_specs=[anywhere, anywhere, anywhere, anywhere],
        out_shape=[
            jax.ShapeDtypeStruct(q.shape, BF16),
            jax.ShapeDtypeStruct(q.shape, BF16),
            jax.ShapeDtypeStruct((rank, width), F32),
            jax.ShapeDtypeStruct((rank, up_width), F32),
        ],
        scratch_shapes=[
            v((rank, width), F32), v((rank, up_width), F32), dma((4,)),
        ],
        name="finish",
    )(*[pltpu.with_memory_space_constraint(a, pltpu.VMEM) for a in (attended, query_grad, result)])
    return attended[None], query_grad[None], down_sum.T, up_sum


def solution(mesh):
    rows = P(("groups", "rep"), "node", None)
    table = P(("groups", "rep"), None)
    return jax.shard_map(
        on_device,
        mesh=mesh,
        in_specs=(rows, rows, rows, rows, P(), P(), rows, table, table),
        out_specs=(rows, rows, P("groups", None), P("groups", None)),
        check_vma=False,
    )
```
